512 devices in a mesh: dp: 64 (over y, z), blk: 8 (over x, core).
Axes of the slice: x: 4, y: 8, z: 8, core: 2. Of those that a mesh axis runs over, the one named last changes fastest.
Arguments:
- queries: bfloat16 [8, 256, 32, 128], P('blk', 'dp'), may hold values from -6 to 6
- passages: bfloat16 [8, 1024, 192, 128], P('blk', 'dp'), may hold values from -6 to 6
- passage_lengths: int32 [8, 1024], P('blk', 'dp'), may hold values from 32 to 192
- positives: bfloat16 [8, 256, 192, 128], P('blk', 'dp'), may hold values from -6 to 6
- positive_lengths: int32 [8, 256], P('blk', 'dp'), may hold values from 32 to 192
- owners: int32 [8, 256, 32, 1], P('blk', 'dp'), may hold values from 0 to 63; in each aligned block of 128 rows (0 to 127, 128 to 255, ..., all dimensions but the last counted through in order) at most 4 rows name the same one
- local_ids: int32 [8, 256, 32], P('blk', 'dp'), may hold values from 0 to 15
- teacher: float32 [8, 256, 32], P('blk', 'dp'), may hold values from -12 to 12
Outputs:
- student: float32 [8, 256, 32], P('blk', 'dp')
- distill: float32 [8, 256], P('blk', 'dp')
- contrast: float32 [8, 256], P('blk', 'dp')
The draws below stay inside these ranges and needn't reach their ends.
Inputs may be any that keep to these rules, and one draw needn't show every extreme that they name: `owners`: among the 128 candidate pairs of the queries of one device, no owner is named more than 4 times, a bound that some block reaches.
All inputs are finite; a program needn't handle non-finite values.
Results may differ from the reference program's by a relative error of at most 0.00062.
Values may be sent and summed in bfloat16 or wider, within the bound.
A program may use at most 64 MiB of HBM per device.

```python
import math
import jax
import jax.numpy as jnp
import numpy as np
from jax import lax

D = 128
QLEN = 32
LMAX = 192
CAND = 32
Q_DEV = 4
PASS_DEV = 16
CAP = 4
QUERIES_G = 256
PASSAGES_G = 1024
N_DP = 64
N_BLK = 8


def plant(result, stream_key, low, top_value):
    longest = result.shape.index(max(result.shape))
    spots = []
    for shift in (0, 1):
        where = [jax.random.randint(jax.random.fold_in(stream_key, axis), (), 0, length) for axis, length in enumerate(result.shape)]
        where[longest] = (where[longest] + shift) % result.shape[longest]
        spots.append(tuple(where))
    return result.at[spots[0]].set(low).at[spots[1]].set(top_value)


def steps_of(stream_key, dims, shards, least, high):
    def one(position, parts):
        heights = jax.random.uniform(jax.random.fold_in(jax.random.fold_in(stream_key, 6), position), (parts,), jnp.float32, least / len(shards), high / len(shards))
        return jnp.repeat(jnp.exp(heights), dims[position] // parts).reshape((-1,) + (1,) * (len(dims) - position - 1))

    gain = one(*shards[0])
    for cut in shards[1:]:
        gain = gain * one(*cut)
    return gain


def shared_out(own_key, own, number, rows, count, top, reach, skew):
    order = jax.random.permutation(own_key, count)
    crowded, ordinary = shares(count, rows * top, reach, skew, True), shares(count, rows * top, reach, skew, False)
    places = jnp.arange(count)

    def named(sizes, rotation):
        used = int((sizes > 0).sum())
        fixed = max(1, used // 4)
        passed = fixed + (places - fixed + rotation * (used - fixed)) % max(1, count - fixed)
        return jnp.zeros((count,), jnp.int32).at[order[jnp.where(places < fixed, places, passed)]].set(jnp.asarray(sizes, jnp.int32))

    sizes = jnp.where(number % 4 == 0, named(crowded, number // 4), named(ordinary, number - number // 4 - 1))
    mixed = jax.random.permutation(jax.random.fold_in(own, 3), count)
    giver, sink = mixed[0:count // 2 * 2:2], mixed[1:count // 2 * 2:2]
    room = jnp.minimum(sizes[giver] - 1, reach - sizes[sink]) // 2
    room = jnp.where((giver == order[0]) | (sink == order[0]) | (sizes[sink] == 0), 0, jnp.maximum(room, 0))
    passed = jax.random.randint(jax.random.fold_in(own, 4), (count // 2,), 0, 1 << 20) % (room + 1)
    sizes = sizes.at[giver].add(-passed).at[sink].add(passed)
    items = jnp.searchsorted(jnp.cumsum(sizes), jnp.arange(rows * top), side="right").astype(jnp.int32)
    listing = items.reshape(top, rows).T
    listing = listing[jax.random.permutation(jax.random.fold_in(own, 1), rows)]
    rotation = jax.random.randint(jax.random.fold_in(own, 2), (rows, 1), 0, top)
    return jnp.take_along_axis(listing, (jnp.arange(top)[None, :] + rotation) % top, axis=1)


def shares(count, total, limit, lean, full):
    weights = [(1 << 20) // math.isqrt(rank ** lean) + 1 for rank in range(1, count + 1)]
    largest = limit if full else min(limit, max(-(-total // count), total * weights[0] // sum(weights)))
    least = 1 if total - largest >= count - 1 else 0
    given, spare = [largest] + [least] * (count - 1), total - largest - least * (count - 1)
    while spare > 0:
        free = [i for i in range(1, count) if given[i] < largest] or [i for i in range(1, count) if given[i] < limit]
        whole, budget = sum([weights[i] for i in free]), spare
        for i in free:
            extra = min(limit - given[i], max(1, budget * weights[i] // whole), spare)
            given[i] = given[i] + extra
            spare = spare - extra
    return np.array(given)


def centred(key, extent, deviation, limit, shards=(), held_as=jnp.bfloat16):
    factor_of = steps_of(key, extent, shards, -0.22, 0.18) if shards else 1.0
    values = jax.random.normal(key, extent, jnp.float32) * deviation * factor_of
    return jnp.minimum(jnp.maximum(values, -limit), limit).astype(held_as)


def setup_inputs(seed: int = 0) -> dict:
    arg_keys = jax.random.split(jax.random.key(seed), 9)
    queries = centred(arg_keys[0], (N_BLK, QUERIES_G, QLEN, D), 1.0, 6.0, ((0, 8), (1, 64)))
    passages = centred(arg_keys[1], (N_BLK, PASSAGES_G, LMAX, D), 1.0, 6.0, ((0, 8), (1, 64)))
    passage_lengths = plant(jax.random.randint(arg_keys[2], (N_BLK, PASSAGES_G), LMAX // 6, LMAX + 1), jax.random.fold_in(arg_keys[2], 1), LMAX // 6, LMAX).astype(jnp.int32)
    positives = centred(arg_keys[3], (N_BLK, QUERIES_G, LMAX, D), 1.0, 6.0, ((0, 8), (1, 64)))
    positive_lengths = plant(jax.random.randint(arg_keys[4], (N_BLK, QUERIES_G), LMAX // 6, LMAX + 1), jax.random.fold_in(arg_keys[4], 1), LMAX // 6, LMAX).astype(jnp.int32)
    owners_keys = jax.random.split(jax.random.fold_in(arg_keys[5], 1), N_BLK * QUERIES_G * CAND // (Q_DEV * CAND))
    owners_turns = jax.random.permutation(jax.random.fold_in(arg_keys[5], 3), N_BLK * QUERIES_G * CAND // (Q_DEV * CAND))
    owners = jax.vmap(lambda own, number: shared_out(jax.random.fold_in(arg_keys[5], 2), own, number, Q_DEV * CAND, N_DP, 1, CAP, 2))(owners_keys, owners_turns).reshape((N_BLK, QUERIES_G, CAND, 1))
    local_ids = plant(jax.random.randint(arg_keys[6], (N_BLK, QUERIES_G, CAND), 0, PASS_DEV), jax.random.fold_in(arg_keys[6], 1), 0, PASS_DEV - 1).astype(jnp.int32)
    teacher = centred(arg_keys[7], (N_BLK, QUERIES_G, CAND), 2.0, 12.0, ((0, 8), (1, 64)), jnp.float32)
    return {"queries": queries, "passages": passages, "passage_lengths": passage_lengths, "positives": positives, "positive_lengths": positive_lengths, "owners": owners, "local_ids": local_ids, "teacher": teacher}


def unit_rows(values):
    wide = values.astype(jnp.float32)
    total = lax.optimization_barrier(jnp.sum(wide * wide, axis=-1, keepdims=True)) + 1e-06
    return (wide * lax.rsqrt(total)).astype(jnp.bfloat16)

def late_score(query, document_rows, lengths):
    similarity_matrix = jnp.einsum('qd,kld->kql', query.astype(jnp.float32), document_rows.astype(jnp.float32))
    usable = jnp.arange(document_rows.shape[1]).astype(jnp.int32)[None, None, :] < lengths[:, None, None]
    similarity_matrix = jnp.where(usable, similarity_matrix, -1000000000.0)
    return lax.optimization_barrier(jnp.sum(lax.optimization_barrier(jnp.max(similarity_matrix, axis=2)), axis=1))

def reference(queries, passages, passage_lengths, positives, positive_lengths, owners, local_ids, teacher):
    query_unit = unit_rows(queries)
    passage_unit = unit_rows(passages)
    positive_unit = unit_rows(positives)
    flat_ids = (owners[..., 0] * PASS_DEV + local_ids).astype(jnp.int32)

    def per_group(group):
        group_queries, group_passages, group_lengths, group_ids = group

        def per_query(inner):
            query, selected_entries = inner
            return late_score(query, group_passages[selected_entries], group_lengths[selected_entries])
        return lax.map(per_query, (group_queries, group_ids))
    student = lax.map(per_group, (query_unit, passage_unit, passage_lengths, flat_ids))
    log_teacher = teacher - jnp.log(lax.optimization_barrier(jnp.sum(jnp.exp(teacher), axis=-1, keepdims=True)))
    log_student = student - jnp.log(lax.optimization_barrier(jnp.sum(jnp.exp(student), axis=-1, keepdims=True)))
    distill = lax.optimization_barrier(jnp.sum(jnp.exp(log_teacher) * (log_teacher - log_student), axis=-1))
    split_queries = jnp.moveaxis(query_unit.reshape(N_BLK, N_DP, Q_DEV, QLEN, D), 1, 0)
    split_docs = jnp.moveaxis(positive_unit.reshape(N_BLK, N_DP, Q_DEV, LMAX, D), 1, 0)
    split_lengths = jnp.moveaxis(positive_lengths.reshape(N_BLK, N_DP, Q_DEV), 1, 0)

    def per_column(column):
        column_queries, column_docs, column_lengths = column
        document_rows = column_docs.reshape(N_BLK * Q_DEV, LMAX, D)
        lengths = column_lengths.reshape(N_BLK * Q_DEV)

        def per_query(query):
            return late_score(query, document_rows, lengths)
        return lax.map(per_query, column_queries.reshape(N_BLK * Q_DEV, QLEN, D))
    logits = lax.map(per_column, (split_queries, split_docs, split_lengths))
    logits = jnp.moveaxis(logits.reshape(N_DP, N_BLK, Q_DEV, N_BLK * Q_DEV), 0, 1)
    logits = logits.reshape(N_BLK, N_DP * Q_DEV, N_BLK * Q_DEV)
    group_index = jnp.arange(N_BLK).astype(jnp.int32)[:, None]
    query_index = (jnp.arange(N_DP * Q_DEV) % Q_DEV).astype(jnp.int32)[None, :]
    own_column = (group_index * Q_DEV + query_index).astype(jnp.int32)
    own_logit = jnp.take_along_axis(logits, own_column[:, :, None], axis=2)[..., 0]
    contrast = jnp.log(lax.optimization_barrier(jnp.sum(jnp.exp(logits), axis=-1))) - own_logit
    return (student, distill, contrast)
```

```python
import functools

import jax
import jax.numpy as jnp
from jax import lax
from jax.experimental import pallas as pl
from jax.experimental.pallas import tpu as pltpu
from jax.sharding import PartitionSpec as P

NEG = -1000000000.0


def unit_rows(values):
    wide = values.astype(jnp.float32)
    total = jnp.sum(wide * wide, axis=-1, keepdims=True) + 1e-06
    return (wide * lax.rsqrt(total)).astype(jnp.bfloat16)


def student_kernel(qrow_ref, pid_ref, len_ref, g_ref, p_ref, o_ref, *, slots):
    sources = g_ref.shape[0]
    qlen = o_ref.shape[1] // slots
    plen = p_ref.shape[1]
    lane_slot = lax.broadcasted_iota(jnp.int32, (1, o_ref.shape[1]), 1) // qlen
    row_ids = lax.broadcasted_iota(jnp.int32, (plen, o_ref.shape[1]), 0)

    def body(s, carry):
        pieces = []
        for r in range(slots):
            j = qrow_ref[s * slots + r]
            pieces.append(g_ref[s, pl.ds(pl.multiple_of(j * qlen, qlen), qlen), :])
        q = jnp.concatenate(pieces, axis=0)
        row = jnp.zeros((1, o_ref.shape[1]), jnp.float32)
        for r in range(slots):
            pidx = pid_ref[s * slots + r]
            sim = lax.dot_general(
                p_ref[pidx], q, (((1,), (1,)), ((), ())), preferred_element_type=jnp.float32
            )
            sim = jnp.where(row_ids < len_ref[pidx], sim, NEG)
            row = jnp.where(lane_slot == r, jnp.max(sim, axis=0, keepdims=True), row)
        o_ref[pl.ds(s, 1), :] = row
        return carry

    lax.fori_loop(0, sources, body, 0)


def student_scores(qrow, pid, lengths, gathered, passage_unit, slots, qlen):
    sources = gathered.shape[0]
    plen, dim = passage_unit.shape[1], passage_unit.shape[2]
    flops = 2 * sources * slots * plen * dim * slots * qlen
    return pl.pallas_call(
        functools.partial(student_kernel, slots=slots),
        out_shape=jax.ShapeDtypeStruct((sources, slots * qlen), jnp.float32),
        in_specs=[pl.BlockSpec(memory_space=pltpu.SMEM)] * 3
        + [pl.BlockSpec(memory_space=pltpu.VMEM)] * 2,
        out_specs=pl.BlockSpec(memory_space=pltpu.VMEM),
        cost_estimate=pl.CostEstimate(
            flops=flops,
            transcendentals=0,
            bytes_accessed=gathered.size * 2 + passage_unit.size * 2 + sources * slots * qlen * 4,
        ),
    )(qrow, pid, lengths, gathered, passage_unit)


def cross_kernel(len_ref, q_ref, p_ref, o_ref):
    plen = p_ref.shape[1]
    row_ids = lax.broadcasted_iota(jnp.int32, (plen, q_ref.shape[0]), 0)
    q = q_ref[...]
    for k in range(p_ref.shape[0]):
        sim = lax.dot_general(
            p_ref[k], q, (((1,), (1,)), ((), ())), preferred_element_type=jnp.float32
        )
        sim = jnp.where(row_ids < len_ref[k], sim, NEG)
        o_ref[pl.ds(k, 1), :] = jnp.max(sim, axis=0, keepdims=True)


def cross_scores(lengths, query_rows, positive_unit):
    docs, plen, dim = positive_unit.shape
    cols = query_rows.shape[0]
    return pl.pallas_call(
        cross_kernel,
        out_shape=jax.ShapeDtypeStruct((docs, cols), jnp.float32),
        in_specs=[pl.BlockSpec(memory_space=pltpu.SMEM)]
        + [pl.BlockSpec(memory_space=pltpu.VMEM)] * 2,
        out_specs=pl.BlockSpec(memory_space=pltpu.VMEM),
        cost_estimate=pl.CostEstimate(
            flops=2 * docs * plen * dim * cols,
            transcendentals=0,
            bytes_accessed=query_rows.size * 2 + positive_unit.size * 2 + docs * cols * 4,
        ),
    )(lengths, query_rows, positive_unit)


def per_device(
    queries, passages, passage_lengths, positives, positive_lengths, owners, local_ids, teacher
):
    peer_count = lax.axis_size("dp")
    me = lax.axis_index("dp")
    query_count, qlen, dim = queries.shape[1], queries.shape[2], queries.shape[3]
    cand_count = owners.shape[2]
    pass_count = passages.shape[1]
    pairs = query_count * cand_count
    slots = 4

    query_unit = unit_rows(queries[0]).reshape(query_count * qlen, dim)
    id_rows = jnp.stack(
        [
            jnp.clip(owners[0, :, :, 0].reshape(pairs), 0, peer_count - 1),
            jnp.clip(local_ids[0].reshape(pairs), 0, pass_count - 1),
        ]
    ).astype(jnp.bfloat16)
    id_rows = id_rows.reshape(2 * pairs // dim, dim)
    id_block = jnp.zeros((16, dim), jnp.bfloat16).at[: id_rows.shape[0]].set(id_rows)
    send = jnp.concatenate([query_unit, id_block], axis=0)

    column_queries = lax.all_gather(query_unit, "blk", axis=0, tiled=True)
    positive_unit = unit_rows(positives[0])
    column_scores = cross_scores(positive_lengths[0], column_queries, positive_unit)
    groups = lax.axis_size("blk")
    column_scores = jnp.sum(
        column_scores.reshape(query_count, groups, query_count, qlen), axis=-1
    )
    every_scores = lax.all_gather(column_scores, "blk", axis=0)
    mine = lax.dynamic_index_in_dim(every_scores, lax.axis_index("blk"), axis=2, keepdims=False)
    logits = jnp.transpose(mine, (2, 0, 1)).reshape(query_count, groups * query_count)
    own_column = lax.axis_index("blk") * query_count + jnp.arange(query_count, dtype=jnp.int32)
    own_logit = jnp.take_along_axis(logits, own_column[:, None], axis=1)[:, 0]
    contrast = jnp.log(jnp.sum(jnp.exp(logits), axis=-1)) - own_logit

    gathered = lax.all_gather(send, "dp", axis=0)
    ids = gathered[:, query_count * qlen : query_count * qlen + 2 * pairs // dim, :]
    ids = ids.reshape(peer_count, 2, pairs).astype(jnp.int32)
    pair_owner, pair_local = ids[:, 0, :], ids[:, 1, :]
    hit = (pair_owner == me).astype(jnp.int32)
    rank = jnp.cumsum(hit, axis=1) - hit
    pair_index = lax.broadcasted_iota(jnp.int32, (peer_count, pairs), 1)
    chosen = [(hit > 0) & (rank == r) for r in range(slots)]
    slot_pair = jnp.stack([jnp.sum(jnp.where(c, pair_index, 0), axis=1) for c in chosen], axis=1)
    slot_local = jnp.stack([jnp.sum(jnp.where(c, pair_local, 0), axis=1) for c in chosen], axis=1)
    qrow = (slot_pair // cand_count).reshape(-1)
    passage_unit = unit_rows(passages[0])
    raw = student_scores(
        qrow,
        slot_local.reshape(-1),
        passage_lengths[0],
        gathered,
        passage_unit,
        slots,
        qlen,
    )
    slot_score = jnp.sum(raw.reshape(peer_count, slots, qlen), axis=-1)
    placed = jnp.zeros((peer_count, pairs), jnp.float32)
    for r in range(slots):
        placed = placed + jnp.where(chosen[r], slot_score[:, r : r + 1], 0.0)
    returned = lax.psum_scatter(placed, "dp", scatter_dimension=0, tiled=True)
    student = returned.reshape(query_count, cand_count)

    teacher_score_rows = teacher[0]
    log_teacher = teacher_score_rows - jnp.log(
        jnp.sum(jnp.exp(teacher_score_rows), axis=-1, keepdims=True)
    )
    log_student = student - jnp.log(jnp.sum(jnp.exp(student), axis=-1, keepdims=True))
    distill = jnp.sum(jnp.exp(log_teacher) * (log_teacher - log_student), axis=-1)
    return (student[None], distill[None], contrast[None])


def solution(mesh):
    in_specs = (
        P("blk", "dp", None, None),
        P("blk", "dp", None, None),
        P("blk", "dp"),
        P("blk", "dp", None, None),
        P("blk", "dp"),
        P("blk", "dp", None, None),
        P("blk", "dp", None),
        P("blk", "dp", None),
    )
    out_specs = (P("blk", "dp", None), P("blk", "dp"), P("blk", "dp"))
    return jax.shard_map(
        per_device, mesh=mesh, in_specs=in_specs, out_specs=out_specs, check_vma=False
    )
```

```python
import functools

import jax
import jax.numpy as jnp
from jax import lax
from jax.experimental import pallas as pl
from jax.experimental.pallas import tpu as pltpu
from jax.sharding import PartitionSpec as P

NEG = -1000000000.0


def unit_rows(values):
    wide = values.astype(jnp.float32)
    total = jnp.sum(wide * wide, axis=-1, keepdims=True) + 1e-06
    return (wide * lax.rsqrt(total)).astype(jnp.bfloat16)


def student_kernel(n_ref, gpid_ref, gsrc_ref, grow_ref, len_ref, g_ref, p_ref, o_ref):
    lanes = o_ref.shape[1]
    slots = gsrc_ref.shape[0] // o_ref.shape[0]
    qlen = lanes // slots
    plen = p_ref.shape[1]
    row_ids = lax.broadcasted_iota(jnp.int32, (plen, lanes), 0)

    def body(g, carry):
        pieces = []
        for r in range(slots):
            src = gsrc_ref[g * slots + r]
            j = grow_ref[g * slots + r]
            pieces.append(g_ref[src, pl.ds(pl.multiple_of(j * qlen, qlen), qlen), :])
        q = jnp.concatenate(pieces, axis=0)
        pidx = gpid_ref[g]
        sim = lax.dot_general(
            p_ref[pidx], q, (((1,), (1,)), ((), ())), preferred_element_type=jnp.float32
        )
        sim = jnp.where(row_ids < len_ref[pidx], sim, NEG)
        o_ref[pl.ds(g, 1), :] = jnp.max(sim, axis=0, keepdims=True)
        return carry

    lax.fori_loop(0, n_ref[0], body, 0)


def student_scores(n_groups, gpid, gsrc, grow, lengths, gathered, passage_unit, group_cap, lanes):
    plen, dim = passage_unit.shape[1], passage_unit.shape[2]
    return pl.pallas_call(
        student_kernel,
        out_shape=jax.ShapeDtypeStruct((group_cap, lanes), jnp.float32),
        in_specs=[pl.BlockSpec(memory_space=pltpu.SMEM)] * 5
        + [pl.BlockSpec(memory_space=pltpu.VMEM)] * 2,
        out_specs=pl.BlockSpec(memory_space=pltpu.VMEM),
        cost_estimate=pl.CostEstimate(
            flops=2 * group_cap * plen * dim * lanes,
            transcendentals=0,
            bytes_accessed=gathered.size * 2 + passage_unit.size * 2 + group_cap * lanes * 4,
        ),
    )(n_groups, gpid, gsrc, grow, lengths, gathered, passage_unit)


def cross_kernel(len_ref, q_ref, p_ref, o_ref, *, plen):
    groups = p_ref.shape[0]
    docs = o_ref.shape[0] // groups
    row_ids = lax.broadcasted_iota(jnp.int32, (plen, q_ref.shape[0]), 0)
    q = q_ref[...]
    for e in range(groups):
        for k in range(docs):
            sim = lax.dot_general(
                p_ref[e, k * plen : (k + 1) * plen, :],
                q,
                (((1,), (1,)), ((), ())),
                preferred_element_type=jnp.float32,
            )
            sim = jnp.where(row_ids < len_ref[e * docs + k], sim, NEG)
            o_ref[pl.ds(e * docs + k, 1), :] = jnp.max(sim, axis=0, keepdims=True)


def cross_scores(lengths, query_rows, gathered_docs, doc_count, plen):
    groups, rows, dim = gathered_docs.shape
    cols = query_rows.shape[0]
    return pl.pallas_call(
        functools.partial(cross_kernel, plen=plen),
        out_shape=jax.ShapeDtypeStruct((groups * doc_count, cols), jnp.float32),
        in_specs=[pl.BlockSpec(memory_space=pltpu.SMEM)]
        + [pl.BlockSpec(memory_space=pltpu.VMEM)] * 2,
        out_specs=pl.BlockSpec(memory_space=pltpu.VMEM),
        cost_estimate=pl.CostEstimate(
            flops=2 * groups * rows * dim * cols,
            transcendentals=0,
            bytes_accessed=query_rows.size * 2 + gathered_docs.size * 2 + groups * doc_count * cols * 4,
        ),
    )(lengths, query_rows, gathered_docs)


def per_device(
    queries, passages, passage_lengths, positives, positive_lengths, owners, local_ids, teacher
):
    peer_count = lax.axis_size("dp")
    me = lax.axis_index("dp")
    query_count, qlen, dim = queries.shape[1], queries.shape[2], queries.shape[3]
    cand_count = owners.shape[2]
    pass_count, plen = passages.shape[1], passages.shape[2]
    pairs = query_count * cand_count
    slots = 4
    lanes = slots * qlen
    group_cap = peer_count * slots // slots + pass_count

    positive_unit = unit_rows(positives[0]).reshape(query_count * plen, dim)
    length_row = jnp.zeros((16, dim), jnp.bfloat16).at[0, :query_count].set(
        positive_lengths[0].astype(jnp.bfloat16)
    )
    doc_block = jnp.concatenate([positive_unit, length_row], axis=0)
    column_docs = lax.all_gather(doc_block, "blk", axis=0)
    groups = column_docs.shape[0]
    doc_lengths = column_docs[:, query_count * plen, :query_count].astype(jnp.int32).reshape(-1)

    query_unit = unit_rows(queries[0]).reshape(query_count * qlen, dim)
    id_rows = jnp.stack(
        [
            jnp.clip(owners[0, :, :, 0].reshape(pairs), 0, peer_count - 1),
            jnp.clip(local_ids[0].reshape(pairs), 0, pass_count - 1),
        ]
    ).astype(jnp.bfloat16)
    id_rows = id_rows.reshape(2 * pairs // dim, dim)
    id_block = jnp.zeros((16, dim), jnp.bfloat16).at[: id_rows.shape[0]].set(id_rows)
    send = jnp.concatenate([query_unit, id_block], axis=0)
    gathered = lax.all_to_all(
        jnp.broadcast_to(send[None], (peer_count,) + send.shape),
        "dp",
        split_axis=0,
        concat_axis=0,
        tiled=True,
    )

    raw_cross = cross_scores(doc_lengths, query_unit, column_docs, query_count, plen)
    logits = jnp.sum(raw_cross.reshape(groups * query_count, query_count, qlen), axis=-1).T
    own_column = lax.axis_index("blk") * query_count + jnp.arange(query_count, dtype=jnp.int32)
    own_logit = jnp.take_along_axis(logits, own_column[:, None], axis=1)[:, 0]
    contrast = jnp.log(jnp.sum(jnp.exp(logits), axis=-1)) - own_logit

    ids = gathered[:, query_count * qlen : query_count * qlen + 2 * pairs // dim, :]
    ids = ids.reshape(peer_count, 2, pairs).astype(jnp.int32)
    pair_owner, pair_local = ids[:, 0, :], ids[:, 1, :]
    hit = (pair_owner == me).astype(jnp.int32)
    rank = jnp.cumsum(hit, axis=1) - hit
    pair_index = lax.broadcasted_iota(jnp.int32, (peer_count, pairs), 1)
    chosen = [(hit > 0) & (rank == r) for r in range(slots)]
    slot_pair = jnp.stack([jnp.sum(jnp.where(c, pair_index, 0), axis=1) for c in chosen], axis=1)
    slot_local = jnp.stack([jnp.sum(jnp.where(c, pair_local, 0), axis=1) for c in chosen], axis=1)
    slot_valid = jnp.stack([jnp.any(c, axis=1) for c in chosen], axis=1).reshape(-1)
    slot_pid = slot_local.reshape(-1)
    slot_src = (lax.broadcasted_iota(jnp.int32, (peer_count, slots), 0)).reshape(-1)
    slot_row = (slot_pair // cand_count).reshape(-1)

    by_pass = (
        slot_valid[:, None] & (slot_pid[:, None] == jnp.arange(pass_count, dtype=jnp.int32)[None, :])
    ).astype(jnp.int32)
    per_pass = jnp.sum(by_pass, axis=0)
    pass_groups = (per_pass + slots - 1) // slots
    pass_base = jnp.cumsum(pass_groups) - pass_groups
    n_groups = jnp.sum(pass_groups).reshape(1)
    in_pass = jnp.sum((jnp.cumsum(by_pass, axis=0) - by_pass) * by_pass, axis=1)
    slot_target = jnp.sum(pass_base[None, :] * by_pass, axis=1) * slots + in_pass
    slot_target = jnp.where(slot_valid, slot_target, group_cap * slots)
    target_hit = slot_target[None, :] == jnp.arange(group_cap * slots, dtype=jnp.int32)[:, None]
    gsrc = jnp.sum(jnp.where(target_hit, slot_src[None, :], 0), axis=1)
    grow = jnp.sum(jnp.where(target_hit, slot_row[None, :], 0), axis=1)
    group_index = jnp.arange(group_cap, dtype=jnp.int32)[:, None]
    gpid = jnp.sum(
        jnp.where(
            (group_index >= pass_base[None, :]) & (group_index < (pass_base + pass_groups)[None, :]),
            jnp.arange(pass_count, dtype=jnp.int32)[None, :],
            0,
        ),
        axis=1,
    )
    passage_unit = unit_rows(passages[0])
    raw = student_scores(
        n_groups, gpid, gsrc, grow, passage_lengths[0], gathered, passage_unit, group_cap, lanes
    )
    group_score = jnp.sum(raw.reshape(group_cap * slots, qlen), axis=-1)
    slot_score = jnp.take(group_score, jnp.minimum(slot_target, group_cap * slots - 1))
    slot_score = jnp.where(slot_valid, slot_score, 0.0).reshape(peer_count, slots)
    returned = lax.all_to_all(slot_score, "dp", split_axis=0, concat_axis=0, tiled=True)

    my_owner = jnp.clip(owners[0, :, :, 0].reshape(pairs), 0, peer_count - 1)
    owner_hot = (my_owner[:, None] == jnp.arange(peer_count, dtype=jnp.int32)[None, :]).astype(
        jnp.int32
    )
    my_rank = jnp.sum((jnp.cumsum(owner_hot, axis=0) - owner_hot) * owner_hot, axis=1)
    student = returned[my_owner, jnp.minimum(my_rank, slots - 1)].reshape(query_count, cand_count)

    teacher_score_rows = teacher[0]
    log_teacher = teacher_score_rows - jnp.log(
        jnp.sum(jnp.exp(teacher_score_rows), axis=-1, keepdims=True)
    )
    log_student = student - jnp.log(jnp.sum(jnp.exp(student), axis=-1, keepdims=True))
    distill = jnp.sum(jnp.exp(log_teacher) * (log_teacher - log_student), axis=-1)
    return (student[None], distill[None], contrast[None])


def solution(mesh):
    in_specs = (
        P("blk", "dp", None, None),
        P("blk", "dp", None, None),
        P("blk", "dp"),
        P("blk", "dp", None, None),
        P("blk", "dp"),
        P("blk", "dp", None, None),
        P("blk", "dp", None),
        P("blk", "dp", None),
    )
    out_specs = (P("blk", "dp", None), P("blk", "dp"), P("blk", "dp"))
    return jax.shard_map(
        per_device, mesh=mesh, in_specs=in_specs, out_specs=out_specs, check_vma=False
    )
```

```python
import functools
import math

import jax
import jax.numpy as jnp
from jax import lax
from jax.experimental import pallas as pl
from jax.experimental.pallas import tpu as pltpu
from jax.sharding import PartitionSpec as P

NEG = -1000000000.0


def unit_rows(values):
    wide = values.astype(jnp.float32)
    total = jnp.sum(wide * wide, axis=-1, keepdims=True) + 1e-06
    return (wide * lax.rsqrt(total)).astype(jnp.bfloat16)


def student_kernel(n_ref, gpid_ref, gsrc_ref, grow_ref, len_ref, g_ref, p_ref, o_ref):
    lanes = o_ref.shape[1]
    slots = gsrc_ref.shape[0] // o_ref.shape[0]
    qlen = lanes // slots
    plen = p_ref.shape[1]
    row_ids = lax.broadcasted_iota(jnp.int32, (plen, lanes), 0)

    def body(g, carry):
        pieces = []
        for r in range(slots):
            src = gsrc_ref[g * slots + r]
            j = grow_ref[g * slots + r]
            pieces.append(g_ref[src, pl.ds(pl.multiple_of(j * qlen, qlen), qlen), :])
        q = jnp.concatenate(pieces, axis=0)
        pidx = gpid_ref[g]
        sim = lax.dot_general(
            p_ref[pidx], q, (((1,), (1,)), ((), ())), preferred_element_type=jnp.float32
        )
        sim = jnp.where(row_ids < len_ref[pidx], sim, NEG)
        o_ref[pl.ds(g, 1), :] = jnp.max(sim, axis=0, keepdims=True)
        return carry

    lax.fori_loop(0, n_ref[0], body, 0)


def student_scores(n_groups, gpid, gsrc, grow, lengths, gathered, passage_unit, group_cap, lanes):
    plen, dim = passage_unit.shape[1], passage_unit.shape[2]
    return pl.pallas_call(
        student_kernel,
        out_shape=jax.ShapeDtypeStruct((group_cap, lanes), jnp.float32),
        in_specs=[pl.BlockSpec(memory_space=pltpu.SMEM)] * 5
        + [pl.BlockSpec(memory_space=pltpu.VMEM)] * 2,
        out_specs=pl.BlockSpec(memory_space=pltpu.VMEM),
        cost_estimate=pl.CostEstimate(
            flops=2 * group_cap * plen * dim * lanes,
            transcendentals=0,
            bytes_accessed=gathered.size * 2 + passage_unit.size * 2 + group_cap * lanes * 4,
        ),
    )(n_groups, gpid, gsrc, grow, lengths, gathered, passage_unit)


def cross_kernel(len_ref, q_ref, p_ref, o_ref, *, plen):
    groups = p_ref.shape[0]
    docs = o_ref.shape[0] // groups
    row_ids = lax.broadcasted_iota(jnp.int32, (plen, q_ref.shape[0]), 0)
    q = q_ref[...]
    for e in range(groups):
        for k in range(docs):
            sim = lax.dot_general(
                p_ref[e, k * plen : (k + 1) * plen, :],
                q,
                (((1,), (1,)), ((), ())),
                preferred_element_type=jnp.float32,
            )
            sim = jnp.where(row_ids < len_ref[e * docs + k], sim, NEG)
            o_ref[pl.ds(e * docs + k, 1), :] = jnp.max(sim, axis=0, keepdims=True)


def cross_scores(lengths, query_rows, gathered_docs, doc_count, plen):
    groups, rows, dim = gathered_docs.shape
    cols = query_rows.shape[0]
    return pl.pallas_call(
        functools.partial(cross_kernel, plen=plen),
        out_shape=jax.ShapeDtypeStruct((groups * doc_count, cols), jnp.float32),
        in_specs=[pl.BlockSpec(memory_space=pltpu.SMEM)]
        + [pl.BlockSpec(memory_space=pltpu.VMEM)] * 2,
        out_specs=pl.BlockSpec(memory_space=pltpu.VMEM),
        cost_estimate=pl.CostEstimate(
            flops=2 * groups * rows * dim * cols,
            transcendentals=0,
            bytes_accessed=query_rows.size * 2 + gathered_docs.size * 2 + groups * doc_count * cols * 4,
        ),
    )(lengths, query_rows, gathered_docs)


def exchange_kernel(x_ref, g_ref, ring_send, ring_recv, up_send, up_recv, dn_send, dn_recv, own_sem, *, side):
    mesh_ids = pl.DeviceIdType.MESH
    dp = lax.axis_index("dp")
    odd = lax.axis_index("blk") % 2
    high, low = dp // side, dp % side
    p1 = odd * high + (1 - odd) * low
    p2 = odd * low + (1 - odd) * high

    def dp_of(q1, q2):
        return odd * (q1 * side + q2) + (1 - odd) * (q2 * side + q1)

    ring_peers = [dp_of((p1 + d) % side, p2) for d in range(1, side)]
    up_peer = dp_of(p1, (p2 + 1) % side)
    dn_peer = dp_of(p1, (p2 + side - 1) % side)

    barrier = pltpu.get_barrier_semaphore()
    for peer in ring_peers + [up_peer, dn_peer]:
        pl.semaphore_signal(barrier, inc=1, device_id={"dp": peer}, device_id_type=mesh_ids)
    pl.semaphore_wait(barrier, len(ring_peers) + 2)

    my_slot = p2 * side + p1
    own = pltpu.make_async_copy(x_ref, g_ref.at[my_slot], own_sem)
    own.start()
    ring = []
    for d in range(1, side):
        copy = pltpu.make_async_remote_copy(
            src_ref=x_ref,
            dst_ref=g_ref.at[my_slot],
            send_sem=ring_send.at[d - 1],
            recv_sem=ring_recv.at[d - 1],
            device_id={"dp": ring_peers[d - 1]},
            device_id_type=mesh_ids,
        )
        copy.start()
        ring.append(copy)
    for copy in ring:
        copy.wait_recv()
    own.wait()

    def row(r):
        return g_ref.at[pl.ds(pl.multiple_of(r * side, side), side)]

    ups, dns = [], []
    up_steps, dn_steps = side // 2, (side - 1) // 2
    for t in range(max(up_steps, dn_steps)):
        if t < up_steps:
            if t > 0:
                ups[t - 1].wait_recv()
            r = (p2 + side - t) % side
            copy = pltpu.make_async_remote_copy(
                src_ref=row(r),
                dst_ref=row(r),
                send_sem=up_send.at[t],
                recv_sem=up_recv.at[t],
                device_id={"dp": up_peer},
                device_id_type=mesh_ids,
            )
            copy.start()
            ups.append(copy)
        if t < dn_steps:
            if t > 0:
                dns[t - 1].wait_recv()
            r = (p2 + t) % side
            copy = pltpu.make_async_remote_copy(
                src_ref=row(r),
                dst_ref=row(r),
                send_sem=dn_send.at[t],
                recv_sem=dn_recv.at[t],
                device_id={"dp": dn_peer},
                device_id_type=mesh_ids,
            )
            copy.start()
            dns.append(copy)
    ups[-1].wait_recv()
    dns[-1].wait_recv()
    for copy in ring + ups + dns:
        copy.wait_send()


def gather_plane(block, side):
    rows, dim = block.shape
    count = side * side
    return pl.pallas_call(
        functools.partial(exchange_kernel, side=side),
        out_shape=jax.ShapeDtypeStruct((count, rows, dim), block.dtype),
        in_specs=[pl.BlockSpec(memory_space=pltpu.VMEM)],
        out_specs=pl.BlockSpec(memory_space=pltpu.VMEM),
        scratch_shapes=[
            pltpu.SemaphoreType.DMA((side - 1,)),
            pltpu.SemaphoreType.DMA((side - 1,)),
            pltpu.SemaphoreType.DMA((side // 2,)),
            pltpu.SemaphoreType.DMA((side // 2,)),
            pltpu.SemaphoreType.DMA(((side - 1) // 2,)),
            pltpu.SemaphoreType.DMA(((side - 1) // 2,)),
            pltpu.SemaphoreType.DMA(()),
        ],
        compiler_params=pltpu.CompilerParams(collective_id=0, has_side_effects=True),
    )(block)


def per_device(
    queries, passages, passage_lengths, positives, positive_lengths, owners, local_ids, teacher
):
    peer_count = lax.axis_size("dp")
    me = lax.axis_index("dp")
    query_count, qlen, dim = queries.shape[1], queries.shape[2], queries.shape[3]
    cand_count = owners.shape[2]
    pass_count, plen = passages.shape[1], passages.shape[2]
    pairs = query_count * cand_count
    slots = 4
    lanes = slots * qlen
    group_cap = peer_count * slots // slots + pass_count

    positive_unit = unit_rows(positives[0]).reshape(query_count * plen, dim)
    length_row = jnp.zeros((16, dim), jnp.bfloat16).at[0, :query_count].set(
        positive_lengths[0].astype(jnp.bfloat16)
    )
    doc_block = jnp.concatenate([positive_unit, length_row], axis=0)
    column_docs = lax.all_gather(doc_block, "blk", axis=0)
    groups = column_docs.shape[0]
    doc_lengths = column_docs[:, query_count * plen, :query_count].astype(jnp.int32).reshape(-1)

    query_unit = unit_rows(queries[0]).reshape(query_count * qlen, dim)
    id_rows = jnp.stack(
        [
            jnp.clip(owners[0, :, :, 0].reshape(pairs), 0, peer_count - 1),
            jnp.clip(local_ids[0].reshape(pairs), 0, pass_count - 1),
        ]
    ).astype(jnp.bfloat16)
    id_rows = id_rows.reshape(2 * pairs // dim, dim)
    id_block = jnp.zeros((16, dim), jnp.bfloat16).at[: id_rows.shape[0]].set(id_rows)
    send = jnp.concatenate([query_unit, id_block], axis=0)
    side = math.isqrt(peer_count)
    gathered = gather_plane(send, side)
    slot_index = jnp.arange(peer_count, dtype=jnp.int32)
    odd = lax.axis_index("blk") % 2
    slot_of_source = jnp.where(odd == 1, (slot_index % side) * side + slot_index // side, slot_index)

    raw_cross = cross_scores(doc_lengths, query_unit, column_docs, query_count, plen)
    logits = jnp.sum(raw_cross.reshape(groups * query_count, query_count, qlen), axis=-1).T
    own_column = lax.axis_index("blk") * query_count + jnp.arange(query_count, dtype=jnp.int32)
    own_logit = jnp.take_along_axis(logits, own_column[:, None], axis=1)[:, 0]
    contrast = jnp.log(jnp.sum(jnp.exp(logits), axis=-1)) - own_logit

    ids = gathered[:, query_count * qlen : query_count * qlen + 2 * pairs // dim, :]
    ids = ids.reshape(peer_count, 2, pairs).astype(jnp.int32)
    pair_owner, pair_local = ids[:, 0, :], ids[:, 1, :]
    hit = (pair_owner == me).astype(jnp.int32)
    rank = jnp.cumsum(hit, axis=1) - hit
    pair_index = lax.broadcasted_iota(jnp.int32, (peer_count, pairs), 1)
    chosen = [(hit > 0) & (rank == r) for r in range(slots)]
    slot_pair = jnp.stack([jnp.sum(jnp.where(c, pair_index, 0), axis=1) for c in chosen], axis=1)
    slot_local = jnp.stack([jnp.sum(jnp.where(c, pair_local, 0), axis=1) for c in chosen], axis=1)
    slot_valid = jnp.stack([jnp.any(c, axis=1) for c in chosen], axis=1).reshape(-1)
    slot_pid = slot_local.reshape(-1)
    slot_src = (lax.broadcasted_iota(jnp.int32, (peer_count, slots), 0)).reshape(-1)
    slot_row = (slot_pair // cand_count).reshape(-1)

    by_pass = (
        slot_valid[:, None] & (slot_pid[:, None] == jnp.arange(pass_count, dtype=jnp.int32)[None, :])
    ).astype(jnp.int32)
    per_pass = jnp.sum(by_pass, axis=0)
    pass_groups = (per_pass + slots - 1) // slots
    pass_base = jnp.cumsum(pass_groups) - pass_groups
    n_groups = jnp.sum(pass_groups).reshape(1)
    in_pass = jnp.sum((jnp.cumsum(by_pass, axis=0) - by_pass) * by_pass, axis=1)
    slot_target = jnp.sum(pass_base[None, :] * by_pass, axis=1) * slots + in_pass
    slot_target = jnp.where(slot_valid, slot_target, group_cap * slots)
    target_hit = slot_target[None, :] == jnp.arange(group_cap * slots, dtype=jnp.int32)[:, None]
    gsrc = jnp.sum(jnp.where(target_hit, slot_src[None, :], 0), axis=1)
    grow = jnp.sum(jnp.where(target_hit, slot_row[None, :], 0), axis=1)
    group_index = jnp.arange(group_cap, dtype=jnp.int32)[:, None]
    gpid = jnp.sum(
        jnp.where(
            (group_index >= pass_base[None, :]) & (group_index < (pass_base + pass_groups)[None, :]),
            jnp.arange(pass_count, dtype=jnp.int32)[None, :],
            0,
        ),
        axis=1,
    )
    passage_unit = unit_rows(passages[0])
    raw = student_scores(
        n_groups, gpid, gsrc, grow, passage_lengths[0], gathered, passage_unit, group_cap, lanes
    )
    group_score = jnp.sum(raw.reshape(group_cap * slots, qlen), axis=-1)
    slot_score = jnp.take(group_score, jnp.minimum(slot_target, group_cap * slots - 1))
    slot_score = jnp.where(slot_valid, slot_score, 0.0).reshape(peer_count, slots)
    slot_score = jnp.take(slot_score, slot_of_source, axis=0)
    returned = lax.all_to_all(slot_score, "dp", split_axis=0, concat_axis=0, tiled=True)

    my_owner = jnp.clip(owners[0, :, :, 0].reshape(pairs), 0, peer_count - 1)
    owner_hot = (my_owner[:, None] == jnp.arange(peer_count, dtype=jnp.int32)[None, :]).astype(
        jnp.int32
    )
    my_rank = jnp.sum((jnp.cumsum(owner_hot, axis=0) - owner_hot) * owner_hot, axis=1)
    student = returned[my_owner, jnp.minimum(my_rank, slots - 1)].reshape(query_count, cand_count)

    teacher_score_rows = teacher[0]
    log_teacher = teacher_score_rows - jnp.log(
        jnp.sum(jnp.exp(teacher_score_rows), axis=-1, keepdims=True)
    )
    log_student = student - jnp.log(jnp.sum(jnp.exp(student), axis=-1, keepdims=True))
    distill = jnp.sum(jnp.exp(log_teacher) * (log_teacher - log_student), axis=-1)
    return (student[None], distill[None], contrast[None])


def solution(mesh):
    in_specs = (
        P("blk", "dp", None, None),
        P("blk", "dp", None, None),
        P("blk", "dp"),
        P("blk", "dp", None, None),
        P("blk", "dp"),
        P("blk", "dp", None, None),
        P("blk", "dp", None),
        P("blk", "dp", None),
    )
    out_specs = (P("blk", "dp", None), P("blk", "dp"), P("blk", "dp"))
    return jax.shard_map(
        per_device, mesh=mesh, in_specs=in_specs, out_specs=out_specs, check_vma=False
    )
```

```python
import functools
import math

import jax
import jax.numpy as jnp
from jax import lax
from jax.experimental import pallas as pl
from jax.experimental.pallas import tpu as pltpu
from jax.sharding import PartitionSpec as P

NEG = -1000000000.0


def unit_rows(values):
    wide = values.astype(jnp.float32)
    total = jnp.sum(wide * wide, axis=-1, keepdims=True) + 1e-06
    return (wide * lax.rsqrt(total)).astype(jnp.bfloat16)


def student_kernel(n_ref, gpid_ref, gsrc_ref, grow_ref, len_ref, g_ref, p_ref, o_ref):
    lanes = o_ref.shape[1]
    slots = gsrc_ref.shape[0] // o_ref.shape[0]
    qlen = lanes // slots
    plen = p_ref.shape[1]
    row_ids = lax.broadcasted_iota(jnp.int32, (plen, lanes), 0)

    def body(g, carry):
        pieces = []
        for r in range(slots):
            src = gsrc_ref[g * slots + r]
            j = grow_ref[g * slots + r]
            pieces.append(g_ref[src, pl.ds(pl.multiple_of(j * qlen, qlen), qlen), :])
        q = jnp.concatenate(pieces, axis=0)
        pidx = gpid_ref[g]
        sim = lax.dot_general(
            p_ref[pidx], q, (((1,), (1,)), ((), ())), preferred_element_type=jnp.float32
        )
        sim = jnp.where(row_ids < len_ref[pidx], sim, NEG)
        o_ref[pl.ds(g, 1), :] = jnp.max(sim, axis=0, keepdims=True)
        return carry

    lax.fori_loop(0, n_ref[0], body, 0)


def student_scores(n_groups, gpid, gsrc, grow, lengths, gathered, passage_unit, group_cap, lanes):
    plen, dim = passage_unit.shape[1], passage_unit.shape[2]
    return pl.pallas_call(
        student_kernel,
        out_shape=jax.ShapeDtypeStruct((group_cap, lanes), jnp.float32),
        in_specs=[pl.BlockSpec(memory_space=pltpu.SMEM)] * 5
        + [pl.BlockSpec(memory_space=pltpu.VMEM)] * 2,
        out_specs=pl.BlockSpec(memory_space=pltpu.VMEM),
        cost_estimate=pl.CostEstimate(
            flops=2 * group_cap * plen * dim * lanes,
            transcendentals=0,
            bytes_accessed=gathered.size * 2 + passage_unit.size * 2 + group_cap * lanes * 4,
        ),
    )(n_groups, gpid, gsrc, grow, lengths, gathered, passage_unit)


def cross_kernel(len_ref, q_ref, p_ref, o_ref, *, plen):
    groups = p_ref.shape[0]
    docs = o_ref.shape[0] // groups
    row_ids = lax.broadcasted_iota(jnp.int32, (plen, q_ref.shape[0]), 0)
    q = q_ref[...]
    for e in range(groups):
        for k in range(docs):
            sim = lax.dot_general(
                p_ref[e, k * plen : (k + 1) * plen, :],
                q,
                (((1,), (1,)), ((), ())),
                preferred_element_type=jnp.float32,
            )
            sim = jnp.where(row_ids < len_ref[e * docs + k], sim, NEG)
            o_ref[pl.ds(e * docs + k, 1), :] = jnp.max(sim, axis=0, keepdims=True)


def cross_scores(lengths, query_rows, gathered_docs, doc_count, plen):
    groups, rows, dim = gathered_docs.shape
    cols = query_rows.shape[0]
    return pl.pallas_call(
        functools.partial(cross_kernel, plen=plen),
        out_shape=jax.ShapeDtypeStruct((groups * doc_count, cols), jnp.float32),
        in_specs=[pl.BlockSpec(memory_space=pltpu.SMEM)]
        + [pl.BlockSpec(memory_space=pltpu.VMEM)] * 2,
        out_specs=pl.BlockSpec(memory_space=pltpu.VMEM),
        cost_estimate=pl.CostEstimate(
            flops=2 * groups * rows * dim * cols,
            transcendentals=0,
            bytes_accessed=query_rows.size * 2 + gathered_docs.size * 2 + groups * doc_count * cols * 4,
        ),
    )(lengths, query_rows, gathered_docs)


def exchange_kernel(
    x_ref, d_ref, g_ref, e_ref, ring_send, ring_recv, up_send, up_recv, dn_send, dn_recv,
    blk_send, blk_recv, own_sem, doc_sem, *, side
):
    mesh_ids = pl.DeviceIdType.MESH
    dp = lax.axis_index("dp")
    odd = lax.axis_index("blk") % 2
    high, low = dp // side, dp % side
    p1 = odd * high + (1 - odd) * low
    p2 = odd * low + (1 - odd) * high

    def dp_of(q1, q2):
        return odd * (q1 * side + q2) + (1 - odd) * (q2 * side + q1)

    ring_peers = [dp_of((p1 + d) % side, p2) for d in range(1, side)]
    up_peer = dp_of(p1, (p2 + 1) % side)
    dn_peer = dp_of(p1, (p2 + side - 1) % side)

    groups = e_ref.shape[0]
    me_blk = lax.axis_index("blk")
    blk_peers = [(me_blk + e) % groups for e in range(1, groups)]

    barrier = pltpu.get_barrier_semaphore()
    for peer in ring_peers + [up_peer, dn_peer]:
        pl.semaphore_signal(barrier, inc=1, device_id={"dp": peer}, device_id_type=mesh_ids)
    for peer in blk_peers:
        pl.semaphore_signal(barrier, inc=1, device_id={"blk": peer}, device_id_type=mesh_ids)
    pl.semaphore_wait(barrier, len(ring_peers) + 2 + len(blk_peers))

    docs = []
    for e in range(1, groups):
        copy = pltpu.make_async_remote_copy(
            src_ref=d_ref,
            dst_ref=e_ref.at[me_blk],
            send_sem=blk_send.at[e - 1],
            recv_sem=blk_recv.at[e - 1],
            device_id={"blk": blk_peers[e - 1]},
            device_id_type=mesh_ids,
        )
        copy.start()
        docs.append(copy)
    own_doc = pltpu.make_async_copy(d_ref, e_ref.at[me_blk], doc_sem)
    own_doc.start()

    my_slot = p2 * side + p1
    own = pltpu.make_async_copy(x_ref, g_ref.at[my_slot], own_sem)
    own.start()
    ring = []
    for d in range(1, side):
        copy = pltpu.make_async_remote_copy(
            src_ref=x_ref,
            dst_ref=g_ref.at[my_slot],
            send_sem=ring_send.at[d - 1],
            recv_sem=ring_recv.at[d - 1],
            device_id={"dp": ring_peers[d - 1]},
            device_id_type=mesh_ids,
        )
        copy.start()
        ring.append(copy)
    for copy in ring:
        copy.wait_recv()
    own.wait()

    def row(r):
        return g_ref.at[pl.ds(pl.multiple_of(r * side, side), side)]

    ups, dns = [], []
    up_steps, dn_steps = side // 2, (side - 1) // 2
    for t in range(max(up_steps, dn_steps)):
        if t < up_steps:
            if t > 0:
                ups[t - 1].wait_recv()
            r = (p2 + side - t) % side
            copy = pltpu.make_async_remote_copy(
                src_ref=row(r),
                dst_ref=row(r),
                send_sem=up_send.at[t],
                recv_sem=up_recv.at[t],
                device_id={"dp": up_peer},
                device_id_type=mesh_ids,
            )
            copy.start()
            ups.append(copy)
        if t < dn_steps:
            if t > 0:
                dns[t - 1].wait_recv()
            r = (p2 + t) % side
            copy = pltpu.make_async_remote_copy(
                src_ref=row(r),
                dst_ref=row(r),
                send_sem=dn_send.at[t],
                recv_sem=dn_recv.at[t],
                device_id={"dp": dn_peer},
                device_id_type=mesh_ids,
            )
            copy.start()
            dns.append(copy)
    ups[-1].wait_recv()
    dns[-1].wait_recv()
    for copy in docs:
        copy.wait_recv()
    own_doc.wait()
    for copy in ring + ups + dns + docs:
        copy.wait_send()


def gather_plane(block, doc_block, side, groups):
    rows, dim = block.shape
    count = side * side
    return pl.pallas_call(
        functools.partial(exchange_kernel, side=side),
        out_shape=(
            jax.ShapeDtypeStruct((count, rows, dim), block.dtype),
            jax.ShapeDtypeStruct((groups,) + doc_block.shape, doc_block.dtype),
        ),
        in_specs=[pl.BlockSpec(memory_space=pltpu.VMEM)] * 2,
        out_specs=(pl.BlockSpec(memory_space=pltpu.VMEM),) * 2,
        scratch_shapes=[
            pltpu.SemaphoreType.DMA((side - 1,)),
            pltpu.SemaphoreType.DMA((side - 1,)),
            pltpu.SemaphoreType.DMA((side // 2,)),
            pltpu.SemaphoreType.DMA((side // 2,)),
            pltpu.SemaphoreType.DMA(((side - 1) // 2,)),
            pltpu.SemaphoreType.DMA(((side - 1) // 2,)),
            pltpu.SemaphoreType.DMA((groups - 1,)),
            pltpu.SemaphoreType.DMA((groups - 1,)),
            pltpu.SemaphoreType.DMA(()),
            pltpu.SemaphoreType.DMA(()),
        ],
        compiler_params=pltpu.CompilerParams(collective_id=0, has_side_effects=True),
    )(block, doc_block)


def return_kernel(x_ref, o_ref, send_sems, recv_sems, own_sem):
    mesh_ids = pl.DeviceIdType.MESH
    count = x_ref.shape[0]
    me = lax.axis_index("dp")
    barrier = pltpu.get_barrier_semaphore()

    def signal(d, carry):
        pl.semaphore_signal(
            barrier, inc=1, device_id={"dp": (me + d) % count}, device_id_type=mesh_ids
        )
        return carry

    lax.fori_loop(1, count, signal, 0)
    pl.semaphore_wait(barrier, count - 1)
    own = pltpu.make_async_copy(x_ref.at[me], o_ref.at[me], own_sem)
    own.start()

    def describe(d):
        target = (me + d) % count
        return pltpu.make_async_remote_copy(
            src_ref=x_ref.at[target],
            dst_ref=o_ref.at[me],
            send_sem=send_sems.at[d - 1],
            recv_sem=recv_sems.at[d - 1],
            device_id={"dp": target},
            device_id_type=mesh_ids,
        )

    def start(d, carry):
        describe(d).start()
        return carry

    def finish(d, carry):
        copy = describe(d)
        copy.wait_recv()
        copy.wait_send()
        return carry

    lax.fori_loop(1, count, start, 0)
    own.wait()
    lax.fori_loop(1, count, finish, 0)


def return_scores(rows):
    count = rows.shape[0]
    return pl.pallas_call(
        return_kernel,
        out_shape=jax.ShapeDtypeStruct(rows.shape, rows.dtype),
        in_specs=[pl.BlockSpec(memory_space=pltpu.VMEM)],
        out_specs=pl.BlockSpec(memory_space=pltpu.VMEM),
        scratch_shapes=[
            pltpu.SemaphoreType.DMA((count - 1,)),
            pltpu.SemaphoreType.DMA((count - 1,)),
            pltpu.SemaphoreType.DMA(()),
        ],
        compiler_params=pltpu.CompilerParams(collective_id=1, has_side_effects=True),
    )(rows)


def per_device(
    queries, passages, passage_lengths, positives, positive_lengths, owners, local_ids, teacher
):
    peer_count = lax.axis_size("dp")
    me = lax.axis_index("dp")
    query_count, qlen, dim = queries.shape[1], queries.shape[2], queries.shape[3]
    cand_count = owners.shape[2]
    pass_count, plen = passages.shape[1], passages.shape[2]
    pairs = query_count * cand_count
    slots = 4
    lanes = slots * qlen
    group_cap = peer_count * slots // slots + pass_count

    positive_unit = unit_rows(positives[0]).reshape(query_count * plen, dim)
    length_row = jnp.zeros((16, dim), jnp.bfloat16).at[0, :query_count].set(
        positive_lengths[0].astype(jnp.bfloat16)
    )
    doc_block = jnp.concatenate([positive_unit, length_row], axis=0)

    query_unit = unit_rows(queries[0]).reshape(query_count * qlen, dim)
    id_rows = jnp.stack(
        [
            jnp.clip(owners[0, :, :, 0].reshape(pairs), 0, peer_count - 1),
            jnp.clip(local_ids[0].reshape(pairs), 0, pass_count - 1),
        ]
    ).astype(jnp.bfloat16)
    id_rows = id_rows.reshape(2 * pairs // dim, dim)
    id_block = jnp.zeros((16, dim), jnp.bfloat16).at[: id_rows.shape[0]].set(id_rows)
    send = jnp.concatenate([query_unit, id_block], axis=0)
    side = math.isqrt(peer_count)
    groups = lax.axis_size("blk")
    gathered, column_docs = gather_plane(send, doc_block, side, groups)
    doc_lengths = column_docs[:, query_count * plen, :query_count].astype(jnp.int32).reshape(-1)
    slot_index = jnp.arange(peer_count, dtype=jnp.int32)
    odd = lax.axis_index("blk") % 2
    slot_of_source = jnp.where(odd == 1, (slot_index % side) * side + slot_index // side, slot_index)

    raw_cross = cross_scores(doc_lengths, query_unit, column_docs, query_count, plen)
    logits = jnp.sum(raw_cross.reshape(groups * query_count, query_count, qlen), axis=-1).T
    own_column = lax.axis_index("blk") * query_count + jnp.arange(query_count, dtype=jnp.int32)
    own_logit = jnp.take_along_axis(logits, own_column[:, None], axis=1)[:, 0]
    contrast = jnp.log(jnp.sum(jnp.exp(logits), axis=-1)) - own_logit

    ids = gathered[:, query_count * qlen : query_count * qlen + 2 * pairs // dim, :]
    ids = ids.reshape(peer_count, 2, pairs).astype(jnp.int32)
    pair_owner, pair_local = ids[:, 0, :], ids[:, 1, :]
    hit = (pair_owner == me).astype(jnp.int32)
    rank = jnp.cumsum(hit, axis=1) - hit
    pair_index = lax.broadcasted_iota(jnp.int32, (peer_count, pairs), 1)
    chosen = [(hit > 0) & (rank == r) for r in range(slots)]
    slot_pair = jnp.stack([jnp.sum(jnp.where(c, pair_index, 0), axis=1) for c in chosen], axis=1)
    slot_local = jnp.stack([jnp.sum(jnp.where(c, pair_local, 0), axis=1) for c in chosen], axis=1)
    slot_valid = jnp.stack([jnp.any(c, axis=1) for c in chosen], axis=1).reshape(-1)
    slot_pid = slot_local.reshape(-1)
    slot_src = (lax.broadcasted_iota(jnp.int32, (peer_count, slots), 0)).reshape(-1)
    slot_row = (slot_pair // cand_count).reshape(-1)

    by_pass = (
        slot_valid[:, None] & (slot_pid[:, None] == jnp.arange(pass_count, dtype=jnp.int32)[None, :])
    ).astype(jnp.int32)
    per_pass = jnp.sum(by_pass, axis=0)
    pass_groups = (per_pass + slots - 1) // slots
    pass_base = jnp.cumsum(pass_groups) - pass_groups
    n_groups = jnp.sum(pass_groups).reshape(1)
    in_pass = jnp.sum((jnp.cumsum(by_pass, axis=0) - by_pass) * by_pass, axis=1)
    slot_target = jnp.sum(pass_base[None, :] * by_pass, axis=1) * slots + in_pass
    slot_target = jnp.where(slot_valid, slot_target, group_cap * slots)
    target_hit = slot_target[None, :] == jnp.arange(group_cap * slots, dtype=jnp.int32)[:, None]
    gsrc = jnp.sum(jnp.where(target_hit, slot_src[None, :], 0), axis=1)
    grow = jnp.sum(jnp.where(target_hit, slot_row[None, :], 0), axis=1)
    group_index = jnp.arange(group_cap, dtype=jnp.int32)[:, None]
    gpid = jnp.sum(
        jnp.where(
            (group_index >= pass_base[None, :]) & (group_index < (pass_base + pass_groups)[None, :]),
            jnp.arange(pass_count, dtype=jnp.int32)[None, :],
            0,
        ),
        axis=1,
    )
    passage_unit = unit_rows(passages[0])
    raw = student_scores(
        n_groups, gpid, gsrc, grow, passage_lengths[0], gathered, passage_unit, group_cap, lanes
    )
    group_score = jnp.sum(raw.reshape(group_cap * slots, qlen), axis=-1)
    slot_score = jnp.take(group_score, jnp.minimum(slot_target, group_cap * slots - 1))
    slot_score = jnp.where(slot_valid, slot_score, 0.0).reshape(peer_count, slots)
    slot_score = jnp.take(slot_score, slot_of_source, axis=0)
    padded = jnp.zeros((peer_count, 8, 128), jnp.float32).at[:, 0, :slots].set(slot_score)
    returned = return_scores(padded)[:, 0, :slots]

    my_owner = jnp.clip(owners[0, :, :, 0].reshape(pairs), 0, peer_count - 1)
    owner_hot = (my_owner[:, None] == jnp.arange(peer_count, dtype=jnp.int32)[None, :]).astype(
        jnp.int32
    )
    my_rank = jnp.sum((jnp.cumsum(owner_hot, axis=0) - owner_hot) * owner_hot, axis=1)
    student = returned[my_owner, jnp.minimum(my_rank, slots - 1)].reshape(query_count, cand_count)

    teacher_score_rows = teacher[0]
    log_teacher = teacher_score_rows - jnp.log(
        jnp.sum(jnp.exp(teacher_score_rows), axis=-1, keepdims=True)
    )
    log_student = student - jnp.log(jnp.sum(jnp.exp(student), axis=-1, keepdims=True))
    distill = jnp.sum(jnp.exp(log_teacher) * (log_teacher - log_student), axis=-1)
    return (student[None], distill[None], contrast[None])


def solution(mesh):
    in_specs = (
        P("blk", "dp", None, None),
        P("blk", "dp", None, None),
        P("blk", "dp"),
        P("blk", "dp", None, None),
        P("blk", "dp"),
        P("blk", "dp", None, None),
        P("blk", "dp", None),
        P("blk", "dp", None),
    )
    out_specs = (P("blk", "dp", None), P("blk", "dp"), P("blk", "dp"))
    return jax.shard_map(
        per_device, mesh=mesh, in_specs=in_specs, out_specs=out_specs, check_vma=False
    )
```

```python
import functools
import math

import jax
import jax.numpy as jnp
from jax import lax
from jax.experimental import pallas as pl
from jax.experimental.pallas import tpu as pltpu
from jax.sharding import PartitionSpec as P

NEG = -1000000000.0


def student_kernel(n_ref, gpid_ref, gsrc_ref, grow_ref, len_ref, g_ref, p_ref, o_ref):
    lanes = o_ref.shape[1]
    slots = gsrc_ref.shape[0] // o_ref.shape[0]
    qlen = lanes // slots
    plen = p_ref.shape[1]
    row_ids = lax.broadcasted_iota(jnp.int32, (plen, lanes), 0)

    def body(g, carry):
        pieces = []
        for r in range(slots):
            src = gsrc_ref[g * slots + r]
            j = grow_ref[g * slots + r]
            pieces.append(g_ref[src, pl.ds(pl.multiple_of(j * qlen, qlen), qlen), :])
        q = jnp.concatenate(pieces, axis=0)
        pidx = gpid_ref[g]
        sim = lax.dot_general(
            p_ref[pidx], q, (((1,), (1,)), ((), ())), preferred_element_type=jnp.float32
        )
        sim = jnp.where(row_ids < len_ref[pidx], sim, NEG)
        o_ref[pl.ds(g, 1), :] = jnp.max(sim, axis=0, keepdims=True)
        return carry

    lax.fori_loop(0, n_ref[0], body, 0)


def student_scores(n_groups, gpid, gsrc, grow, lengths, gathered, passage_unit, group_cap, lanes):
    plen, dim = passage_unit.shape[1], passage_unit.shape[2]
    return pl.pallas_call(
        student_kernel,
        out_shape=jax.ShapeDtypeStruct((group_cap, lanes), jnp.float32),
        in_specs=[pl.BlockSpec(memory_space=pltpu.SMEM)] * 5
        + [pl.BlockSpec(memory_space=pltpu.VMEM)] * 2,
        out_specs=pl.BlockSpec(memory_space=pltpu.VMEM),
        cost_estimate=pl.CostEstimate(
            flops=2 * group_cap * plen * dim * lanes,
            transcendentals=0,
            bytes_accessed=gathered.size * 2 + passage_unit.size * 2 + group_cap * lanes * 4,
        ),
    )(n_groups, gpid, gsrc, grow, lengths, gathered, passage_unit)


def unit_block(values):
    wide = values.astype(jnp.float32)
    total = jnp.sum(wide * wide, axis=-1, keepdims=True) + 1e-06
    return (wide * lax.rsqrt(total)).astype(jnp.bfloat16)


def exchange_kernel(
    q_ref, id_ref, pos_ref, lrow_ref, pas_ref,
    g_ref, e_ref, pu_ref, c_ref,
    x_buf, d_buf, ring_send, ring_recv, up_send, up_recv, dn_send, dn_recv,
    blk_send, blk_recv, own_sem, doc_sem, *, side, plen
):
    mesh_ids = pl.DeviceIdType.MESH
    dp = lax.axis_index("dp")
    odd = lax.axis_index("blk") % 2
    high, low = dp // side, dp % side
    p1 = odd * high + (1 - odd) * low
    p2 = odd * low + (1 - odd) * high

    def dp_of(q1, q2):
        return odd * (q1 * side + q2) + (1 - odd) * (q2 * side + q1)

    ring_peers = [dp_of((p1 + d) % side, p2) for d in range(1, side)]
    up_peer = dp_of(p1, (p2 + 1) % side)
    dn_peer = dp_of(p1, (p2 + side - 1) % side)
    groups = e_ref.shape[0]
    me_blk = lax.axis_index("blk")
    blk_peers = [(me_blk + e) % groups for e in range(1, groups)]

    barrier = pltpu.get_barrier_semaphore()
    for peer in ring_peers + [up_peer, dn_peer]:
        pl.semaphore_signal(barrier, inc=1, device_id={"dp": peer}, device_id_type=mesh_ids)
    for peer in blk_peers:
        pl.semaphore_signal(barrier, inc=1, device_id={"blk": peer}, device_id_type=mesh_ids)

    nq, npos = q_ref.shape[0], pos_ref.shape[0]
    x_buf[0:nq, :] = unit_block(q_ref[...])
    x_buf[nq:, :] = id_ref[...]
    d_buf[0:npos, :] = unit_block(pos_ref[...])
    d_buf[npos:, :] = lrow_ref[...]
    pl.semaphore_wait(barrier, len(ring_peers) + 2 + len(blk_peers))

    docs = []
    for e in range(1, groups):
        copy = pltpu.make_async_remote_copy(
            src_ref=d_buf,
            dst_ref=e_ref.at[me_blk],
            send_sem=blk_send.at[e - 1],
            recv_sem=blk_recv.at[e - 1],
            device_id={"blk": blk_peers[e - 1]},
            device_id_type=mesh_ids,
        )
        copy.start()
        docs.append(copy)
    own_doc = pltpu.make_async_copy(d_buf, e_ref.at[me_blk], doc_sem)
    own_doc.start()

    my_slot = p2 * side + p1
    own = pltpu.make_async_copy(x_buf, g_ref.at[my_slot], own_sem)
    own.start()
    ring = []
    for d in range(1, side):
        copy = pltpu.make_async_remote_copy(
            src_ref=x_buf,
            dst_ref=g_ref.at[my_slot],
            send_sem=ring_send.at[d - 1],
            recv_sem=ring_recv.at[d - 1],
            device_id={"dp": ring_peers[d - 1]},
            device_id_type=mesh_ids,
        )
        copy.start()
        ring.append(copy)
    for copy in ring:
        copy.wait_recv()
    own.wait()

    def row(r):
        return g_ref.at[pl.ds(pl.multiple_of(r * side, side), side)]

    def normalize_passages():
        for p in range(pas_ref.shape[0]):
            pu_ref[p] = unit_block(pas_ref[p])

    def score_positives():
        for copy in docs:
            copy.wait_recv()
        own_doc.wait()
        docs_per_group = c_ref.shape[0] // groups
        q = x_buf[0:nq, :]
        row_ids = lax.broadcasted_iota(jnp.int32, (plen, nq), 0).astype(jnp.float32)
        lane = lax.broadcasted_iota(jnp.int32, (1, lrow_ref.shape[1]), 1)
        for e in range(groups):
            lengths = e_ref[e, npos:, :].astype(jnp.float32)[0:1, :]
            for k in range(docs_per_group):
                kept = jnp.sum(jnp.where(lane == k, lengths, 0.0), axis=1, keepdims=True)
                sim = lax.dot_general(
                    e_ref[e, k * plen : (k + 1) * plen, :],
                    q,
                    (((1,), (1,)), ((), ())),
                    preferred_element_type=jnp.float32,
                )
                sim = jnp.where(row_ids < kept, sim, NEG)
                c_ref[pl.ds(e * docs_per_group + k, 1), :] = jnp.max(sim, axis=0, keepdims=True)

    ups, dns = [], []
    up_steps, dn_steps = side // 2, (side - 1) // 2
    steps = max(up_steps, dn_steps)
    for t in range(steps):
        if t < up_steps:
            if t > 0:
                ups[t - 1].wait_recv()
            r = (p2 + side - t) % side
            copy = pltpu.make_async_remote_copy(
                src_ref=row(r),
                dst_ref=row(r),
                send_sem=up_send.at[t],
                recv_sem=up_recv.at[t],
                device_id={"dp": up_peer},
                device_id_type=mesh_ids,
            )
            copy.start()
            ups.append(copy)
        if t < dn_steps:
            if t > 0:
                dns[t - 1].wait_recv()
            r = (p2 + t) % side
            copy = pltpu.make_async_remote_copy(
                src_ref=row(r),
                dst_ref=row(r),
                send_sem=dn_send.at[t],
                recv_sem=dn_recv.at[t],
                device_id={"dp": dn_peer},
                device_id_type=mesh_ids,
            )
            copy.start()
            dns.append(copy)
        if t == 0:
            normalize_passages()
        if t == min(2, steps - 1):
            score_positives()
    ups[-1].wait_recv()
    dns[-1].wait_recv()
    for copy in ring + ups + dns + docs:
        copy.wait_send()


def gather_plane(queries, id_block, positives, length_row, passages, side, groups, doc_count):
    nq, dim = queries.shape
    rows = nq + id_block.shape[0]
    doc_rows = positives.shape[0] + length_row.shape[0]
    plen = passages.shape[1]
    count = side * side
    return pl.pallas_call(
        functools.partial(exchange_kernel, side=side, plen=plen),
        out_shape=(
            jax.ShapeDtypeStruct((count, rows, dim), jnp.bfloat16),
            jax.ShapeDtypeStruct((groups, doc_rows, dim), jnp.bfloat16),
            jax.ShapeDtypeStruct(passages.shape, jnp.bfloat16),
            jax.ShapeDtypeStruct((groups * doc_count, nq), jnp.float32),
        ),
        in_specs=[pl.BlockSpec(memory_space=pltpu.VMEM)] * 5,
        out_specs=(pl.BlockSpec(memory_space=pltpu.VMEM),) * 4,
        scratch_shapes=[
            pltpu.VMEM((rows, dim), jnp.bfloat16),
            pltpu.VMEM((doc_rows, dim), jnp.bfloat16),
            pltpu.SemaphoreType.DMA((side - 1,)),
            pltpu.SemaphoreType.DMA((side - 1,)),
            pltpu.SemaphoreType.DMA((side // 2,)),
            pltpu.SemaphoreType.DMA((side // 2,)),
            pltpu.SemaphoreType.DMA(((side - 1) // 2,)),
            pltpu.SemaphoreType.DMA(((side - 1) // 2,)),
            pltpu.SemaphoreType.DMA((groups - 1,)),
            pltpu.SemaphoreType.DMA((groups - 1,)),
            pltpu.SemaphoreType.DMA(()),
            pltpu.SemaphoreType.DMA(()),
        ],
        compiler_params=pltpu.CompilerParams(collective_id=0, has_side_effects=True),
    )(queries, id_block, positives, length_row, passages)


def return_kernel(x_ref, o_ref, send_sems, recv_sems, own_sem):
    mesh_ids = pl.DeviceIdType.MESH
    count = x_ref.shape[0]
    me = lax.axis_index("dp")
    barrier = pltpu.get_barrier_semaphore()

    def signal(d, carry):
        pl.semaphore_signal(
            barrier, inc=1, device_id={"dp": (me + d) % count}, device_id_type=mesh_ids
        )
        return carry

    lax.fori_loop(1, count, signal, 0)
    pl.semaphore_wait(barrier, count - 1)
    own = pltpu.make_async_copy(x_ref.at[me], o_ref.at[me], own_sem)
    own.start()

    def describe(d):
        target = (me + d) % count
        return pltpu.make_async_remote_copy(
            src_ref=x_ref.at[target],
            dst_ref=o_ref.at[me],
            send_sem=send_sems.at[d - 1],
            recv_sem=recv_sems.at[d - 1],
            device_id={"dp": target},
            device_id_type=mesh_ids,
        )

    def start(d, carry):
        describe(d).start()
        return carry

    def finish(d, carry):
        copy = describe(d)
        copy.wait_recv()
        copy.wait_send()
        return carry

    lax.fori_loop(1, count, start, 0)
    own.wait()
    lax.fori_loop(1, count, finish, 0)


def return_scores(rows):
    count = rows.shape[0]
    return pl.pallas_call(
        return_kernel,
        out_shape=jax.ShapeDtypeStruct(rows.shape, rows.dtype),
        in_specs=[pl.BlockSpec(memory_space=pltpu.VMEM)],
        out_specs=pl.BlockSpec(memory_space=pltpu.VMEM),
        scratch_shapes=[
            pltpu.SemaphoreType.DMA((count - 1,)),
            pltpu.SemaphoreType.DMA((count - 1,)),
            pltpu.SemaphoreType.DMA(()),
        ],
        compiler_params=pltpu.CompilerParams(collective_id=1, has_side_effects=True),
    )(rows)


def per_device(
    queries, passages, passage_lengths, positives, positive_lengths, owners, local_ids, teacher
):
    peer_count = lax.axis_size("dp")
    me = lax.axis_index("dp")
    query_count, qlen, dim = queries.shape[1], queries.shape[2], queries.shape[3]
    cand_count = owners.shape[2]
    pass_count, plen = passages.shape[1], passages.shape[2]
    pairs = query_count * cand_count
    slots = 4
    lanes = slots * qlen
    group_cap = peer_count * slots // slots + pass_count

    groups = lax.axis_size("blk")
    length_row = jnp.zeros((16, dim), jnp.bfloat16).at[0, :query_count].set(
        positive_lengths[0].astype(jnp.bfloat16)
    )
    id_rows = jnp.stack(
        [
            jnp.clip(owners[0, :, :, 0].reshape(pairs), 0, peer_count - 1),
            jnp.clip(local_ids[0].reshape(pairs), 0, pass_count - 1),
        ]
    ).astype(jnp.bfloat16)
    id_rows = id_rows.reshape(2 * pairs // dim, dim)
    id_block = jnp.zeros((16, dim), jnp.bfloat16).at[: id_rows.shape[0]].set(id_rows)
    side = math.isqrt(peer_count)
    gathered, column_docs, passage_unit, raw_cross = gather_plane(
        queries[0].reshape(query_count * qlen, dim),
        id_block,
        positives[0].reshape(query_count * plen, dim),
        length_row,
        passages[0],
        side,
        groups,
        query_count,
    )
    slot_index = jnp.arange(peer_count, dtype=jnp.int32)
    odd = lax.axis_index("blk") % 2
    slot_of_source = jnp.where(odd == 1, (slot_index % side) * side + slot_index // side, slot_index)

    logits = jnp.sum(raw_cross.reshape(groups * query_count, query_count, qlen), axis=-1).T
    own_column = lax.axis_index("blk") * query_count + jnp.arange(query_count, dtype=jnp.int32)
    own_logit = jnp.take_along_axis(logits, own_column[:, None], axis=1)[:, 0]
    contrast = jnp.log(jnp.sum(jnp.exp(logits), axis=-1)) - own_logit

    ids = gathered[:, query_count * qlen : query_count * qlen + 2 * pairs // dim, :]
    ids = ids.reshape(peer_count, 2, pairs).astype(jnp.int32)
    pair_owner, pair_local = ids[:, 0, :], ids[:, 1, :]
    hit = (pair_owner == me).astype(jnp.int32)
    rank = jnp.cumsum(hit, axis=1) - hit
    pair_index = lax.broadcasted_iota(jnp.int32, (peer_count, pairs), 1)
    chosen = [(hit > 0) & (rank == r) for r in range(slots)]
    slot_pair = jnp.stack([jnp.sum(jnp.where(c, pair_index, 0), axis=1) for c in chosen], axis=1)
    slot_local = jnp.stack([jnp.sum(jnp.where(c, pair_local, 0), axis=1) for c in chosen], axis=1)
    slot_valid = jnp.stack([jnp.any(c, axis=1) for c in chosen], axis=1).reshape(-1)
    slot_pid = slot_local.reshape(-1)
    slot_src = (lax.broadcasted_iota(jnp.int32, (peer_count, slots), 0)).reshape(-1)
    slot_row = (slot_pair // cand_count).reshape(-1)

    by_pass = (
        slot_valid[:, None] & (slot_pid[:, None] == jnp.arange(pass_count, dtype=jnp.int32)[None, :])
    ).astype(jnp.int32)
    per_pass = jnp.sum(by_pass, axis=0)
    pass_groups = (per_pass + slots - 1) // slots
    pass_base = jnp.cumsum(pass_groups) - pass_groups
    n_groups = jnp.sum(pass_groups).reshape(1)
    in_pass = jnp.sum((jnp.cumsum(by_pass, axis=0) - by_pass) * by_pass, axis=1)
    slot_target = jnp.sum(pass_base[None, :] * by_pass, axis=1) * slots + in_pass
    slot_target = jnp.where(slot_valid, slot_target, group_cap * slots)
    target_hit = slot_target[None, :] == jnp.arange(group_cap * slots, dtype=jnp.int32)[:, None]
    gsrc = jnp.sum(jnp.where(target_hit, slot_src[None, :], 0), axis=1)
    grow = jnp.sum(jnp.where(target_hit, slot_row[None, :], 0), axis=1)
    group_index = jnp.arange(group_cap, dtype=jnp.int32)[:, None]
    gpid = jnp.sum(
        jnp.where(
            (group_index >= pass_base[None, :]) & (group_index < (pass_base + pass_groups)[None, :]),
            jnp.arange(pass_count, dtype=jnp.int32)[None, :],
            0,
        ),
        axis=1,
    )
    raw = student_scores(
        n_groups, gpid, gsrc, grow, passage_lengths[0], gathered, passage_unit, group_cap, lanes
    )
    group_score = jnp.sum(raw.reshape(group_cap * slots, qlen), axis=-1)
    slot_score = jnp.take(group_score, jnp.minimum(slot_target, group_cap * slots - 1))
    slot_score = jnp.where(slot_valid, slot_score, 0.0).reshape(peer_count, slots)
    slot_score = jnp.take(slot_score, slot_of_source, axis=0)
    padded = jnp.zeros((peer_count, 8, 128), jnp.float32).at[:, 0, :slots].set(slot_score)
    returned = return_scores(padded)[:, 0, :slots]

    my_owner = jnp.clip(owners[0, :, :, 0].reshape(pairs), 0, peer_count - 1)
    owner_hot = (my_owner[:, None] == jnp.arange(peer_count, dtype=jnp.int32)[None, :]).astype(
        jnp.int32
    )
    my_rank = jnp.sum((jnp.cumsum(owner_hot, axis=0) - owner_hot) * owner_hot, axis=1)
    student = returned[my_owner, jnp.minimum(my_rank, slots - 1)].reshape(query_count, cand_count)

    teacher_score_rows = teacher[0]
    log_teacher = teacher_score_rows - jnp.log(
        jnp.sum(jnp.exp(teacher_score_rows), axis=-1, keepdims=True)
    )
    log_student = student - jnp.log(jnp.sum(jnp.exp(student), axis=-1, keepdims=True))
    distill = jnp.sum(jnp.exp(log_teacher) * (log_teacher - log_student), axis=-1)
    return (student[None], distill[None], contrast[None])


def solution(mesh):
    in_specs = (
        P("blk", "dp", None, None),
        P("blk", "dp", None, None),
        P("blk", "dp"),
        P("blk", "dp", None, None),
        P("blk", "dp"),
        P("blk", "dp", None, None),
        P("blk", "dp", None),
        P("blk", "dp", None),
    )
    out_specs = (P("blk", "dp", None), P("blk", "dp"), P("blk", "dp"))
    return jax.shard_map(
        per_device, mesh=mesh, in_specs=in_specs, out_specs=out_specs, check_vma=False
    )
```

```python
import functools
import math

import jax
import jax.numpy as jnp
from jax import lax
from jax.experimental import pallas as pl
from jax.experimental.pallas import tpu as pltpu
from jax.sharding import PartitionSpec as P

NEG = -1000000000.0


def student_kernel(n_ref, gpid_ref, gsrc_ref, grow_ref, len_ref, g_ref, p_ref, o_ref):
    lanes = o_ref.shape[1]
    slots = gsrc_ref.shape[0] // o_ref.shape[0]
    qlen = lanes // slots
    plen = p_ref.shape[1]
    row_ids = lax.broadcasted_iota(jnp.int32, (plen, lanes), 0)

    def body(g, carry):
        pieces = []
        for r in range(slots):
            src = gsrc_ref[g * slots + r]
            j = grow_ref[g * slots + r]
            pieces.append(g_ref[src, pl.ds(pl.multiple_of(j * qlen, qlen), qlen), :])
        q = jnp.concatenate(pieces, axis=0)
        pidx = gpid_ref[g]
        sim = lax.dot_general(
            p_ref[pidx], q, (((1,), (1,)), ((), ())), preferred_element_type=jnp.float32
        )
        sim = jnp.where(row_ids < len_ref[pidx], sim, NEG)
        o_ref[pl.ds(g, 1), :] = jnp.max(sim, axis=0, keepdims=True)
        return carry

    lax.fori_loop(0, n_ref[0], body, 0)


def student_scores(n_groups, gpid, gsrc, grow, lengths, gathered, passage_unit, group_cap, lanes):
    plen, dim = passage_unit.shape[1], passage_unit.shape[2]
    return pl.pallas_call(
        student_kernel,
        out_shape=jax.ShapeDtypeStruct((group_cap, lanes), jnp.float32),
        in_specs=[pl.BlockSpec(memory_space=pltpu.SMEM)] * 5
        + [pl.BlockSpec(memory_space=pltpu.VMEM)] * 2,
        out_specs=pl.BlockSpec(memory_space=pltpu.VMEM),
        cost_estimate=pl.CostEstimate(
            flops=2 * group_cap * plen * dim * lanes,
            transcendentals=0,
            bytes_accessed=gathered.size * 2 + passage_unit.size * 2 + group_cap * lanes * 4,
        ),
    )(n_groups, gpid, gsrc, grow, lengths, gathered, passage_unit)


def unit_block(values):
    wide = values.astype(jnp.float32)
    total = jnp.sum(wide * wide, axis=-1, keepdims=True) + 1e-06
    return (wide * lax.rsqrt(total)).astype(jnp.bfloat16)


def exchange_kernel(
    q_ref, id_ref, pos_ref, lrow_ref, pas_ref,
    g_ref, e_ref, pu_ref, c_ref,
    x_buf, d_buf, ring_send, ring_recv, up_send, up_recv, dn_send, dn_recv,
    blk_send, blk_recv, own_sem, doc_sem, *, side, plen
):
    mesh_ids = pl.DeviceIdType.MESH
    dp = lax.axis_index("dp")
    odd = lax.axis_index("blk") % 2
    high, low = dp // side, dp % side
    p1 = odd * high + (1 - odd) * low
    p2 = odd * low + (1 - odd) * high

    def dp_of(q1, q2):
        return odd * (q1 * side + q2) + (1 - odd) * (q2 * side + q1)

    ring_peers = [dp_of((p1 + d) % side, p2) for d in range(1, side)]
    up_peer = dp_of(p1, (p2 + 1) % side)
    dn_peer = dp_of(p1, (p2 + side - 1) % side)
    groups = e_ref.shape[0]
    me_blk = lax.axis_index("blk")
    blk_peers = [(me_blk + e) % groups for e in range(1, groups)]

    barrier = pltpu.get_barrier_semaphore()
    for peer in ring_peers + [up_peer, dn_peer]:
        pl.semaphore_signal(barrier, inc=1, device_id={"dp": peer}, device_id_type=mesh_ids)
    for peer in blk_peers:
        pl.semaphore_signal(barrier, inc=1, device_id={"blk": peer}, device_id_type=mesh_ids)

    nq, npos = q_ref.shape[0], pos_ref.shape[0]
    x_buf[0:nq, :] = unit_block(q_ref[...])
    x_buf[nq:, :] = id_ref[...]
    d_buf[0:npos, :] = unit_block(pos_ref[...])
    d_buf[npos:, :] = lrow_ref[...]
    pl.semaphore_wait(barrier, len(ring_peers) + 2 + len(blk_peers))

    docs = []
    for e in range(1, groups):
        copy = pltpu.make_async_remote_copy(
            src_ref=d_buf,
            dst_ref=e_ref.at[me_blk],
            send_sem=blk_send.at[e - 1],
            recv_sem=blk_recv.at[e - 1],
            device_id={"blk": blk_peers[e - 1]},
            device_id_type=mesh_ids,
        )
        copy.start()
        docs.append(copy)
    own_doc = pltpu.make_async_copy(d_buf, e_ref.at[me_blk], doc_sem)
    own_doc.start()

    def normalize_passages():
        for p in range(pas_ref.shape[0]):
            pu_ref[p] = unit_block(pas_ref[p])

    def score_positives():
        for copy in docs:
            copy.wait_recv()
        own_doc.wait()
        docs_per_group = c_ref.shape[0] // groups
        q = x_buf[0:nq, :]
        row_ids = lax.broadcasted_iota(jnp.int32, (plen, nq), 0).astype(jnp.float32)
        lane = lax.broadcasted_iota(jnp.int32, (1, lrow_ref.shape[1]), 1)
        for e in range(groups):
            lengths = e_ref[e, npos:, :].astype(jnp.float32)[0:1, :]
            for k in range(docs_per_group):
                kept = jnp.sum(jnp.where(lane == k, lengths, 0.0), axis=1, keepdims=True)
                sim = lax.dot_general(
                    e_ref[e, k * plen : (k + 1) * plen, :],
                    q,
                    (((1,), (1,)), ((), ())),
                    preferred_element_type=jnp.float32,
                )
                sim = jnp.where(row_ids < kept, sim, NEG)
                c_ref[pl.ds(e * docs_per_group + k, 1), :] = jnp.max(sim, axis=0, keepdims=True)

    my_slot = p2 * side + p1
    own = pltpu.make_async_copy(x_buf, g_ref.at[my_slot], own_sem)
    own.start()
    ring = []
    for d in range(1, side):
        copy = pltpu.make_async_remote_copy(
            src_ref=x_buf,
            dst_ref=g_ref.at[my_slot],
            send_sem=ring_send.at[d - 1],
            recv_sem=ring_recv.at[d - 1],
            device_id={"dp": ring_peers[d - 1]},
            device_id_type=mesh_ids,
        )
        copy.start()
        ring.append(copy)
    normalize_passages()
    for copy in ring:
        copy.wait_recv()
    own.wait()

    chunks = up_send.shape[1]
    width = side // chunks
    up_steps, dn_steps = side // 2, (side - 1) // 2
    steps = max(up_steps, dn_steps)

    def forward(t, c, peer, r, sends, recvs):
        part = pl.ds(pl.multiple_of(r * side + c * width, width), width)
        copy = pltpu.make_async_remote_copy(
            src_ref=g_ref.at[part],
            dst_ref=g_ref.at[part],
            send_sem=sends.at[t, c],
            recv_sem=recvs.at[t, c],
            device_id={"dp": peer},
            device_id_type=mesh_ids,
        )
        copy.start()
        return copy

    ups, dns = [], []
    for t in range(steps):
        ups.append([])
        dns.append([])
        for c in range(chunks):
            if t < up_steps:
                if t > 0:
                    ups[t - 1][c].wait_recv()
                ups[t].append(forward(t, c, up_peer, (p2 + side - t) % side, up_send, up_recv))
            if t < dn_steps:
                if t > 0:
                    dns[t - 1][c].wait_recv()
                dns[t].append(forward(t, c, dn_peer, (p2 + t) % side, dn_send, dn_recv))
    score_positives()
    for copy in ups[up_steps - 1] + dns[dn_steps - 1]:
        copy.wait_recv()
    sent = [copy for step in ups + dns for copy in step]
    for copy in ring + sent + docs:
        copy.wait_send()


def gather_plane(queries, id_block, positives, length_row, passages, side, groups, doc_count):
    nq, dim = queries.shape
    rows = nq + id_block.shape[0]
    doc_rows = positives.shape[0] + length_row.shape[0]
    plen = passages.shape[1]
    count = side * side
    chunks = math.gcd(side, 4)
    return pl.pallas_call(
        functools.partial(exchange_kernel, side=side, plen=plen),
        out_shape=(
            jax.ShapeDtypeStruct((count, rows, dim), jnp.bfloat16),
            jax.ShapeDtypeStruct((groups, doc_rows, dim), jnp.bfloat16),
            jax.ShapeDtypeStruct(passages.shape, jnp.bfloat16),
            jax.ShapeDtypeStruct((groups * doc_count, nq), jnp.float32),
        ),
        in_specs=[pl.BlockSpec(memory_space=pltpu.VMEM)] * 5,
        out_specs=(pl.BlockSpec(memory_space=pltpu.VMEM),) * 4,
        scratch_shapes=[
            pltpu.VMEM((rows, dim), jnp.bfloat16),
            pltpu.VMEM((doc_rows, dim), jnp.bfloat16),
            pltpu.SemaphoreType.DMA((side - 1,)),
            pltpu.SemaphoreType.DMA((side - 1,)),
            pltpu.SemaphoreType.DMA((side // 2, chunks)),
            pltpu.SemaphoreType.DMA((side // 2, chunks)),
            pltpu.SemaphoreType.DMA(((side - 1) // 2, chunks)),
            pltpu.SemaphoreType.DMA(((side - 1) // 2, chunks)),
            pltpu.SemaphoreType.DMA((groups - 1,)),
            pltpu.SemaphoreType.DMA((groups - 1,)),
            pltpu.SemaphoreType.DMA(()),
            pltpu.SemaphoreType.DMA(()),
        ],
        compiler_params=pltpu.CompilerParams(collective_id=0, has_side_effects=True),
    )(queries, id_block, positives, length_row, passages)


def return_kernel(x_ref, o_ref, send_sems, recv_sems, own_sem):
    mesh_ids = pl.DeviceIdType.MESH
    count = x_ref.shape[0]
    me = lax.axis_index("dp")
    barrier = pltpu.get_barrier_semaphore()

    def signal(d, carry):
        pl.semaphore_signal(
            barrier, inc=1, device_id={"dp": (me + d) % count}, device_id_type=mesh_ids
        )
        return carry

    lax.fori_loop(1, count, signal, 0)
    pl.semaphore_wait(barrier, count - 1)
    own = pltpu.make_async_copy(x_ref.at[me], o_ref.at[me], own_sem)
    own.start()

    def describe(d):
        target = (me + d) % count
        return pltpu.make_async_remote_copy(
            src_ref=x_ref.at[target],
            dst_ref=o_ref.at[me],
            send_sem=send_sems.at[d - 1],
            recv_sem=recv_sems.at[d - 1],
            device_id={"dp": target},
            device_id_type=mesh_ids,
        )

    def start(d, carry):
        describe(d).start()
        return carry

    def finish(d, carry):
        copy = describe(d)
        copy.wait_recv()
        copy.wait_send()
        return carry

    lax.fori_loop(1, count, start, 0)
    own.wait()
    lax.fori_loop(1, count, finish, 0)


def return_scores(rows):
    count = rows.shape[0]
    return pl.pallas_call(
        return_kernel,
        out_shape=jax.ShapeDtypeStruct(rows.shape, rows.dtype),
        in_specs=[pl.BlockSpec(memory_space=pltpu.VMEM)],
        out_specs=pl.BlockSpec(memory_space=pltpu.VMEM),
        scratch_shapes=[
            pltpu.SemaphoreType.DMA((count - 1,)),
            pltpu.SemaphoreType.DMA((count - 1,)),
            pltpu.SemaphoreType.DMA(()),
        ],
        compiler_params=pltpu.CompilerParams(collective_id=1, has_side_effects=True),
    )(rows)


def per_device(
    queries, passages, passage_lengths, positives, positive_lengths, owners, local_ids, teacher
):
    peer_count = lax.axis_size("dp")
    me = lax.axis_index("dp")
    query_count, qlen, dim = queries.shape[1], queries.shape[2], queries.shape[3]
    cand_count = owners.shape[2]
    pass_count, plen = passages.shape[1], passages.shape[2]
    pairs = query_count * cand_count
    slots = 4
    lanes = slots * qlen
    group_cap = peer_count * slots // slots + pass_count

    groups = lax.axis_size("blk")
    length_row = jnp.zeros((16, dim), jnp.bfloat16).at[0, :query_count].set(
        positive_lengths[0].astype(jnp.bfloat16)
    )
    id_rows = jnp.stack(
        [
            jnp.clip(owners[0, :, :, 0].reshape(pairs), 0, peer_count - 1),
            jnp.clip(local_ids[0].reshape(pairs), 0, pass_count - 1),
        ]
    ).astype(jnp.bfloat16)
    id_rows = id_rows.reshape(2 * pairs // dim, dim)
    id_block = jnp.zeros((16, dim), jnp.bfloat16).at[: id_rows.shape[0]].set(id_rows)
    side = math.isqrt(peer_count)
    gathered, column_docs, passage_unit, raw_cross = gather_plane(
        queries[0].reshape(query_count * qlen, dim),
        id_block,
        positives[0].reshape(query_count * plen, dim),
        length_row,
        passages[0],
        side,
        groups,
        query_count,
    )
    slot_index = jnp.arange(peer_count, dtype=jnp.int32)
    odd = lax.axis_index("blk") % 2
    slot_of_source = jnp.where(odd == 1, (slot_index % side) * side + slot_index // side, slot_index)

    logits = jnp.sum(raw_cross.reshape(groups * query_count, query_count, qlen), axis=-1).T
    own_column = lax.axis_index("blk") * query_count + jnp.arange(query_count, dtype=jnp.int32)
    own_logit = jnp.take_along_axis(logits, own_column[:, None], axis=1)[:, 0]
    contrast = jnp.log(jnp.sum(jnp.exp(logits), axis=-1)) - own_logit

    ids = gathered[:, query_count * qlen : query_count * qlen + 2 * pairs // dim, :]
    ids = ids.reshape(peer_count, 2, pairs).astype(jnp.int32)
    pair_owner, pair_local = ids[:, 0, :], ids[:, 1, :]
    hit = (pair_owner == me).astype(jnp.int32)
    rank = jnp.cumsum(hit, axis=1) - hit
    pair_index = lax.broadcasted_iota(jnp.int32, (peer_count, pairs), 1)
    chosen = [(hit > 0) & (rank == r) for r in range(slots)]
    slot_pair = jnp.stack([jnp.sum(jnp.where(c, pair_index, 0), axis=1) for c in chosen], axis=1)
    slot_local = jnp.stack([jnp.sum(jnp.where(c, pair_local, 0), axis=1) for c in chosen], axis=1)
    slot_valid = jnp.stack([jnp.any(c, axis=1) for c in chosen], axis=1).reshape(-1)
    slot_pid = slot_local.reshape(-1)
    slot_src = (lax.broadcasted_iota(jnp.int32, (peer_count, slots), 0)).reshape(-1)
    slot_row = (slot_pair // cand_count).reshape(-1)

    by_pass = (
        slot_valid[:, None] & (slot_pid[:, None] == jnp.arange(pass_count, dtype=jnp.int32)[None, :])
    ).astype(jnp.int32)
    per_pass = jnp.sum(by_pass, axis=0)
    pass_groups = (per_pass + slots - 1) // slots
    pass_base = jnp.cumsum(pass_groups) - pass_groups
    n_groups = jnp.sum(pass_groups).reshape(1)
    in_pass = jnp.sum((jnp.cumsum(by_pass, axis=0) - by_pass) * by_pass, axis=1)
    slot_target = jnp.sum(pass_base[None, :] * by_pass, axis=1) * slots + in_pass
    slot_target = jnp.where(slot_valid, slot_target, group_cap * slots)
    target_hit = slot_target[None, :] == jnp.arange(group_cap * slots, dtype=jnp.int32)[:, None]
    gsrc = jnp.sum(jnp.where(target_hit, slot_src[None, :], 0), axis=1)
    grow = jnp.sum(jnp.where(target_hit, slot_row[None, :], 0), axis=1)
    group_index = jnp.arange(group_cap, dtype=jnp.int32)[:, None]
    gpid = jnp.sum(
        jnp.where(
            (group_index >= pass_base[None, :]) & (group_index < (pass_base + pass_groups)[None, :]),
            jnp.arange(pass_count, dtype=jnp.int32)[None, :],
            0,
        ),
        axis=1,
    )
    raw = student_scores(
        n_groups, gpid, gsrc, grow, passage_lengths[0], gathered, passage_unit, group_cap, lanes
    )
    group_score = jnp.sum(raw.reshape(group_cap * slots, qlen), axis=-1)
    slot_score = jnp.take(group_score, jnp.minimum(slot_target, group_cap * slots - 1))
    slot_score = jnp.where(slot_valid, slot_score, 0.0).reshape(peer_count, slots)
    slot_score = jnp.take(slot_score, slot_of_source, axis=0)
    padded = jnp.zeros((peer_count, 8, 128), jnp.float32).at[:, 0, :slots].set(slot_score)
    returned = return_scores(padded)[:, 0, :slots]

    my_owner = jnp.clip(owners[0, :, :, 0].reshape(pairs), 0, peer_count - 1)
    owner_hot = (my_owner[:, None] == jnp.arange(peer_count, dtype=jnp.int32)[None, :]).astype(
        jnp.int32
    )
    my_rank = jnp.sum((jnp.cumsum(owner_hot, axis=0) - owner_hot) * owner_hot, axis=1)
    student = returned[my_owner, jnp.minimum(my_rank, slots - 1)].reshape(query_count, cand_count)

    teacher_score_rows = teacher[0]
    log_teacher = teacher_score_rows - jnp.log(
        jnp.sum(jnp.exp(teacher_score_rows), axis=-1, keepdims=True)
    )
    log_student = student - jnp.log(jnp.sum(jnp.exp(student), axis=-1, keepdims=True))
    distill = jnp.sum(jnp.exp(log_teacher) * (log_teacher - log_student), axis=-1)
    return (student[None], distill[None], contrast[None])


def solution(mesh):
    in_specs = (
        P("blk", "dp", None, None),
        P("blk", "dp", None, None),
        P("blk", "dp"),
        P("blk", "dp", None, None),
        P("blk", "dp"),
        P("blk", "dp", None, None),
        P("blk", "dp", None),
        P("blk", "dp", None),
    )
    out_specs = (P("blk", "dp", None), P("blk", "dp"), P("blk", "dp"))
    return jax.shard_map(
        per_device, mesh=mesh, in_specs=in_specs, out_specs=out_specs, check_vma=False
    )
```

```python
import functools
import math

import jax
import jax.numpy as jnp
from jax import lax
from jax.experimental import pallas as pl
from jax.experimental.pallas import tpu as pltpu
from jax.sharding import PartitionSpec as P

NEG = -1000000000.0


def unit_block(values):
    wide = values.astype(jnp.float32)
    total = jnp.sum(wide * wide, axis=-1, keepdims=True) + 1e-06
    return (wide * lax.rsqrt(total)).astype(jnp.bfloat16)


def exchange_kernel(
    q_ref, id_ref, pos_ref, lrow_ref, pas_ref,
    g_ref, e_ref, pu_ref, c_ref,
    x_buf, d_buf, ring_send, ring_recv, up_send, up_recv, dn_send, dn_recv,
    blk_send, blk_recv, own_sem, doc_sem, *, side, plen
):
    mesh_ids = pl.DeviceIdType.MESH
    dp = lax.axis_index("dp")
    odd = lax.axis_index("blk") % 2
    high, low = dp // side, dp % side
    p1 = odd * high + (1 - odd) * low
    p2 = odd * low + (1 - odd) * high

    def dp_of(q1, q2):
        return odd * (q1 * side + q2) + (1 - odd) * (q2 * side + q1)

    ring_peers = [dp_of((p1 + d) % side, p2) for d in range(1, side)]
    up_peer = dp_of(p1, (p2 + 1) % side)
    dn_peer = dp_of(p1, (p2 + side - 1) % side)
    groups = e_ref.shape[0]
    me_blk = lax.axis_index("blk")
    blk_peers = [(me_blk + e) % groups for e in range(1, groups)]

    barrier = pltpu.get_barrier_semaphore()
    for peer in ring_peers + [up_peer, dn_peer]:
        pl.semaphore_signal(barrier, inc=1, device_id={"dp": peer}, device_id_type=mesh_ids)
    for peer in blk_peers:
        pl.semaphore_signal(barrier, inc=1, device_id={"blk": peer}, device_id_type=mesh_ids)

    nq, npos = q_ref.shape[0], pos_ref.shape[0]
    x_buf[0:nq, :] = unit_block(q_ref[...])
    x_buf[nq:, :] = id_ref[...]
    d_buf[0:npos, :] = unit_block(pos_ref[...])
    d_buf[npos:, :] = lrow_ref[...]
    pl.semaphore_wait(barrier, len(ring_peers) + 2 + len(blk_peers))

    docs = []
    for e in range(1, groups):
        copy = pltpu.make_async_remote_copy(
            src_ref=d_buf,
            dst_ref=e_ref.at[me_blk],
            send_sem=blk_send.at[e - 1],
            recv_sem=blk_recv.at[e - 1],
            device_id={"blk": blk_peers[e - 1]},
            device_id_type=mesh_ids,
        )
        copy.start()
        docs.append(copy)
    own_doc = pltpu.make_async_copy(d_buf, e_ref.at[me_blk], doc_sem)
    own_doc.start()

    def normalize_passages():
        for p in range(pas_ref.shape[0]):
            pu_ref[p] = unit_block(pas_ref[p])

    def score_positives():
        for copy in docs:
            copy.wait_recv()
        own_doc.wait()
        docs_per_group = c_ref.shape[0] // groups
        q = x_buf[0:nq, :]
        row_ids = lax.broadcasted_iota(jnp.int32, (plen, nq), 0).astype(jnp.float32)
        lane = lax.broadcasted_iota(jnp.int32, (1, lrow_ref.shape[1]), 1)
        for e in range(groups):
            lengths = e_ref[e, npos:, :].astype(jnp.float32)[0:1, :]
            for k in range(docs_per_group):
                kept = jnp.sum(jnp.where(lane == k, lengths, 0.0), axis=1, keepdims=True)
                sim = lax.dot_general(
                    e_ref[e, k * plen : (k + 1) * plen, :],
                    q,
                    (((1,), (1,)), ((), ())),
                    preferred_element_type=jnp.float32,
                )
                sim = jnp.where(row_ids < kept, sim, NEG)
                c_ref[pl.ds(e * docs_per_group + k, 1), :] = jnp.max(sim, axis=0, keepdims=True)

    my_slot = p2 * side + p1
    own = pltpu.make_async_copy(x_buf, g_ref.at[my_slot], own_sem)
    own.start()
    ring = []
    for d in range(1, side):
        copy = pltpu.make_async_remote_copy(
            src_ref=x_buf,
            dst_ref=g_ref.at[my_slot],
            send_sem=ring_send.at[d - 1],
            recv_sem=ring_recv.at[d - 1],
            device_id={"dp": ring_peers[d - 1]},
            device_id_type=mesh_ids,
        )
        copy.start()
        ring.append(copy)
    normalize_passages()
    for copy in ring:
        copy.wait_recv()
    own.wait()

    chunks = up_send.shape[1]
    width = side // chunks
    up_steps, dn_steps = side // 2, (side - 1) // 2
    steps = max(up_steps, dn_steps)

    def forward(t, c, peer, r, sends, recvs):
        part = pl.ds(pl.multiple_of(r * side + c * width, width), width)
        copy = pltpu.make_async_remote_copy(
            src_ref=g_ref.at[part],
            dst_ref=g_ref.at[part],
            send_sem=sends.at[t, c],
            recv_sem=recvs.at[t, c],
            device_id={"dp": peer},
            device_id_type=mesh_ids,
        )
        copy.start()
        return copy

    ups, dns = [], []
    for t in range(steps):
        ups.append([])
        dns.append([])
        for c in range(chunks):
            if t < up_steps:
                if t > 0:
                    ups[t - 1][c].wait_recv()
                ups[t].append(forward(t, c, up_peer, (p2 + side - t) % side, up_send, up_recv))
            if t < dn_steps:
                if t > 0:
                    dns[t - 1][c].wait_recv()
                dns[t].append(forward(t, c, dn_peer, (p2 + t) % side, dn_send, dn_recv))
    score_positives()
    for copy in ups[up_steps - 1] + dns[dn_steps - 1]:
        copy.wait_recv()
    sent = [copy for step in ups + dns for copy in step]
    for copy in ring + sent + docs:
        copy.wait_send()


def gather_plane(queries, id_block, positives, length_row, passages, side, groups, doc_count):
    nq, dim = queries.shape
    rows = nq + id_block.shape[0]
    doc_rows = positives.shape[0] + length_row.shape[0]
    plen = passages.shape[1]
    count = side * side
    chunks = math.gcd(side, 4)
    return pl.pallas_call(
        functools.partial(exchange_kernel, side=side, plen=plen),
        out_shape=(
            jax.ShapeDtypeStruct((count, rows, dim), jnp.bfloat16),
            jax.ShapeDtypeStruct((groups, doc_rows, dim), jnp.bfloat16),
            jax.ShapeDtypeStruct(passages.shape, jnp.bfloat16),
            jax.ShapeDtypeStruct((groups * doc_count, nq), jnp.float32),
        ),
        in_specs=[pl.BlockSpec(memory_space=pltpu.VMEM)] * 5,
        out_specs=(pl.BlockSpec(memory_space=pltpu.VMEM),) * 4,
        scratch_shapes=[
            pltpu.VMEM((rows, dim), jnp.bfloat16),
            pltpu.VMEM((doc_rows, dim), jnp.bfloat16),
            pltpu.SemaphoreType.DMA((side - 1,)),
            pltpu.SemaphoreType.DMA((side - 1,)),
            pltpu.SemaphoreType.DMA((side // 2, chunks)),
            pltpu.SemaphoreType.DMA((side // 2, chunks)),
            pltpu.SemaphoreType.DMA(((side - 1) // 2, chunks)),
            pltpu.SemaphoreType.DMA(((side - 1) // 2, chunks)),
            pltpu.SemaphoreType.DMA((groups - 1,)),
            pltpu.SemaphoreType.DMA((groups - 1,)),
            pltpu.SemaphoreType.DMA(()),
            pltpu.SemaphoreType.DMA(()),
        ],
        compiler_params=pltpu.CompilerParams(collective_id=0, has_side_effects=True),
    )(queries, id_block, positives, length_row, passages)


def score_return_kernel(
    pid_ref, len_ref, g_ref, p_ref, o_ref, x_buf, send_sems, recv_sems, own_sem, *, side
):
    mesh_ids = pl.DeviceIdType.MESH
    count = g_ref.shape[0]
    slots = pid_ref.shape[0] // count
    lanes = o_ref.shape[2]
    plen = p_ref.shape[1]
    me = lax.axis_index("dp")
    odd = lax.axis_index("blk") % 2
    barrier = pltpu.get_barrier_semaphore()

    def signal(d, carry):
        pl.semaphore_signal(
            barrier, inc=1, device_id={"dp": (me + d) % count}, device_id_type=mesh_ids
        )
        return carry

    lax.fori_loop(1, count, signal, 0)
    x_buf[...] = jnp.zeros(x_buf.shape, jnp.float32)
    row_ids = lax.broadcasted_iota(jnp.int32, (plen, lanes), 0)

    def body(s, carry):
        q = g_ref[s, 0:lanes, :]
        for r in range(slots):
            pidx = pid_ref[s * slots + r]
            sim = lax.dot_general(
                p_ref[pidx], q, (((1,), (1,)), ((), ())), preferred_element_type=jnp.float32
            )
            sim = jnp.where(row_ids < len_ref[pidx], sim, NEG)
            x_buf[s, pl.ds(r, 1), :] = jnp.max(sim, axis=0, keepdims=True)
        return carry

    lax.fori_loop(0, count, body, 0)
    pl.semaphore_wait(barrier, count - 1)

    def slot_of(t):
        return odd * ((t % side) * side + t // side) + (1 - odd) * t

    own = pltpu.make_async_copy(x_buf.at[slot_of(me)], o_ref.at[me], own_sem)
    own.start()

    def describe(d):
        target = (me + d) % count
        return pltpu.make_async_remote_copy(
            src_ref=x_buf.at[slot_of(target)],
            dst_ref=o_ref.at[me],
            send_sem=send_sems.at[d - 1],
            recv_sem=recv_sems.at[d - 1],
            device_id={"dp": target},
            device_id_type=mesh_ids,
        )

    def start(d, carry):
        describe(d).start()
        return carry

    def finish(d, carry):
        copy = describe(d)
        copy.wait_recv()
        copy.wait_send()
        return carry

    lax.fori_loop(1, count, start, 0)
    own.wait()
    lax.fori_loop(1, count, finish, 0)


def score_and_return(pid, lengths, gathered, passage_unit, side, lanes):
    count = gathered.shape[0]
    plen, dim = passage_unit.shape[1], passage_unit.shape[2]
    slots = pid.shape[0] // count
    return pl.pallas_call(
        functools.partial(score_return_kernel, side=side),
        out_shape=jax.ShapeDtypeStruct((count, 8, lanes), jnp.float32),
        in_specs=[pl.BlockSpec(memory_space=pltpu.SMEM)] * 2
        + [pl.BlockSpec(memory_space=pltpu.VMEM)] * 2,
        out_specs=pl.BlockSpec(memory_space=pltpu.VMEM),
        scratch_shapes=[
            pltpu.VMEM((count, 8, lanes), jnp.float32),
            pltpu.SemaphoreType.DMA((count - 1,)),
            pltpu.SemaphoreType.DMA((count - 1,)),
            pltpu.SemaphoreType.DMA(()),
        ],
        cost_estimate=pl.CostEstimate(
            flops=2 * count * slots * plen * dim * lanes,
            transcendentals=0,
            bytes_accessed=gathered.size * 2 + passage_unit.size * 2,
        ),
        compiler_params=pltpu.CompilerParams(collective_id=1, has_side_effects=True),
    )(pid, lengths, gathered, passage_unit)


def per_device(
    queries, passages, passage_lengths, positives, positive_lengths, owners, local_ids, teacher
):
    peer_count = lax.axis_size("dp")
    me = lax.axis_index("dp")
    query_count, qlen, dim = queries.shape[1], queries.shape[2], queries.shape[3]
    cand_count = owners.shape[2]
    pass_count, plen = passages.shape[1], passages.shape[2]
    pairs = query_count * cand_count
    slots = 4
    lanes = slots * qlen

    groups = lax.axis_size("blk")
    length_row = jnp.zeros((16, dim), jnp.bfloat16).at[0, :query_count].set(
        positive_lengths[0].astype(jnp.bfloat16)
    )
    id_rows = jnp.stack(
        [
            jnp.clip(owners[0, :, :, 0].reshape(pairs), 0, peer_count - 1),
            jnp.clip(local_ids[0].reshape(pairs), 0, pass_count - 1),
        ]
    ).astype(jnp.bfloat16)
    id_rows = id_rows.reshape(2 * pairs // dim, dim)
    id_block = jnp.zeros((16, dim), jnp.bfloat16).at[: id_rows.shape[0]].set(id_rows)
    side = math.isqrt(peer_count)
    gathered, column_docs, passage_unit, raw_cross = gather_plane(
        queries[0].reshape(query_count * qlen, dim),
        id_block,
        positives[0].reshape(query_count * plen, dim),
        length_row,
        passages[0],
        side,
        groups,
        query_count,
    )

    logits = jnp.sum(raw_cross.reshape(groups * query_count, query_count, qlen), axis=-1).T
    own_column = lax.axis_index("blk") * query_count + jnp.arange(query_count, dtype=jnp.int32)
    own_logit = jnp.take_along_axis(logits, own_column[:, None], axis=1)[:, 0]
    contrast = jnp.log(jnp.sum(jnp.exp(logits), axis=-1)) - own_logit

    ids = gathered[:, query_count * qlen : query_count * qlen + 2 * pairs // dim, :]
    ids = ids.reshape(peer_count, 2, pairs).astype(jnp.int32)
    pair_owner, pair_local = ids[:, 0, :], ids[:, 1, :]
    hit = (pair_owner == me).astype(jnp.int32)
    rank = jnp.cumsum(hit, axis=1) - hit
    chosen = [(hit > 0) & (rank == r) for r in range(slots)]
    slot_local = jnp.stack([jnp.sum(jnp.where(c, pair_local, 0), axis=1) for c in chosen], axis=1)
    returned = score_and_return(
        slot_local.reshape(-1), passage_lengths[0], gathered, passage_unit, side, lanes
    )
    per_query = jnp.sum(
        returned[:, :slots, :].reshape(peer_count, slots, query_count, qlen), axis=-1
    )

    my_owner = jnp.clip(owners[0, :, :, 0].reshape(pairs), 0, peer_count - 1)
    owner_hot = (my_owner[:, None] == jnp.arange(peer_count, dtype=jnp.int32)[None, :]).astype(
        jnp.int32
    )
    my_rank = jnp.sum((jnp.cumsum(owner_hot, axis=0) - owner_hot) * owner_hot, axis=1)
    my_query = jnp.arange(pairs, dtype=jnp.int32) // cand_count
    student = per_query[my_owner, jnp.minimum(my_rank, slots - 1), my_query].reshape(
        query_count, cand_count
    )

    teacher_score_rows = teacher[0]
    log_teacher = teacher_score_rows - jnp.log(
        jnp.sum(jnp.exp(teacher_score_rows), axis=-1, keepdims=True)
    )
    log_student = student - jnp.log(jnp.sum(jnp.exp(student), axis=-1, keepdims=True))
    distill = jnp.sum(jnp.exp(log_teacher) * (log_teacher - log_student), axis=-1)
    return (student[None], distill[None], contrast[None])


def solution(mesh):
    in_specs = (
        P("blk", "dp", None, None),
        P("blk", "dp", None, None),
        P("blk", "dp"),
        P("blk", "dp", None, None),
        P("blk", "dp"),
        P("blk", "dp", None, None),
        P("blk", "dp", None),
        P("blk", "dp", None),
    )
    out_specs = (P("blk", "dp", None), P("blk", "dp"), P("blk", "dp"))
    return jax.shard_map(
        per_device, mesh=mesh, in_specs=in_specs, out_specs=out_specs, check_vma=False
    )
```

```python
import functools
import math

import jax
import jax.numpy as jnp
from jax import lax
from jax.experimental import pallas as pl
from jax.experimental.pallas import tpu as pltpu
from jax.sharding import PartitionSpec as P

NEG = -1000000000.0


def unit_block(values):
    wide = values.astype(jnp.float32)
    total = jnp.sum(wide * wide, axis=-1, keepdims=True) + 1e-06
    return (wide * lax.rsqrt(total)).astype(jnp.bfloat16)


def exchange_kernel(
    q_ref, id_ref, pos_ref, lrow_ref, pas_ref,
    g_ref, e_ref, pu_ref, c_ref,
    x_buf, d_buf, ring_send, ring_recv, up_send, up_recv, dn_send, dn_recv,
    blk_send, blk_recv, own_sem, doc_sem, *, side, plen
):
    mesh_ids = pl.DeviceIdType.MESH
    dp = lax.axis_index("dp")
    odd = lax.axis_index("blk") % 2
    high, low = dp // side, dp % side
    p1 = odd * high + (1 - odd) * low
    p2 = odd * low + (1 - odd) * high

    def dp_of(q1, q2):
        return odd * (q1 * side + q2) + (1 - odd) * (q2 * side + q1)

    ring_peers = [dp_of((p1 + d) % side, p2) for d in range(1, side)]
    up_peer = dp_of(p1, (p2 + 1) % side)
    dn_peer = dp_of(p1, (p2 + side - 1) % side)
    groups = e_ref.shape[0]
    me_blk = lax.axis_index("blk")
    blk_peers = [(me_blk + e) % groups for e in range(1, groups)]

    barrier = pltpu.get_barrier_semaphore()
    for peer in ring_peers + [up_peer, dn_peer]:
        pl.semaphore_signal(barrier, inc=1, device_id={"dp": peer}, device_id_type=mesh_ids)
    for peer in blk_peers:
        pl.semaphore_signal(barrier, inc=1, device_id={"blk": peer}, device_id_type=mesh_ids)

    nq, npos = q_ref.shape[0], pos_ref.shape[0]
    x_buf[0:nq, :] = unit_block(q_ref[...])
    x_buf[nq:, :] = id_ref[...]
    d_buf[0:npos, :] = unit_block(pos_ref[...])
    d_buf[npos:, :] = lrow_ref[...]
    pl.semaphore_wait(barrier, len(ring_peers) + 2 + len(blk_peers))

    docs = []
    for e in range(1, groups):
        copy = pltpu.make_async_remote_copy(
            src_ref=d_buf,
            dst_ref=e_ref.at[me_blk],
            send_sem=blk_send.at[e - 1],
            recv_sem=blk_recv.at[e - 1],
            device_id={"blk": blk_peers[e - 1]},
            device_id_type=mesh_ids,
        )
        copy.start()
        docs.append(copy)
    own_doc = pltpu.make_async_copy(d_buf, e_ref.at[me_blk], doc_sem)
    own_doc.start()

    def normalize_passages():
        for p in range(pas_ref.shape[0]):
            pu_ref[p] = unit_block(pas_ref[p])

    def score_positives():
        for copy in docs:
            copy.wait_recv()
        own_doc.wait()
        docs_per_group = c_ref.shape[0] // groups
        q = x_buf[0:nq, :]
        row_ids = lax.broadcasted_iota(jnp.int32, (plen, nq), 0).astype(jnp.float32)
        lane = lax.broadcasted_iota(jnp.int32, (1, lrow_ref.shape[1]), 1)
        for e in range(groups):
            lengths = e_ref[e, npos:, :].astype(jnp.float32)[0:1, :]
            for k in range(docs_per_group):
                kept = jnp.sum(jnp.where(lane == k, lengths, 0.0), axis=1, keepdims=True)
                sim = lax.dot_general(
                    e_ref[e, k * plen : (k + 1) * plen, :],
                    q,
                    (((1,), (1,)), ((), ())),
                    preferred_element_type=jnp.float32,
                )
                sim = jnp.where(row_ids < kept, sim, NEG)
                c_ref[pl.ds(e * docs_per_group + k, 1), :] = jnp.max(sim, axis=0, keepdims=True)

    my_slot = p2 * side + p1
    own = pltpu.make_async_copy(x_buf, g_ref.at[my_slot], own_sem)
    own.start()
    ring = []
    for d in range(1, side):
        copy = pltpu.make_async_remote_copy(
            src_ref=x_buf,
            dst_ref=g_ref.at[my_slot],
            send_sem=ring_send.at[d - 1],
            recv_sem=ring_recv.at[d - 1],
            device_id={"dp": ring_peers[d - 1]},
            device_id_type=mesh_ids,
        )
        copy.start()
        ring.append(copy)
    normalize_passages()
    for copy in ring:
        copy.wait_recv()
    own.wait()

    chunks = up_send.shape[1]
    width = side // chunks
    up_steps, dn_steps = side // 2, (side - 1) // 2
    steps = max(up_steps, dn_steps)

    def forward(t, c, peer, r, sends, recvs):
        part = pl.ds(pl.multiple_of(r * side + c * width, width), width)
        copy = pltpu.make_async_remote_copy(
            src_ref=g_ref.at[part],
            dst_ref=g_ref.at[part],
            send_sem=sends.at[t, c],
            recv_sem=recvs.at[t, c],
            device_id={"dp": peer},
            device_id_type=mesh_ids,
        )
        copy.start()
        return copy

    ups, dns = [], []
    for t in range(steps):
        ups.append([])
        dns.append([])
        for c in range(chunks):
            if t < up_steps:
                if t > 0:
                    ups[t - 1][c].wait_recv()
                ups[t].append(forward(t, c, up_peer, (p2 + side - t) % side, up_send, up_recv))
            if t < dn_steps:
                if t > 0:
                    dns[t - 1][c].wait_recv()
                dns[t].append(forward(t, c, dn_peer, (p2 + t) % side, dn_send, dn_recv))
    score_positives()
    for copy in ups[up_steps - 1] + dns[dn_steps - 1]:
        copy.wait_recv()
    sent = [copy for step in ups + dns for copy in step]
    for copy in ring + sent + docs:
        copy.wait_send()


def gather_plane(queries, id_block, positives, length_row, passages, side, groups, doc_count):
    nq, dim = queries.shape
    rows = nq + id_block.shape[0]
    doc_rows = positives.shape[0] + length_row.shape[0]
    plen = passages.shape[1]
    count = side * side
    chunks = math.gcd(side, 8)
    return pl.pallas_call(
        functools.partial(exchange_kernel, side=side, plen=plen),
        out_shape=(
            jax.ShapeDtypeStruct((count, rows, dim), jnp.bfloat16),
            jax.ShapeDtypeStruct((groups, doc_rows, dim), jnp.bfloat16),
            jax.ShapeDtypeStruct(passages.shape, jnp.bfloat16),
            jax.ShapeDtypeStruct((groups * doc_count, nq), jnp.float32),
        ),
        in_specs=[pl.BlockSpec(memory_space=pltpu.VMEM)] * 5,
        out_specs=(pl.BlockSpec(memory_space=pltpu.VMEM),) * 4,
        scratch_shapes=[
            pltpu.VMEM((rows, dim), jnp.bfloat16),
            pltpu.VMEM((doc_rows, dim), jnp.bfloat16),
            pltpu.SemaphoreType.DMA((side - 1,)),
            pltpu.SemaphoreType.DMA((side - 1,)),
            pltpu.SemaphoreType.DMA((side // 2, chunks)),
            pltpu.SemaphoreType.DMA((side // 2, chunks)),
            pltpu.SemaphoreType.DMA(((side - 1) // 2, chunks)),
            pltpu.SemaphoreType.DMA(((side - 1) // 2, chunks)),
            pltpu.SemaphoreType.DMA((groups - 1,)),
            pltpu.SemaphoreType.DMA((groups - 1,)),
            pltpu.SemaphoreType.DMA(()),
            pltpu.SemaphoreType.DMA(()),
        ],
        compiler_params=pltpu.CompilerParams(collective_id=0, has_side_effects=True),
    )(queries, id_block, positives, length_row, passages)


def score_return_kernel(
    pid_ref, len_ref, g_ref, p_ref, o_ref, x_buf, send_sems, recv_sems, own_sem, *, side
):
    mesh_ids = pl.DeviceIdType.MESH
    count = g_ref.shape[0]
    slots = pid_ref.shape[0] // count
    lanes = o_ref.shape[2]
    plen = p_ref.shape[1]
    me = lax.axis_index("dp")
    odd = lax.axis_index("blk") % 2
    barrier = pltpu.get_barrier_semaphore()

    def signal(d, carry):
        pl.semaphore_signal(
            barrier, inc=1, device_id={"dp": (me + d) % count}, device_id_type=mesh_ids
        )
        return carry

    lax.fori_loop(1, count, signal, 0)
    x_buf[...] = jnp.zeros(x_buf.shape, jnp.float32)
    row_ids = lax.broadcasted_iota(jnp.int32, (plen, lanes), 0)

    def body(s, carry):
        q = g_ref[s, 0:lanes, :]
        for r in range(slots):
            pidx = pid_ref[s * slots + r]
            sim = lax.dot_general(
                p_ref[pidx], q, (((1,), (1,)), ((), ())), preferred_element_type=jnp.float32
            )
            sim = jnp.where(row_ids < len_ref[pidx], sim, NEG)
            x_buf[s, pl.ds(r, 1), :] = jnp.max(sim, axis=0, keepdims=True)
        return carry

    lax.fori_loop(0, count, body, 0)
    pl.semaphore_wait(barrier, count - 1)

    def slot_of(t):
        return odd * ((t % side) * side + t // side) + (1 - odd) * t

    own = pltpu.make_async_copy(x_buf.at[slot_of(me)], o_ref.at[me], own_sem)
    own.start()

    def describe(d):
        target = (me + d) % count
        return pltpu.make_async_remote_copy(
            src_ref=x_buf.at[slot_of(target)],
            dst_ref=o_ref.at[me],
            send_sem=send_sems.at[d - 1],
            recv_sem=recv_sems.at[d - 1],
            device_id={"dp": target},
            device_id_type=mesh_ids,
        )

    def start(d, carry):
        describe(d).start()
        return carry

    def finish(d, carry):
        copy = describe(d)
        copy.wait_recv()
        copy.wait_send()
        return carry

    lax.fori_loop(1, count, start, 0)
    own.wait()
    lax.fori_loop(1, count, finish, 0)


def score_and_return(pid, lengths, gathered, passage_unit, side, lanes):
    count = gathered.shape[0]
    plen, dim = passage_unit.shape[1], passage_unit.shape[2]
    slots = pid.shape[0] // count
    return pl.pallas_call(
        functools.partial(score_return_kernel, side=side),
        out_shape=jax.ShapeDtypeStruct((count, 8, lanes), jnp.float32),
        in_specs=[pl.BlockSpec(memory_space=pltpu.SMEM)] * 2
        + [pl.BlockSpec(memory_space=pltpu.VMEM)] * 2,
        out_specs=pl.BlockSpec(memory_space=pltpu.VMEM),
        scratch_shapes=[
            pltpu.VMEM((count, 8, lanes), jnp.float32),
            pltpu.SemaphoreType.DMA((count - 1,)),
            pltpu.SemaphoreType.DMA((count - 1,)),
            pltpu.SemaphoreType.DMA(()),
        ],
        cost_estimate=pl.CostEstimate(
            flops=2 * count * slots * plen * dim * lanes,
            transcendentals=0,
            bytes_accessed=gathered.size * 2 + passage_unit.size * 2,
        ),
        compiler_params=pltpu.CompilerParams(collective_id=1, has_side_effects=True),
    )(pid, lengths, gathered, passage_unit)


def per_device(
    queries, passages, passage_lengths, positives, positive_lengths, owners, local_ids, teacher
):
    peer_count = lax.axis_size("dp")
    me = lax.axis_index("dp")
    query_count, qlen, dim = queries.shape[1], queries.shape[2], queries.shape[3]
    cand_count = owners.shape[2]
    pass_count, plen = passages.shape[1], passages.shape[2]
    pairs = query_count * cand_count
    slots = 4
    lanes = slots * qlen

    groups = lax.axis_size("blk")
    length_row = jnp.zeros((16, dim), jnp.bfloat16).at[0, :query_count].set(
        positive_lengths[0].astype(jnp.bfloat16)
    )
    id_rows = jnp.stack(
        [
            jnp.clip(owners[0, :, :, 0].reshape(pairs), 0, peer_count - 1),
            jnp.clip(local_ids[0].reshape(pairs), 0, pass_count - 1),
        ]
    ).astype(jnp.bfloat16)
    id_rows = id_rows.reshape(2 * pairs // dim, dim)
    id_block = jnp.zeros((16, dim), jnp.bfloat16).at[: id_rows.shape[0]].set(id_rows)
    side = math.isqrt(peer_count)
    gathered, column_docs, passage_unit, raw_cross = gather_plane(
        queries[0].reshape(query_count * qlen, dim),
        id_block,
        positives[0].reshape(query_count * plen, dim),
        length_row,
        passages[0],
        side,
        groups,
        query_count,
    )

    logits = jnp.sum(raw_cross.reshape(groups * query_count, query_count, qlen), axis=-1).T
    own_column = lax.axis_index("blk") * query_count + jnp.arange(query_count, dtype=jnp.int32)
    own_logit = jnp.take_along_axis(logits, own_column[:, None], axis=1)[:, 0]
    contrast = jnp.log(jnp.sum(jnp.exp(logits), axis=-1)) - own_logit

    ids = gathered[:, query_count * qlen : query_count * qlen + 2 * pairs // dim, :]
    ids = ids.reshape(peer_count, 2, pairs).astype(jnp.int32)
    pair_owner, pair_local = ids[:, 0, :], ids[:, 1, :]
    hit = (pair_owner == me).astype(jnp.int32)
    rank = jnp.cumsum(hit, axis=1) - hit
    chosen = [(hit > 0) & (rank == r) for r in range(slots)]
    slot_local = jnp.stack([jnp.sum(jnp.where(c, pair_local, 0), axis=1) for c in chosen], axis=1)
    returned = score_and_return(
        slot_local.reshape(-1), passage_lengths[0], gathered, passage_unit, side, lanes
    )
    per_query = jnp.sum(
        returned[:, :slots, :].reshape(peer_count, slots, query_count, qlen), axis=-1
    )

    my_owner = jnp.clip(owners[0, :, :, 0].reshape(pairs), 0, peer_count - 1)
    owner_hot = (my_owner[:, None] == jnp.arange(peer_count, dtype=jnp.int32)[None, :]).astype(
        jnp.int32
    )
    my_rank = jnp.sum((jnp.cumsum(owner_hot, axis=0) - owner_hot) * owner_hot, axis=1)
    my_query = jnp.arange(pairs, dtype=jnp.int32) // cand_count
    student = per_query[my_owner, jnp.minimum(my_rank, slots - 1), my_query].reshape(
        query_count, cand_count
    )

    teacher_score_rows = teacher[0]
    log_teacher = teacher_score_rows - jnp.log(
        jnp.sum(jnp.exp(teacher_score_rows), axis=-1, keepdims=True)
    )
    log_student = student - jnp.log(jnp.sum(jnp.exp(student), axis=-1, keepdims=True))
    distill = jnp.sum(jnp.exp(log_teacher) * (log_teacher - log_student), axis=-1)
    return (student[None], distill[None], contrast[None])


def solution(mesh):
    in_specs = (
        P("blk", "dp", None, None),
        P("blk", "dp", None, None),
        P("blk", "dp"),
        P("blk", "dp", None, None),
        P("blk", "dp"),
        P("blk", "dp", None, None),
        P("blk", "dp", None),
        P("blk", "dp", None),
    )
    out_specs = (P("blk", "dp", None), P("blk", "dp"), P("blk", "dp"))
    return jax.shard_map(
        per_device, mesh=mesh, in_specs=in_specs, out_specs=out_specs, check_vma=False
    )
```

```python
import functools
import math

import jax
import jax.numpy as jnp
from jax import lax
from jax.experimental import pallas as pl
from jax.experimental.pallas import tpu as pltpu
from jax.sharding import PartitionSpec as P

NEG = -1000000000.0


def unit_block(values):
    wide = values.astype(jnp.float32)
    total = jnp.sum(wide * wide, axis=-1, keepdims=True) + 1e-06
    return (wide * lax.rsqrt(total)).astype(jnp.bfloat16)


def exchange_kernel(
    q_ref, id_ref, pos_ref, lrow_ref, pas_ref,
    g_ref, e_ref, pu_ref, c_ref,
    x_buf, d_buf, ring_send, ring_recv, up_send, up_recv, dn_send, dn_recv,
    blk_send, blk_recv, own_sem, doc_sem, *, side, plen
):
    mesh_ids = pl.DeviceIdType.MESH
    dp = lax.axis_index("dp")
    odd = lax.axis_index("blk") % 2
    high, low = dp // side, dp % side
    p1 = odd * high + (1 - odd) * low
    p2 = odd * low + (1 - odd) * high

    def dp_of(q1, q2):
        return odd * (q1 * side + q2) + (1 - odd) * (q2 * side + q1)

    ring_peers = [dp_of((p1 + d) % side, p2) for d in range(1, side)]
    up_peer = dp_of(p1, (p2 + 1) % side)
    dn_peer = dp_of(p1, (p2 + side - 1) % side)
    groups = e_ref.shape[0]
    me_blk = lax.axis_index("blk")
    blk_peers = [(me_blk + e) % groups for e in range(1, groups)]

    barrier = pltpu.get_barrier_semaphore()
    for peer in ring_peers + [up_peer, dn_peer]:
        pl.semaphore_signal(barrier, inc=1, device_id={"dp": peer}, device_id_type=mesh_ids)
    for peer in blk_peers:
        pl.semaphore_signal(barrier, inc=1, device_id={"blk": peer}, device_id_type=mesh_ids)

    nq, npos = q_ref.shape[0], pos_ref.shape[0]
    x_buf[0:nq, :] = unit_block(q_ref[...])
    x_buf[nq:, :] = id_ref[...]
    d_buf[0:npos, :] = unit_block(pos_ref[...])
    d_buf[npos:, :] = lrow_ref[...]
    pl.semaphore_wait(barrier, len(ring_peers) + 2 + len(blk_peers))

    docs = []
    for e in range(1, groups):
        copy = pltpu.make_async_remote_copy(
            src_ref=d_buf,
            dst_ref=e_ref.at[me_blk],
            send_sem=blk_send.at[e - 1],
            recv_sem=blk_recv.at[e - 1],
            device_id={"blk": blk_peers[e - 1]},
            device_id_type=mesh_ids,
        )
        copy.start()
        docs.append(copy)
    own_doc = pltpu.make_async_copy(d_buf, e_ref.at[me_blk], doc_sem)
    own_doc.start()

    def normalize_passages():
        for p in range(pas_ref.shape[0]):
            pu_ref[p] = unit_block(pas_ref[p])

    def score_positives():
        for copy in docs:
            copy.wait_recv()
        own_doc.wait()
        docs_per_group = c_ref.shape[0] // groups
        q = x_buf[0:nq, :]
        row_ids = lax.broadcasted_iota(jnp.int32, (plen, nq), 0).astype(jnp.float32)
        lane = lax.broadcasted_iota(jnp.int32, (1, lrow_ref.shape[1]), 1)
        for e in range(groups):
            lengths = e_ref[e, npos:, :].astype(jnp.float32)[0:1, :]
            for k in range(docs_per_group):
                kept = jnp.sum(jnp.where(lane == k, lengths, 0.0), axis=1, keepdims=True)
                sim = lax.dot_general(
                    e_ref[e, k * plen : (k + 1) * plen, :],
                    q,
                    (((1,), (1,)), ((), ())),
                    preferred_element_type=jnp.float32,
                )
                sim = jnp.where(row_ids < kept, sim, NEG)
                c_ref[pl.ds(e * docs_per_group + k, 1), :] = jnp.max(sim, axis=0, keepdims=True)

    my_slot = p2 * side + p1
    own = pltpu.make_async_copy(x_buf, g_ref.at[my_slot], own_sem)
    own.start()
    ring = []
    for d in range(1, side):
        copy = pltpu.make_async_remote_copy(
            src_ref=x_buf,
            dst_ref=g_ref.at[my_slot],
            send_sem=ring_send.at[d - 1],
            recv_sem=ring_recv.at[d - 1],
            device_id={"dp": ring_peers[d - 1]},
            device_id_type=mesh_ids,
        )
        copy.start()
        ring.append(copy)
    normalize_passages()
    for copy in ring:
        copy.wait_recv()
    own.wait()

    chunks = up_send.shape[1]
    width = side // chunks
    up_steps, dn_steps = side // 2, (side - 1) // 2
    steps = max(up_steps, dn_steps)

    def forward(t, c, peer, r, sends, recvs):
        part = pl.ds(pl.multiple_of(r * side + c * width, width), width)
        copy = pltpu.make_async_remote_copy(
            src_ref=g_ref.at[part],
            dst_ref=g_ref.at[part],
            send_sem=sends.at[t, c],
            recv_sem=recvs.at[t, c],
            device_id={"dp": peer},
            device_id_type=mesh_ids,
        )
        copy.start()
        return copy

    ups, dns = [], []
    for t in range(steps):
        ups.append([])
        dns.append([])
        for c in range(chunks):
            if t < up_steps:
                if t > 0:
                    ups[t - 1][c].wait_recv()
                ups[t].append(forward(t, c, up_peer, (p2 + side - t) % side, up_send, up_recv))
            if t < dn_steps:
                if t > 0:
                    dns[t - 1][c].wait_recv()
                dns[t].append(forward(t, c, dn_peer, (p2 + t) % side, dn_send, dn_recv))
    score_positives()
    for copy in ups[up_steps - 1] + dns[dn_steps - 1]:
        copy.wait_recv()
    sent = [copy for step in ups + dns for copy in step]
    for copy in ring + sent + docs:
        copy.wait_send()


def gather_plane(queries, id_block, positives, length_row, passages, side, groups, doc_count):
    nq, dim = queries.shape
    rows = nq + id_block.shape[0]
    doc_rows = positives.shape[0] + length_row.shape[0]
    plen = passages.shape[1]
    count = side * side
    chunks = math.gcd(side, 4)
    return pl.pallas_call(
        functools.partial(exchange_kernel, side=side, plen=plen),
        out_shape=(
            jax.ShapeDtypeStruct((count, rows, dim), jnp.bfloat16),
            jax.ShapeDtypeStruct((groups, doc_rows, dim), jnp.bfloat16),
            jax.ShapeDtypeStruct(passages.shape, jnp.bfloat16),
            jax.ShapeDtypeStruct((groups * doc_count, nq), jnp.float32),
        ),
        in_specs=[pl.BlockSpec(memory_space=pltpu.VMEM)] * 5,
        out_specs=(pl.BlockSpec(memory_space=pltpu.VMEM),) * 4,
        scratch_shapes=[
            pltpu.VMEM((rows, dim), jnp.bfloat16),
            pltpu.VMEM((doc_rows, dim), jnp.bfloat16),
            pltpu.SemaphoreType.DMA((side - 1,)),
            pltpu.SemaphoreType.DMA((side - 1,)),
            pltpu.SemaphoreType.DMA((side // 2, chunks)),
            pltpu.SemaphoreType.DMA((side // 2, chunks)),
            pltpu.SemaphoreType.DMA(((side - 1) // 2, chunks)),
            pltpu.SemaphoreType.DMA(((side - 1) // 2, chunks)),
            pltpu.SemaphoreType.DMA((groups - 1,)),
            pltpu.SemaphoreType.DMA((groups - 1,)),
            pltpu.SemaphoreType.DMA(()),
            pltpu.SemaphoreType.DMA(()),
        ],
        compiler_params=pltpu.CompilerParams(collective_id=0, has_side_effects=True),
    )(queries, id_block, positives, length_row, passages)


def score_return_kernel(
    pid_ref, len_ref, g_ref, p_ref, o_ref, x_buf, send_sems, recv_sems, own_sem, *, side
):
    mesh_ids = pl.DeviceIdType.MESH
    count = g_ref.shape[0]
    slots = pid_ref.shape[0] // count
    lanes = o_ref.shape[2]
    plen = p_ref.shape[1]
    me = lax.axis_index("dp")
    odd = lax.axis_index("blk") % 2
    barrier = pltpu.get_barrier_semaphore()

    def signal(d, carry):
        pl.semaphore_signal(
            barrier, inc=1, device_id={"dp": (me + d) % count}, device_id_type=mesh_ids
        )
        return carry

    lax.fori_loop(1, count, signal, 0)
    x_buf[...] = jnp.zeros(x_buf.shape, jnp.float32)
    row_ids = lax.broadcasted_iota(jnp.int32, (plen, lanes), 0)

    def body(s, carry):
        q = g_ref[s, 0:lanes, :]
        for r in range(slots):
            pidx = pid_ref[s * slots + r]
            sim = lax.dot_general(
                p_ref[pidx], q, (((1,), (1,)), ((), ())), preferred_element_type=jnp.float32
            )
            sim = jnp.where(row_ids < len_ref[pidx], sim, NEG)
            x_buf[s, pl.ds(r, 1), :] = jnp.max(sim, axis=0, keepdims=True)
        return carry

    lax.fori_loop(0, count, body, 0)
    pl.semaphore_wait(barrier, count - 1)

    def slot_of(t):
        return odd * ((t % side) * side + t // side) + (1 - odd) * t

    own = pltpu.make_async_copy(x_buf.at[slot_of(me)], o_ref.at[me], own_sem)
    own.start()

    def describe(d):
        target = (me + d) % count
        return pltpu.make_async_remote_copy(
            src_ref=x_buf.at[slot_of(target)],
            dst_ref=o_ref.at[me],
            send_sem=send_sems.at[d - 1],
            recv_sem=recv_sems.at[d - 1],
            device_id={"dp": target},
            device_id_type=mesh_ids,
        )

    def start(d, carry):
        describe(d).start()
        return carry

    def finish(d, carry):
        copy = describe(d)
        copy.wait_recv()
        copy.wait_send()
        return carry

    lax.fori_loop(1, count, start, 0)
    own.wait()
    lax.fori_loop(1, count, finish, 0)


def score_and_return(pid, lengths, gathered, passage_unit, side, lanes):
    count = gathered.shape[0]
    plen, dim = passage_unit.shape[1], passage_unit.shape[2]
    slots = pid.shape[0] // count
    return pl.pallas_call(
        functools.partial(score_return_kernel, side=side),
        out_shape=jax.ShapeDtypeStruct((count, 8, lanes), jnp.float32),
        in_specs=[pl.BlockSpec(memory_space=pltpu.SMEM)] * 2
        + [pl.BlockSpec(memory_space=pltpu.VMEM)] * 2,
        out_specs=pl.BlockSpec(memory_space=pltpu.VMEM),
        scratch_shapes=[
            pltpu.VMEM((count, 8, lanes), jnp.float32),
            pltpu.SemaphoreType.DMA((count - 1,)),
            pltpu.SemaphoreType.DMA((count - 1,)),
            pltpu.SemaphoreType.DMA(()),
        ],
        cost_estimate=pl.CostEstimate(
            flops=2 * count * slots * plen * dim * lanes,
            transcendentals=0,
            bytes_accessed=gathered.size * 2 + passage_unit.size * 2,
        ),
        compiler_params=pltpu.CompilerParams(collective_id=1, has_side_effects=True),
    )(pid, lengths, gathered, passage_unit)


def per_device(
    queries, passages, passage_lengths, positives, positive_lengths, owners, local_ids, teacher
):
    peer_count = lax.axis_size("dp")
    me = lax.axis_index("dp")
    query_count, qlen, dim = queries.shape[1], queries.shape[2], queries.shape[3]
    cand_count = owners.shape[2]
    pass_count, plen = passages.shape[1], passages.shape[2]
    pairs = query_count * cand_count
    slots = 4
    lanes = slots * qlen

    groups = lax.axis_size("blk")
    length_row = jnp.pad(
        positive_lengths[0].astype(jnp.bfloat16), (0, 16 * dim - query_count)
    ).reshape(16, dim)
    id_rows = jnp.concatenate(
        [
            jnp.clip(owners[0, :, :, 0].reshape(pairs), 0, peer_count - 1),
            jnp.clip(local_ids[0].reshape(pairs), 0, pass_count - 1),
        ]
    ).astype(jnp.bfloat16)
    id_block = jnp.pad(id_rows, (0, 16 * dim - 2 * pairs)).reshape(16, dim)
    side = math.isqrt(peer_count)
    gathered, column_docs, passage_unit, raw_cross = gather_plane(
        queries[0].reshape(query_count * qlen, dim),
        id_block,
        positives[0].reshape(query_count * plen, dim),
        length_row,
        passages[0],
        side,
        groups,
        query_count,
    )

    logits = jnp.sum(raw_cross.reshape(groups * query_count, query_count, qlen), axis=-1).T
    own_column = lax.axis_index("blk") * query_count + jnp.arange(query_count, dtype=jnp.int32)
    own_logit = jnp.take_along_axis(logits, own_column[:, None], axis=1)[:, 0]
    contrast = jnp.log(jnp.sum(jnp.exp(logits), axis=-1)) - own_logit

    ids = gathered[:, query_count * qlen : query_count * qlen + 2 * pairs // dim, :]
    ids = ids.reshape(peer_count, 2, pairs).astype(jnp.int32)
    pair_owner, pair_local = ids[:, 0, :], ids[:, 1, :]
    hit = (pair_owner == me).astype(jnp.int32)
    rank = jnp.cumsum(hit, axis=1) - hit
    chosen = [(hit > 0) & (rank == r) for r in range(slots)]
    slot_local = jnp.stack([jnp.sum(jnp.where(c, pair_local, 0), axis=1) for c in chosen], axis=1)
    returned = score_and_return(
        slot_local.reshape(-1), passage_lengths[0], gathered, passage_unit, side, lanes
    )
    per_query = jnp.sum(
        returned[:, :slots, :].reshape(peer_count, slots, query_count, qlen), axis=-1
    )

    my_owner = jnp.clip(owners[0, :, :, 0].reshape(pairs), 0, peer_count - 1)
    owner_hot = (my_owner[:, None] == jnp.arange(peer_count, dtype=jnp.int32)[None, :]).astype(
        jnp.int32
    )
    my_rank = jnp.sum((jnp.cumsum(owner_hot, axis=0) - owner_hot) * owner_hot, axis=1)
    my_query = jnp.arange(pairs, dtype=jnp.int32) // cand_count
    student = per_query[my_owner, jnp.minimum(my_rank, slots - 1), my_query].reshape(
        query_count, cand_count
    )

    teacher_score_rows = teacher[0]
    log_teacher = teacher_score_rows - jnp.log(
        jnp.sum(jnp.exp(teacher_score_rows), axis=-1, keepdims=True)
    )
    log_student = student - jnp.log(jnp.sum(jnp.exp(student), axis=-1, keepdims=True))
    distill = jnp.sum(jnp.exp(log_teacher) * (log_teacher - log_student), axis=-1)
    return (student[None], distill[None], contrast[None])


def solution(mesh):
    in_specs = (
        P("blk", "dp", None, None),
        P("blk", "dp", None, None),
        P("blk", "dp"),
        P("blk", "dp", None, None),
        P("blk", "dp"),
        P("blk", "dp", None, None),
        P("blk", "dp", None),
        P("blk", "dp", None),
    )
    out_specs = (P("blk", "dp", None), P("blk", "dp"), P("blk", "dp"))
    return jax.shard_map(
        per_device, mesh=mesh, in_specs=in_specs, out_specs=out_specs, check_vma=False
    )
```

```python
import functools
import math

import jax
import jax.numpy as jnp
from jax import lax
from jax.experimental import pallas as pl
from jax.experimental.pallas import tpu as pltpu
from jax.sharding import PartitionSpec as P

NEG = -1000000000.0


def unit_block(values):
    wide = values.astype(jnp.float32)
    total = jnp.sum(wide * wide, axis=-1, keepdims=True) + 1e-06
    return (wide * lax.rsqrt(total)).astype(jnp.bfloat16)


def exchange_kernel(
    q_ref, id_ref, pos_ref, lrow_ref, pas_ref,
    g_ref, e_ref, pu_ref, c_ref,
    x_buf, d_buf, ring_send, ring_recv, up_send, up_recv, dn_send, dn_recv,
    blk_send, blk_recv, own_sem, doc_sem, *, side, plen
):
    mesh_ids = pl.DeviceIdType.MESH
    dp = lax.axis_index("dp")
    odd = lax.axis_index("blk") % 2
    high, low = dp // side, dp % side
    p1 = odd * high + (1 - odd) * low
    p2 = odd * low + (1 - odd) * high

    def dp_of(q1, q2):
        return odd * (q1 * side + q2) + (1 - odd) * (q2 * side + q1)

    ring_peers = [dp_of((p1 + d) % side, p2) for d in range(1, side)]
    up_peer = dp_of(p1, (p2 + 1) % side)
    dn_peer = dp_of(p1, (p2 + side - 1) % side)
    groups = e_ref.shape[0]
    me_blk = lax.axis_index("blk")
    blk_peers = [(me_blk + e) % groups for e in range(1, groups)]

    barrier = pltpu.get_barrier_semaphore()
    for peer in ring_peers + [up_peer, dn_peer]:
        pl.semaphore_signal(barrier, inc=1, device_id={"dp": peer}, device_id_type=mesh_ids)
    for peer in blk_peers:
        pl.semaphore_signal(barrier, inc=1, device_id={"blk": peer}, device_id_type=mesh_ids)

    nq, npos = q_ref.shape[0], pos_ref.shape[0]
    x_buf[0:nq, :] = unit_block(q_ref[...])
    x_buf[nq:, :] = id_ref[...]
    d_buf[0:npos, :] = unit_block(pos_ref[...])
    d_buf[npos:, :] = lrow_ref[...]
    pl.semaphore_wait(barrier, len(ring_peers) + 2 + len(blk_peers))

    docs = []
    for e in range(1, groups):
        copy = pltpu.make_async_remote_copy(
            src_ref=d_buf,
            dst_ref=e_ref.at[me_blk],
            send_sem=blk_send.at[e - 1],
            recv_sem=blk_recv.at[e - 1],
            device_id={"blk": blk_peers[e - 1]},
            device_id_type=mesh_ids,
        )
        copy.start()
        docs.append(copy)
    own_doc = pltpu.make_async_copy(d_buf, e_ref.at[me_blk], doc_sem)
    own_doc.start()

    def normalize_passages():
        for p in range(pas_ref.shape[0]):
            pu_ref[p] = unit_block(pas_ref[p])

    def score_positives():
        for copy in docs:
            copy.wait_recv()
        own_doc.wait()
        docs_per_group = c_ref.shape[0] // groups
        q = x_buf[0:nq, :]
        row_ids = lax.broadcasted_iota(jnp.int32, (plen, nq), 0).astype(jnp.float32)
        lane = lax.broadcasted_iota(jnp.int32, (1, lrow_ref.shape[1]), 1)
        for e in range(groups):
            lengths = e_ref[e, npos:, :].astype(jnp.float32)[0:1, :]
            for k in range(docs_per_group):
                kept = jnp.sum(jnp.where(lane == k, lengths, 0.0), axis=1, keepdims=True)
                sim = lax.dot_general(
                    e_ref[e, k * plen : (k + 1) * plen, :],
                    q,
                    (((1,), (1,)), ((), ())),
                    preferred_element_type=jnp.float32,
                )
                sim = jnp.where(row_ids < kept, sim, NEG)
                c_ref[pl.ds(e * docs_per_group + k, 1), :] = jnp.max(sim, axis=0, keepdims=True)

    my_slot = p2 * side + p1
    own = pltpu.make_async_copy(x_buf, g_ref.at[my_slot], own_sem)
    own.start()
    ring = []
    for d in range(1, side):
        copy = pltpu.make_async_remote_copy(
            src_ref=x_buf,
            dst_ref=g_ref.at[my_slot],
            send_sem=ring_send.at[d - 1],
            recv_sem=ring_recv.at[d - 1],
            device_id={"dp": ring_peers[d - 1]},
            device_id_type=mesh_ids,
        )
        copy.start()
        ring.append(copy)
    normalize_passages()
    for copy in ring:
        copy.wait_recv()
    own.wait()

    chunks = up_send.shape[1]
    width = side // chunks
    up_steps, dn_steps = side // 2, (side - 1) // 2
    steps = max(up_steps, dn_steps)

    def forward(t, c, peer, r, sends, recvs):
        part = pl.ds(pl.multiple_of(r * side + c * width, width), width)
        copy = pltpu.make_async_remote_copy(
            src_ref=g_ref.at[part],
            dst_ref=g_ref.at[part],
            send_sem=sends.at[t, c],
            recv_sem=recvs.at[t, c],
            device_id={"dp": peer},
            device_id_type=mesh_ids,
        )
        copy.start()
        return copy

    ups, dns = [], []
    for t in range(steps):
        ups.append([])
        dns.append([])
        for c in range(chunks):
            if t < up_steps:
                if t > 0:
                    ups[t - 1][c].wait_recv()
                ups[t].append(forward(t, c, up_peer, (p2 + side - t) % side, up_send, up_recv))
            if t < dn_steps:
                if t > 0:
                    dns[t - 1][c].wait_recv()
                dns[t].append(forward(t, c, dn_peer, (p2 + t) % side, dn_send, dn_recv))
    score_positives()
    for copy in ups[up_steps - 1] + dns[dn_steps - 1]:
        copy.wait_recv()
    sent = [copy for step in ups + dns for copy in step]
    for copy in ring + sent + docs:
        copy.wait_send()


def gather_plane(queries, id_block, positives, length_row, passages, side, groups, doc_count):
    nq, dim = queries.shape
    rows = nq + id_block.shape[0]
    doc_rows = positives.shape[0] + length_row.shape[0]
    plen = passages.shape[1]
    count = side * side
    chunks = math.gcd(side, 4)
    return pl.pallas_call(
        functools.partial(exchange_kernel, side=side, plen=plen),
        out_shape=(
            jax.ShapeDtypeStruct((count, rows, dim), jnp.bfloat16),
            jax.ShapeDtypeStruct((groups, doc_rows, dim), jnp.bfloat16),
            jax.ShapeDtypeStruct(passages.shape, jnp.bfloat16),
            jax.ShapeDtypeStruct((groups * doc_count, nq), jnp.float32),
        ),
        in_specs=[pl.BlockSpec(memory_space=pltpu.VMEM)] * 5,
        out_specs=(pl.BlockSpec(memory_space=pltpu.VMEM),) * 4,
        scratch_shapes=[
            pltpu.VMEM((rows, dim), jnp.bfloat16),
            pltpu.VMEM((doc_rows, dim), jnp.bfloat16),
            pltpu.SemaphoreType.DMA((side - 1,)),
            pltpu.SemaphoreType.DMA((side - 1,)),
            pltpu.SemaphoreType.DMA((side // 2, chunks)),
            pltpu.SemaphoreType.DMA((side // 2, chunks)),
            pltpu.SemaphoreType.DMA(((side - 1) // 2, chunks)),
            pltpu.SemaphoreType.DMA(((side - 1) // 2, chunks)),
            pltpu.SemaphoreType.DMA((groups - 1,)),
            pltpu.SemaphoreType.DMA((groups - 1,)),
            pltpu.SemaphoreType.DMA(()),
            pltpu.SemaphoreType.DMA(()),
        ],
        compiler_params=pltpu.CompilerParams(collective_id=0, has_side_effects=True),
    )(queries, id_block, positives, length_row, passages)


def score_return_kernel(
    pid_ref, len_ref, g_ref, p_ref, o_ref, x_buf, send_sems, recv_sems, own_sem, *, side
):
    mesh_ids = pl.DeviceIdType.MESH
    count = g_ref.shape[0]
    slots = pid_ref.shape[0] // count
    lanes = o_ref.shape[2]
    plen = p_ref.shape[1]
    me = lax.axis_index("dp")
    odd = lax.axis_index("blk") % 2
    barrier = pltpu.get_barrier_semaphore()

    def signal(d, carry):
        pl.semaphore_signal(
            barrier, inc=1, device_id={"dp": (me + d) % count}, device_id_type=mesh_ids
        )
        return carry

    lax.fori_loop(1, count, signal, 0)
    x_buf[...] = jnp.zeros(x_buf.shape, jnp.float32)
    row_ids = lax.broadcasted_iota(jnp.int32, (plen, lanes), 0)

    def body(s, carry):
        q = g_ref[s, 0:lanes, :]
        for r in range(slots):
            pidx = pid_ref[s * slots + r]
            sim = lax.dot_general(
                p_ref[pidx], q, (((1,), (1,)), ((), ())), preferred_element_type=jnp.float32
            )
            sim = jnp.where(row_ids < len_ref[pidx], sim, NEG)
            x_buf[s, pl.ds(r, 1), :] = jnp.max(sim, axis=0, keepdims=True)
        return carry

    def slot_of(t):
        return odd * ((t % side) * side + t // side) + (1 - odd) * t

    def source_of(s):
        return odd * ((s % side) * side + s // side) + (1 - odd) * s

    own = pltpu.make_async_copy(x_buf.at[slot_of(me)], o_ref.at[me], own_sem)

    def describe(d):
        target = (me + d) % count
        return pltpu.make_async_remote_copy(
            src_ref=x_buf.at[slot_of(target)],
            dst_ref=o_ref.at[me],
            send_sem=send_sems.at[d - 1],
            recv_sem=recv_sems.at[d - 1],
            device_id={"dp": target},
            device_id_type=mesh_ids,
        )

    def send(s):
        d = (source_of(s) + count - me) % count

        @pl.when(d == 0)
        def _():
            own.start()

        @pl.when(d != 0)
        def _():
            describe(d).start()

    def send_one(s, carry):
        send(s)
        return carry

    def score_then_send(s, carry):
        body(s, carry)
        send(s - 1)
        return carry

    early = count // 4
    lax.fori_loop(0, early, body, 0)
    pl.semaphore_wait(barrier, count - 1)
    lax.fori_loop(0, early - 1, send_one, 0)
    lax.fori_loop(early, count, score_then_send, 0)
    send(count - 1)

    def finish(d, carry):
        copy = describe(d)
        copy.wait_recv()
        copy.wait_send()
        return carry

    own.wait()
    lax.fori_loop(1, count, finish, 0)


def score_and_return(pid, lengths, gathered, passage_unit, side, lanes):
    count = gathered.shape[0]
    plen, dim = passage_unit.shape[1], passage_unit.shape[2]
    slots = pid.shape[0] // count
    return pl.pallas_call(
        functools.partial(score_return_kernel, side=side),
        out_shape=jax.ShapeDtypeStruct((count, 8, lanes), jnp.float32),
        in_specs=[pl.BlockSpec(memory_space=pltpu.SMEM)] * 2
        + [pl.BlockSpec(memory_space=pltpu.VMEM)] * 2,
        out_specs=pl.BlockSpec(memory_space=pltpu.VMEM),
        scratch_shapes=[
            pltpu.VMEM((count, 8, lanes), jnp.float32),
            pltpu.SemaphoreType.DMA((count - 1,)),
            pltpu.SemaphoreType.DMA((count - 1,)),
            pltpu.SemaphoreType.DMA(()),
        ],
        cost_estimate=pl.CostEstimate(
            flops=2 * count * slots * plen * dim * lanes,
            transcendentals=0,
            bytes_accessed=gathered.size * 2 + passage_unit.size * 2,
        ),
        compiler_params=pltpu.CompilerParams(collective_id=1, has_side_effects=True),
    )(pid, lengths, gathered, passage_unit)


def per_device(
    queries, passages, passage_lengths, positives, positive_lengths, owners, local_ids, teacher
):
    peer_count = lax.axis_size("dp")
    me = lax.axis_index("dp")
    query_count, qlen, dim = queries.shape[1], queries.shape[2], queries.shape[3]
    cand_count = owners.shape[2]
    pass_count, plen = passages.shape[1], passages.shape[2]
    pairs = query_count * cand_count
    slots = 4
    lanes = slots * qlen

    groups = lax.axis_size("blk")
    length_row = jnp.zeros((16, dim), jnp.bfloat16).at[0, :query_count].set(
        positive_lengths[0].astype(jnp.bfloat16)
    )
    id_rows = jnp.stack(
        [
            jnp.clip(owners[0, :, :, 0].reshape(pairs), 0, peer_count - 1),
            jnp.clip(local_ids[0].reshape(pairs), 0, pass_count - 1),
        ]
    ).astype(jnp.bfloat16)
    id_rows = id_rows.reshape(2 * pairs // dim, dim)
    id_block = jnp.zeros((16, dim), jnp.bfloat16).at[: id_rows.shape[0]].set(id_rows)
    side = math.isqrt(peer_count)
    gathered, column_docs, passage_unit, raw_cross = gather_plane(
        queries[0].reshape(query_count * qlen, dim),
        id_block,
        positives[0].reshape(query_count * plen, dim),
        length_row,
        passages[0],
        side,
        groups,
        query_count,
    )

    logits = jnp.sum(raw_cross.reshape(groups * query_count, query_count, qlen), axis=-1).T
    own_column = lax.axis_index("blk") * query_count + jnp.arange(query_count, dtype=jnp.int32)
    own_logit = jnp.take_along_axis(logits, own_column[:, None], axis=1)[:, 0]
    contrast = jnp.log(jnp.sum(jnp.exp(logits), axis=-1)) - own_logit

    ids = gathered[:, query_count * qlen : query_count * qlen + 2 * pairs // dim, :]
    ids = ids.reshape(peer_count, 2, pairs).astype(jnp.int32)
    pair_owner, pair_local = ids[:, 0, :], ids[:, 1, :]
    hit = (pair_owner == me).astype(jnp.int32)
    rank = jnp.cumsum(hit, axis=1) - hit
    chosen = [(hit > 0) & (rank == r) for r in range(slots)]
    slot_local = jnp.stack([jnp.sum(jnp.where(c, pair_local, 0), axis=1) for c in chosen], axis=1)
    returned = score_and_return(
        slot_local.reshape(-1), passage_lengths[0], gathered, passage_unit, side, lanes
    )
    per_query = jnp.sum(
        returned[:, :slots, :].reshape(peer_count, slots, query_count, qlen), axis=-1
    )

    my_owner = jnp.clip(owners[0, :, :, 0].reshape(pairs), 0, peer_count - 1)
    owner_hot = (my_owner[:, None] == jnp.arange(peer_count, dtype=jnp.int32)[None, :]).astype(
        jnp.int32
    )
    my_rank = jnp.sum((jnp.cumsum(owner_hot, axis=0) - owner_hot) * owner_hot, axis=1)
    my_query = jnp.arange(pairs, dtype=jnp.int32) // cand_count
    student = per_query[my_owner, jnp.minimum(my_rank, slots - 1), my_query].reshape(
        query_count, cand_count
    )

    teacher_score_rows = teacher[0]
    log_teacher = teacher_score_rows - jnp.log(
        jnp.sum(jnp.exp(teacher_score_rows), axis=-1, keepdims=True)
    )
    log_student = student - jnp.log(jnp.sum(jnp.exp(student), axis=-1, keepdims=True))
    distill = jnp.sum(jnp.exp(log_teacher) * (log_teacher - log_student), axis=-1)
    return (student[None], distill[None], contrast[None])


def solution(mesh):
    in_specs = (
        P("blk", "dp", None, None),
        P("blk", "dp", None, None),
        P("blk", "dp"),
        P("blk", "dp", None, None),
        P("blk", "dp"),
        P("blk", "dp", None, None),
        P("blk", "dp", None),
        P("blk", "dp", None),
    )
    out_specs = (P("blk", "dp", None), P("blk", "dp"), P("blk", "dp"))
    return jax.shard_map(
        per_device, mesh=mesh, in_specs=in_specs, out_specs=out_specs, check_vma=False
    )
```

```python
import functools
import math

import jax
import jax.numpy as jnp
from jax import lax
from jax.experimental import pallas as pl
from jax.experimental.pallas import tpu as pltpu
from jax.sharding import PartitionSpec as P

NEG = -1000000000.0


def unit_block(values):
    wide = values.astype(jnp.float32)
    total = jnp.sum(wide * wide, axis=-1, keepdims=True) + 1e-06
    return (wide * lax.rsqrt(total)).astype(jnp.bfloat16)


def exchange_kernel(
    q_ref, id_ref, pos_ref, lrow_ref, pas_ref,
    g_ref, e_ref, pu_ref, c_ref,
    x_buf, d_buf, ring_send, ring_recv, up_send, up_recv, dn_send, dn_recv,
    blk_send, blk_recv, own_sem, doc_sem, *, side, plen
):
    mesh_ids = pl.DeviceIdType.MESH
    dp = lax.axis_index("dp")
    odd = lax.axis_index("blk") % 2
    high, low = dp // side, dp % side
    p1 = odd * high + (1 - odd) * low
    p2 = odd * low + (1 - odd) * high

    def dp_of(q1, q2):
        return odd * (q1 * side + q2) + (1 - odd) * (q2 * side + q1)

    ring_peers = [dp_of((p1 + d) % side, p2) for d in range(1, side)]
    up_peer = dp_of(p1, (p2 + 1) % side)
    dn_peer = dp_of(p1, (p2 + side - 1) % side)
    groups = e_ref.shape[0]
    me_blk = lax.axis_index("blk")
    blk_peers = [(me_blk + e) % groups for e in range(1, groups)]

    barrier = pltpu.get_barrier_semaphore()
    for peer in ring_peers + [up_peer, dn_peer]:
        pl.semaphore_signal(barrier, inc=1, device_id={"dp": peer}, device_id_type=mesh_ids)
    for peer in blk_peers:
        pl.semaphore_signal(barrier, inc=1, device_id={"blk": peer}, device_id_type=mesh_ids)

    nq, npos = q_ref.shape[0], pos_ref.shape[0]
    x_buf[0:nq, :] = unit_block(q_ref[...])
    x_buf[nq:, :] = id_ref[...]
    d_buf[0:npos, :] = unit_block(pos_ref[...])
    d_buf[npos:, :] = lrow_ref[...]
    pl.semaphore_wait(barrier, len(ring_peers) + 2 + len(blk_peers))

    docs = []
    for e in range(1, groups):
        copy = pltpu.make_async_remote_copy(
            src_ref=d_buf,
            dst_ref=e_ref.at[me_blk],
            send_sem=blk_send.at[e - 1],
            recv_sem=blk_recv.at[e - 1],
            device_id={"blk": blk_peers[e - 1]},
            device_id_type=mesh_ids,
        )
        copy.start()
        docs.append(copy)
    own_doc = pltpu.make_async_copy(d_buf, e_ref.at[me_blk], doc_sem)
    own_doc.start()

    def normalize_passages():
        for p in range(pas_ref.shape[0]):
            pu_ref[p] = unit_block(pas_ref[p])

    def score_positives():
        for copy in docs:
            copy.wait_recv()
        own_doc.wait()
        docs_per_group = c_ref.shape[0] // groups
        q = x_buf[0:nq, :]
        row_ids = lax.broadcasted_iota(jnp.int32, (plen, nq), 0).astype(jnp.float32)
        lane = lax.broadcasted_iota(jnp.int32, (1, lrow_ref.shape[1]), 1)
        for e in range(groups):
            lengths = e_ref[e, npos:, :].astype(jnp.float32)[0:1, :]
            for k in range(docs_per_group):
                kept = jnp.sum(jnp.where(lane == k, lengths, 0.0), axis=1, keepdims=True)
                sim = lax.dot_general(
                    e_ref[e, k * plen : (k + 1) * plen, :],
                    q,
                    (((1,), (1,)), ((), ())),
                    preferred_element_type=jnp.float32,
                )
                sim = jnp.where(row_ids < kept, sim, NEG)
                c_ref[pl.ds(e * docs_per_group + k, 1), :] = jnp.max(sim, axis=0, keepdims=True)

    my_slot = p2 * side + p1
    own = pltpu.make_async_copy(x_buf, g_ref.at[my_slot], own_sem)
    own.start()
    ring = []
    for d in range(1, side):
        copy = pltpu.make_async_remote_copy(
            src_ref=x_buf,
            dst_ref=g_ref.at[my_slot],
            send_sem=ring_send.at[d - 1],
            recv_sem=ring_recv.at[d - 1],
            device_id={"dp": ring_peers[d - 1]},
            device_id_type=mesh_ids,
        )
        copy.start()
        ring.append(copy)
    normalize_passages()
    for copy in ring:
        copy.wait_recv()
    own.wait()

    chunks = up_send.shape[1]
    width = side // chunks
    up_steps, dn_steps = side // 2, (side - 1) // 2
    steps = max(up_steps, dn_steps)

    def forward(t, c, peer, r, sends, recvs):
        part = pl.ds(pl.multiple_of(r * side + c * width, width), width)
        copy = pltpu.make_async_remote_copy(
            src_ref=g_ref.at[part],
            dst_ref=g_ref.at[part],
            send_sem=sends.at[t, c],
            recv_sem=recvs.at[t, c],
            device_id={"dp": peer},
            device_id_type=mesh_ids,
        )
        copy.start()
        return copy

    ups, dns = [], []
    for t in range(steps):
        ups.append([])
        dns.append([])
        for c in range(chunks):
            if t < up_steps:
                if t > 0:
                    ups[t - 1][c].wait_recv()
                ups[t].append(forward(t, c, up_peer, (p2 + side - t) % side, up_send, up_recv))
            if t < dn_steps:
                if t > 0:
                    dns[t - 1][c].wait_recv()
                dns[t].append(forward(t, c, dn_peer, (p2 + t) % side, dn_send, dn_recv))
    score_positives()
    for copy in ups[up_steps - 1] + dns[dn_steps - 1]:
        copy.wait_recv()
    sent = [copy for step in ups + dns for copy in step]
    for copy in ring + sent + docs:
        copy.wait_send()


def gather_plane(queries, id_block, positives, length_row, passages, side, groups, doc_count):
    nq, dim = queries.shape
    rows = nq + id_block.shape[0]
    doc_rows = positives.shape[0] + length_row.shape[0]
    plen = passages.shape[1]
    count = side * side
    chunks = math.gcd(side, 4)
    return pl.pallas_call(
        functools.partial(exchange_kernel, side=side, plen=plen),
        out_shape=(
            jax.ShapeDtypeStruct((count, rows, dim), jnp.bfloat16),
            jax.ShapeDtypeStruct((groups, doc_rows, dim), jnp.bfloat16),
            jax.ShapeDtypeStruct(passages.shape, jnp.bfloat16),
            jax.ShapeDtypeStruct((groups * doc_count, nq), jnp.float32),
        ),
        in_specs=[pl.BlockSpec(memory_space=pltpu.VMEM)] * 5,
        out_specs=(pl.BlockSpec(memory_space=pltpu.VMEM),) * 4,
        scratch_shapes=[
            pltpu.VMEM((rows, dim), jnp.bfloat16),
            pltpu.VMEM((doc_rows, dim), jnp.bfloat16),
            pltpu.SemaphoreType.DMA((side - 1,)),
            pltpu.SemaphoreType.DMA((side - 1,)),
            pltpu.SemaphoreType.DMA((side // 2, chunks)),
            pltpu.SemaphoreType.DMA((side // 2, chunks)),
            pltpu.SemaphoreType.DMA(((side - 1) // 2, chunks)),
            pltpu.SemaphoreType.DMA(((side - 1) // 2, chunks)),
            pltpu.SemaphoreType.DMA((groups - 1,)),
            pltpu.SemaphoreType.DMA((groups - 1,)),
            pltpu.SemaphoreType.DMA(()),
            pltpu.SemaphoreType.DMA(()),
        ],
        compiler_params=pltpu.CompilerParams(collective_id=0, has_side_effects=True),
    )(queries, id_block, positives, length_row, passages)


def score_return_kernel(
    pid_ref, len_ref, g_ref, p_ref, o_ref, x_buf, send_sems, recv_sems, own_sem, *, side
):
    mesh_ids = pl.DeviceIdType.MESH
    count = g_ref.shape[0]
    slots = pid_ref.shape[0] // count
    lanes = o_ref.shape[2]
    plen = p_ref.shape[1]
    me = lax.axis_index("dp")
    odd = lax.axis_index("blk") % 2
    barrier = pltpu.get_barrier_semaphore()

    def signal(d, carry):
        pl.semaphore_signal(
            barrier, inc=1, device_id={"dp": (me + d) % count}, device_id_type=mesh_ids
        )
        return carry

    lax.fori_loop(1, count, signal, 0)
    x_buf[...] = jnp.zeros(x_buf.shape, jnp.float32)
    row_ids = lax.broadcasted_iota(jnp.int32, (plen, lanes), 0)
    always = lanes // slots

    def body(s, carry):
        q = g_ref[s, 0:lanes, :]
        for r in range(slots):
            pidx = pid_ref[s * slots + r]
            sim = lax.dot_general(
                p_ref[pidx], q, (((1,), (1,)), ((), ())), preferred_element_type=jnp.float32
            )
            tail = jnp.where(row_ids[always:] < len_ref[pidx], sim[always:], NEG)
            x_buf[s, pl.ds(r, 1), :] = jnp.maximum(
                jnp.max(sim[:always], axis=0, keepdims=True), jnp.max(tail, axis=0, keepdims=True)
            )
        return carry

    def slot_of(t):
        return odd * ((t % side) * side + t // side) + (1 - odd) * t

    def source_of(s):
        return odd * ((s % side) * side + s // side) + (1 - odd) * s

    own = pltpu.make_async_copy(x_buf.at[slot_of(me)], o_ref.at[me], own_sem)

    def describe(d):
        target = (me + d) % count
        return pltpu.make_async_remote_copy(
            src_ref=x_buf.at[slot_of(target)],
            dst_ref=o_ref.at[me],
            send_sem=send_sems.at[d - 1],
            recv_sem=recv_sems.at[d - 1],
            device_id={"dp": target},
            device_id_type=mesh_ids,
        )

    def send(s):
        d = (source_of(s) + count - me) % count

        @pl.when(d == 0)
        def _():
            own.start()

        @pl.when(d != 0)
        def _():
            describe(d).start()

    def send_one(s, carry):
        send(s)
        return carry

    def score_then_send(s, carry):
        body(s, carry)
        send(s - 1)
        return carry

    early = count // 4
    lax.fori_loop(0, early, body, 0)
    pl.semaphore_wait(barrier, count - 1)
    lax.fori_loop(0, early - 1, send_one, 0)
    lax.fori_loop(early, count, score_then_send, 0)
    send(count - 1)

    def finish(d, carry):
        copy = describe(d)
        copy.wait_recv()
        copy.wait_send()
        return carry

    own.wait()
    lax.fori_loop(1, count, finish, 0)


def score_and_return(pid, lengths, gathered, passage_unit, side, lanes):
    count = gathered.shape[0]
    plen, dim = passage_unit.shape[1], passage_unit.shape[2]
    slots = pid.shape[0] // count
    return pl.pallas_call(
        functools.partial(score_return_kernel, side=side),
        out_shape=jax.ShapeDtypeStruct((count, 8, lanes), jnp.float32),
        in_specs=[pl.BlockSpec(memory_space=pltpu.SMEM)] * 2
        + [pl.BlockSpec(memory_space=pltpu.VMEM)] * 2,
        out_specs=pl.BlockSpec(memory_space=pltpu.VMEM),
        scratch_shapes=[
            pltpu.VMEM((count, 8, lanes), jnp.float32),
            pltpu.SemaphoreType.DMA((count - 1,)),
            pltpu.SemaphoreType.DMA((count - 1,)),
            pltpu.SemaphoreType.DMA(()),
        ],
        cost_estimate=pl.CostEstimate(
            flops=2 * count * slots * plen * dim * lanes,
            transcendentals=0,
            bytes_accessed=gathered.size * 2 + passage_unit.size * 2,
        ),
        compiler_params=pltpu.CompilerParams(collective_id=1, has_side_effects=True),
    )(pid, lengths, gathered, passage_unit)


def per_device(
    queries, passages, passage_lengths, positives, positive_lengths, owners, local_ids, teacher
):
    peer_count = lax.axis_size("dp")
    me = lax.axis_index("dp")
    query_count, qlen, dim = queries.shape[1], queries.shape[2], queries.shape[3]
    cand_count = owners.shape[2]
    pass_count, plen = passages.shape[1], passages.shape[2]
    pairs = query_count * cand_count
    slots = 4
    lanes = slots * qlen

    groups = lax.axis_size("blk")
    length_row = jnp.zeros((16, dim), jnp.bfloat16).at[0, :query_count].set(
        positive_lengths[0].astype(jnp.bfloat16)
    )
    id_rows = jnp.stack(
        [
            jnp.clip(owners[0, :, :, 0].reshape(pairs), 0, peer_count - 1),
            jnp.clip(local_ids[0].reshape(pairs), 0, pass_count - 1),
        ]
    ).astype(jnp.bfloat16)
    id_rows = id_rows.reshape(2 * pairs // dim, dim)
    id_block = jnp.zeros((16, dim), jnp.bfloat16).at[: id_rows.shape[0]].set(id_rows)
    side = math.isqrt(peer_count)
    gathered, column_docs, passage_unit, raw_cross = gather_plane(
        queries[0].reshape(query_count * qlen, dim),
        id_block,
        positives[0].reshape(query_count * plen, dim),
        length_row,
        passages[0],
        side,
        groups,
        query_count,
    )

    logits = jnp.sum(raw_cross.reshape(groups * query_count, query_count, qlen), axis=-1).T
    own_column = lax.axis_index("blk") * query_count + jnp.arange(query_count, dtype=jnp.int32)
    own_logit = jnp.take_along_axis(logits, own_column[:, None], axis=1)[:, 0]
    contrast = jnp.log(jnp.sum(jnp.exp(logits), axis=-1)) - own_logit

    ids = gathered[:, query_count * qlen : query_count * qlen + 2 * pairs // dim, :]
    ids = ids.reshape(peer_count, 2, pairs).astype(jnp.int32)
    pair_owner, pair_local = ids[:, 0, :], ids[:, 1, :]
    hit = (pair_owner == me).astype(jnp.int32)
    rank = jnp.cumsum(hit, axis=1) - hit
    chosen = [(hit > 0) & (rank == r) for r in range(slots)]
    slot_local = jnp.stack([jnp.sum(jnp.where(c, pair_local, 0), axis=1) for c in chosen], axis=1)
    returned = score_and_return(
        slot_local.reshape(-1), passage_lengths[0], gathered, passage_unit, side, lanes
    )
    per_query = jnp.sum(
        returned[:, :slots, :].reshape(peer_count, slots, query_count, qlen), axis=-1
    )

    my_owner = jnp.clip(owners[0, :, :, 0].reshape(pairs), 0, peer_count - 1)
    owner_hot = (my_owner[:, None] == jnp.arange(peer_count, dtype=jnp.int32)[None, :]).astype(
        jnp.int32
    )
    my_rank = jnp.sum((jnp.cumsum(owner_hot, axis=0) - owner_hot) * owner_hot, axis=1)
    my_query = jnp.arange(pairs, dtype=jnp.int32) // cand_count
    student = per_query[my_owner, jnp.minimum(my_rank, slots - 1), my_query].reshape(
        query_count, cand_count
    )

    teacher_score_rows = teacher[0]
    log_teacher = teacher_score_rows - jnp.log(
        jnp.sum(jnp.exp(teacher_score_rows), axis=-1, keepdims=True)
    )
    log_student = student - jnp.log(jnp.sum(jnp.exp(student), axis=-1, keepdims=True))
    distill = jnp.sum(jnp.exp(log_teacher) * (log_teacher - log_student), axis=-1)
    return (student[None], distill[None], contrast[None])


def solution(mesh):
    in_specs = (
        P("blk", "dp", None, None),
        P("blk", "dp", None, None),
        P("blk", "dp"),
        P("blk", "dp", None, None),
        P("blk", "dp"),
        P("blk", "dp", None, None),
        P("blk", "dp", None),
        P("blk", "dp", None),
    )
    out_specs = (P("blk", "dp", None), P("blk", "dp"), P("blk", "dp"))
    return jax.shard_map(
        per_device, mesh=mesh, in_specs=in_specs, out_specs=out_specs, check_vma=False
    )
```

```python
import functools
import math

import jax
import jax.numpy as jnp
from jax import lax
from jax.experimental import pallas as pl
from jax.experimental.pallas import tpu as pltpu
from jax.sharding import PartitionSpec as P

NEG = -1000000000.0


def unit_block(values):
    wide = values.astype(jnp.float32)
    total = jnp.sum(wide * wide, axis=-1, keepdims=True) + 1e-06
    return (wide * lax.rsqrt(total)).astype(jnp.bfloat16)


def exchange_kernel(
    q_ref, id_ref, pos_ref, lrow_ref, pas_ref,
    g_ref, e_ref, pu_ref, c_ref,
    x_buf, d_buf, ring_send, ring_recv, up_send, up_recv, dn_send, dn_recv,
    blk_send, blk_recv, own_sem, doc_sem, *, side, plen
):
    mesh_ids = pl.DeviceIdType.MESH
    dp = lax.axis_index("dp")
    odd = lax.axis_index("blk") % 2
    high, low = dp // side, dp % side
    p1 = odd * high + (1 - odd) * low
    p2 = odd * low + (1 - odd) * high

    def dp_of(q1, q2):
        return odd * (q1 * side + q2) + (1 - odd) * (q2 * side + q1)

    ring_peers = [dp_of((p1 + d) % side, p2) for d in range(1, side)]
    up_peer = dp_of(p1, (p2 + 1) % side)
    dn_peer = dp_of(p1, (p2 + side - 1) % side)
    groups = e_ref.shape[0]
    me_blk = lax.axis_index("blk")
    blk_peers = [(me_blk + e) % groups for e in range(1, groups)]

    barrier = pltpu.get_barrier_semaphore()
    for peer in ring_peers + [up_peer, dn_peer]:
        pl.semaphore_signal(barrier, inc=1, device_id={"dp": peer}, device_id_type=mesh_ids)
    for peer in blk_peers:
        pl.semaphore_signal(barrier, inc=1, device_id={"blk": peer}, device_id_type=mesh_ids)

    nq, npos = q_ref.shape[0], pos_ref.shape[0]
    x_buf[0:nq, :] = unit_block(q_ref[...])
    x_buf[nq:, :] = id_ref[...]
    d_buf[0:npos, :] = unit_block(pos_ref[...])
    d_buf[npos:, :] = lrow_ref[...]
    pl.semaphore_wait(barrier, len(ring_peers) + 2 + len(blk_peers))

    docs = []
    for e in range(1, groups):
        copy = pltpu.make_async_remote_copy(
            src_ref=d_buf,
            dst_ref=e_ref.at[me_blk],
            send_sem=blk_send.at[e - 1],
            recv_sem=blk_recv.at[e - 1],
            device_id={"blk": blk_peers[e - 1]},
            device_id_type=mesh_ids,
        )
        copy.start()
        docs.append(copy)
    own_doc = pltpu.make_async_copy(d_buf, e_ref.at[me_blk], doc_sem)
    own_doc.start()

    def normalize_passages():
        for p in range(pas_ref.shape[0]):
            pu_ref[p] = unit_block(pas_ref[p])

    def score_positives():
        for copy in docs:
            copy.wait_recv()
        own_doc.wait()
        docs_per_group = c_ref.shape[0] // groups
        q = x_buf[0:nq, :]
        row_ids = lax.broadcasted_iota(jnp.int32, (plen, nq), 0).astype(jnp.float32)
        lane = lax.broadcasted_iota(jnp.int32, (1, lrow_ref.shape[1]), 1)
        for e in range(groups):
            lengths = e_ref[e, npos:, :].astype(jnp.float32)[0:1, :]
            for k in range(docs_per_group):
                kept = jnp.sum(jnp.where(lane == k, lengths, 0.0), axis=1, keepdims=True)
                sim = lax.dot_general(
                    e_ref[e, k * plen : (k + 1) * plen, :],
                    q,
                    (((1,), (1,)), ((), ())),
                    preferred_element_type=jnp.float32,
                )
                sim = jnp.where(row_ids < kept, sim, NEG)
                c_ref[pl.ds(e * docs_per_group + k, 1), :] = jnp.max(sim, axis=0, keepdims=True)

    my_slot = p2 * side + p1
    own = pltpu.make_async_copy(x_buf, g_ref.at[my_slot], own_sem)
    own.start()
    ring = []
    for d in range(1, side):
        copy = pltpu.make_async_remote_copy(
            src_ref=x_buf,
            dst_ref=g_ref.at[my_slot],
            send_sem=ring_send.at[d - 1],
            recv_sem=ring_recv.at[d - 1],
            device_id={"dp": ring_peers[d - 1]},
            device_id_type=mesh_ids,
        )
        copy.start()
        ring.append(copy)
    normalize_passages()
    for copy in ring:
        copy.wait_recv()
    own.wait()

    chunks = up_send.shape[1]
    width = side // chunks
    up_steps, dn_steps = side // 2, (side - 1) // 2
    steps = max(up_steps, dn_steps)

    def forward(t, c, peer, r, sends, recvs):
        part = pl.ds(pl.multiple_of(r * side + c * width, width), width)
        copy = pltpu.make_async_remote_copy(
            src_ref=g_ref.at[part],
            dst_ref=g_ref.at[part],
            send_sem=sends.at[t, c],
            recv_sem=recvs.at[t, c],
            device_id={"dp": peer},
            device_id_type=mesh_ids,
        )
        copy.start()
        return copy

    ups, dns = [], []
    for t in range(steps):
        ups.append([])
        dns.append([])
        for c in range(chunks):
            if t < up_steps:
                if t > 0:
                    ups[t - 1][c].wait_recv()
                ups[t].append(forward(t, c, up_peer, (p2 + side - t) % side, up_send, up_recv))
            if t < dn_steps:
                if t > 0:
                    dns[t - 1][c].wait_recv()
                dns[t].append(forward(t, c, dn_peer, (p2 + t) % side, dn_send, dn_recv))
    score_positives()
    for copy in ups[up_steps - 1] + dns[dn_steps - 1]:
        copy.wait_recv()
    sent = [copy for step in ups + dns for copy in step]
    for copy in ring + sent + docs:
        copy.wait_send()


def gather_plane(queries, id_block, positives, length_row, passages, side, groups, doc_count):
    nq, dim = queries.shape
    rows = nq + id_block.shape[0]
    doc_rows = positives.shape[0] + length_row.shape[0]
    plen = passages.shape[1]
    count = side * side
    chunks = math.gcd(side, 4)
    return pl.pallas_call(
        functools.partial(exchange_kernel, side=side, plen=plen),
        out_shape=(
            jax.ShapeDtypeStruct((count, rows, dim), jnp.bfloat16),
            jax.ShapeDtypeStruct((groups, doc_rows, dim), jnp.bfloat16),
            jax.ShapeDtypeStruct(passages.shape, jnp.bfloat16),
            jax.ShapeDtypeStruct((groups * doc_count, nq), jnp.float32),
        ),
        in_specs=[pl.BlockSpec(memory_space=pltpu.VMEM)] * 5,
        out_specs=(pl.BlockSpec(memory_space=pltpu.VMEM),) * 4,
        scratch_shapes=[
            pltpu.VMEM((rows, dim), jnp.bfloat16),
            pltpu.VMEM((doc_rows, dim), jnp.bfloat16),
            pltpu.SemaphoreType.DMA((side - 1,)),
            pltpu.SemaphoreType.DMA((side - 1,)),
            pltpu.SemaphoreType.DMA((side // 2, chunks)),
            pltpu.SemaphoreType.DMA((side // 2, chunks)),
            pltpu.SemaphoreType.DMA(((side - 1) // 2, chunks)),
            pltpu.SemaphoreType.DMA(((side - 1) // 2, chunks)),
            pltpu.SemaphoreType.DMA((groups - 1,)),
            pltpu.SemaphoreType.DMA((groups - 1,)),
            pltpu.SemaphoreType.DMA(()),
            pltpu.SemaphoreType.DMA(()),
        ],
        compiler_params=pltpu.CompilerParams(collective_id=0, has_side_effects=True),
    )(queries, id_block, positives, length_row, passages)


def score_return_kernel(
    pid_ref, len_ref, g_ref, p_ref, o_ref, x_buf, send_sems, recv_sems, own_sem, *, side
):
    mesh_ids = pl.DeviceIdType.MESH
    count = g_ref.shape[0]
    slots = pid_ref.shape[0] // count
    lanes = o_ref.shape[2]
    plen = p_ref.shape[1]
    me = lax.axis_index("dp")
    odd = lax.axis_index("blk") % 2
    barrier = pltpu.get_barrier_semaphore()

    def signal(d, carry):
        pl.semaphore_signal(
            barrier, inc=1, device_id={"dp": (me + d) % count}, device_id_type=mesh_ids
        )
        return carry

    lax.fori_loop(1, count, signal, 0)
    x_buf[...] = jnp.zeros(x_buf.shape, jnp.float32)
    row_ids = lax.broadcasted_iota(jnp.int32, (plen, lanes), 0)

    def body(s, carry):
        q = g_ref[s, 0:lanes, :]
        for r in range(slots):
            pidx = pid_ref[s * slots + r]
            sim = lax.dot_general(
                p_ref[pidx], q, (((1,), (1,)), ((), ())), preferred_element_type=jnp.float32
            )
            sim = jnp.where(row_ids < len_ref[pidx], sim, NEG)
            x_buf[s, pl.ds(r, 1), :] = jnp.max(sim, axis=0, keepdims=True)
        return carry

    def slot_of(t):
        return odd * ((t % side) * side + t // side) + (1 - odd) * t

    def source_of(s):
        return odd * ((s % side) * side + s // side) + (1 - odd) * s

    own = pltpu.make_async_copy(x_buf.at[slot_of(me)], o_ref.at[me], own_sem)

    def describe(d):
        target = (me + d) % count
        return pltpu.make_async_remote_copy(
            src_ref=x_buf.at[slot_of(target)],
            dst_ref=o_ref.at[me],
            send_sem=send_sems.at[d - 1],
            recv_sem=recv_sems.at[d - 1],
            device_id={"dp": target},
            device_id_type=mesh_ids,
        )

    def send(s):
        d = (source_of(s) + count - me) % count

        @pl.when(d == 0)
        def _():
            own.start()

        @pl.when(d != 0)
        def _():
            describe(d).start()

    def send_one(s, carry):
        send(s)
        return carry

    def score_then_send(s, carry):
        body(s, carry)
        send(s - 1)
        return carry

    early = count // 8
    lax.fori_loop(0, early, body, 0)
    pl.semaphore_wait(barrier, count - 1)
    lax.fori_loop(0, early - 1, send_one, 0)
    lax.fori_loop(early, count, score_then_send, 0)
    send(count - 1)

    def finish(d, carry):
        copy = describe(d)
        copy.wait_recv()
        copy.wait_send()
        return carry

    own.wait()
    lax.fori_loop(1, count, finish, 0)


def score_and_return(pid, lengths, gathered, passage_unit, side, lanes):
    count = gathered.shape[0]
    plen, dim = passage_unit.shape[1], passage_unit.shape[2]
    slots = pid.shape[0] // count
    return pl.pallas_call(
        functools.partial(score_return_kernel, side=side),
        out_shape=jax.ShapeDtypeStruct((count, 8, lanes), jnp.float32),
        in_specs=[pl.BlockSpec(memory_space=pltpu.SMEM)] * 2
        + [pl.BlockSpec(memory_space=pltpu.VMEM)] * 2,
        out_specs=pl.BlockSpec(memory_space=pltpu.VMEM),
        scratch_shapes=[
            pltpu.VMEM((count, 8, lanes), jnp.float32),
            pltpu.SemaphoreType.DMA((count - 1,)),
            pltpu.SemaphoreType.DMA((count - 1,)),
            pltpu.SemaphoreType.DMA(()),
        ],
        cost_estimate=pl.CostEstimate(
            flops=2 * count * slots * plen * dim * lanes,
            transcendentals=0,
            bytes_accessed=gathered.size * 2 + passage_unit.size * 2,
        ),
        compiler_params=pltpu.CompilerParams(collective_id=1, has_side_effects=True),
    )(pid, lengths, gathered, passage_unit)


def per_device(
    queries, passages, passage_lengths, positives, positive_lengths, owners, local_ids, teacher
):
    peer_count = lax.axis_size("dp")
    me = lax.axis_index("dp")
    query_count, qlen, dim = queries.shape[1], queries.shape[2], queries.shape[3]
    cand_count = owners.shape[2]
    pass_count, plen = passages.shape[1], passages.shape[2]
    pairs = query_count * cand_count
    slots = 4
    lanes = slots * qlen

    groups = lax.axis_size("blk")
    length_row = jnp.zeros((16, dim), jnp.bfloat16).at[0, :query_count].set(
        positive_lengths[0].astype(jnp.bfloat16)
    )
    id_rows = jnp.stack(
        [
            jnp.clip(owners[0, :, :, 0].reshape(pairs), 0, peer_count - 1),
            jnp.clip(local_ids[0].reshape(pairs), 0, pass_count - 1),
        ]
    ).astype(jnp.bfloat16)
    id_rows = id_rows.reshape(2 * pairs // dim, dim)
    id_block = jnp.zeros((16, dim), jnp.bfloat16).at[: id_rows.shape[0]].set(id_rows)
    side = math.isqrt(peer_count)
    gathered, column_docs, passage_unit, raw_cross = gather_plane(
        queries[0].reshape(query_count * qlen, dim),
        id_block,
        positives[0].reshape(query_count * plen, dim),
        length_row,
        passages[0],
        side,
        groups,
        query_count,
    )

    logits = jnp.sum(raw_cross.reshape(groups * query_count, query_count, qlen), axis=-1).T
    own_column = lax.axis_index("blk") * query_count + jnp.arange(query_count, dtype=jnp.int32)
    own_logit = jnp.take_along_axis(logits, own_column[:, None], axis=1)[:, 0]
    contrast = jnp.log(jnp.sum(jnp.exp(logits), axis=-1)) - own_logit

    ids = gathered[:, query_count * qlen : query_count * qlen + 2 * pairs // dim, :]
    ids = ids.reshape(peer_count, 2, pairs).astype(jnp.int32)
    pair_owner, pair_local = ids[:, 0, :], ids[:, 1, :]
    hit = (pair_owner == me).astype(jnp.int32)
    rank = jnp.cumsum(hit, axis=1) - hit
    chosen = [(hit > 0) & (rank == r) for r in range(slots)]
    slot_local = jnp.stack([jnp.sum(jnp.where(c, pair_local, 0), axis=1) for c in chosen], axis=1)
    returned = score_and_return(
        slot_local.reshape(-1), passage_lengths[0], gathered, passage_unit, side, lanes
    )
    per_query = jnp.sum(
        returned[:, :slots, :].reshape(peer_count, slots, query_count, qlen), axis=-1
    )

    my_owner = jnp.clip(owners[0, :, :, 0].reshape(pairs), 0, peer_count - 1)
    owner_hot = (my_owner[:, None] == jnp.arange(peer_count, dtype=jnp.int32)[None, :]).astype(
        jnp.int32
    )
    my_rank = jnp.sum((jnp.cumsum(owner_hot, axis=0) - owner_hot) * owner_hot, axis=1)
    my_query = jnp.arange(pairs, dtype=jnp.int32) // cand_count
    student = per_query[my_owner, jnp.minimum(my_rank, slots - 1), my_query].reshape(
        query_count, cand_count
    )

    teacher_score_rows = teacher[0]
    log_teacher = teacher_score_rows - jnp.log(
        jnp.sum(jnp.exp(teacher_score_rows), axis=-1, keepdims=True)
    )
    log_student = student - jnp.log(jnp.sum(jnp.exp(student), axis=-1, keepdims=True))
    distill = jnp.sum(jnp.exp(log_teacher) * (log_teacher - log_student), axis=-1)
    return (student[None], distill[None], contrast[None])


def solution(mesh):
    in_specs = (
        P("blk", "dp", None, None),
        P("blk", "dp", None, None),
        P("blk", "dp"),
        P("blk", "dp", None, None),
        P("blk", "dp"),
        P("blk", "dp", None, None),
        P("blk", "dp", None),
        P("blk", "dp", None),
    )
    out_specs = (P("blk", "dp", None), P("blk", "dp"), P("blk", "dp"))
    return jax.shard_map(
        per_device, mesh=mesh, in_specs=in_specs, out_specs=out_specs, check_vma=False
    )
```

```python
import functools
import math

import jax
import jax.numpy as jnp
from jax import lax
from jax.experimental import pallas as pl
from jax.experimental.pallas import tpu as pltpu
from jax.sharding import PartitionSpec as P

NEG = -1000000000.0


def unit_block(values):
    wide = values.astype(jnp.float32)
    total = jnp.sum(wide * wide, axis=-1, keepdims=True) + 1e-06
    return (wide * lax.rsqrt(total)).astype(jnp.bfloat16)


def exchange_kernel(
    q_ref, id_ref, pos_ref, lrow_ref, pas_ref,
    g_ref, e_ref, pu_ref, c_ref,
    x_buf, d_buf, ring_send, ring_recv, up_send, up_recv, dn_send, dn_recv,
    blk_send, blk_recv, own_sem, doc_sem, *, side, plen
):
    mesh_ids = pl.DeviceIdType.MESH
    dp = lax.axis_index("dp")
    odd = lax.axis_index("blk") % 2
    high, low = dp // side, dp % side
    p1 = odd * high + (1 - odd) * low
    p2 = odd * low + (1 - odd) * high

    def dp_of(q1, q2):
        return odd * (q1 * side + q2) + (1 - odd) * (q2 * side + q1)

    ring_peers = [dp_of((p1 + d) % side, p2) for d in range(1, side)]
    up_peer = dp_of(p1, (p2 + 1) % side)
    dn_peer = dp_of(p1, (p2 + side - 1) % side)
    groups = e_ref.shape[0]
    me_blk = lax.axis_index("blk")
    blk_peers = [(me_blk + e) % groups for e in range(1, groups)]

    barrier = pltpu.get_barrier_semaphore()
    for peer in ring_peers + [up_peer, dn_peer]:
        pl.semaphore_signal(barrier, inc=1, device_id={"dp": peer}, device_id_type=mesh_ids)
    for peer in blk_peers:
        pl.semaphore_signal(barrier, inc=1, device_id={"blk": peer}, device_id_type=mesh_ids)

    nq, npos = q_ref.shape[0], pos_ref.shape[0]
    x_buf[0:nq, :] = unit_block(q_ref[...])
    x_buf[nq:, :] = id_ref[...]
    d_buf[0:npos, :] = unit_block(pos_ref[...])
    d_buf[npos:, :] = lrow_ref[...]
    pl.semaphore_wait(barrier, len(ring_peers) + 2 + len(blk_peers))

    docs = []
    for e in range(1, groups):
        copy = pltpu.make_async_remote_copy(
            src_ref=d_buf,
            dst_ref=e_ref.at[me_blk],
            send_sem=blk_send.at[e - 1],
            recv_sem=blk_recv.at[e - 1],
            device_id={"blk": blk_peers[e - 1]},
            device_id_type=mesh_ids,
        )
        copy.start()
        docs.append(copy)
    own_doc = pltpu.make_async_copy(d_buf, e_ref.at[me_blk], doc_sem)
    own_doc.start()

    def normalize_passages():
        for p in range(pas_ref.shape[0]):
            pu_ref[p] = unit_block(pas_ref[p])

    def score_positives():
        for copy in docs:
            copy.wait_recv()
        own_doc.wait()
        docs_per_group = c_ref.shape[0] // groups
        q = x_buf[0:nq, :]
        row_ids = lax.broadcasted_iota(jnp.int32, (plen, nq), 0).astype(jnp.float32)
        lane = lax.broadcasted_iota(jnp.int32, (1, lrow_ref.shape[1]), 1)
        for e in range(groups):
            lengths = e_ref[e, npos:, :].astype(jnp.float32)[0:1, :]
            for k in range(docs_per_group):
                kept = jnp.sum(jnp.where(lane == k, lengths, 0.0), axis=1, keepdims=True)
                sim = lax.dot_general(
                    e_ref[e, k * plen : (k + 1) * plen, :],
                    q,
                    (((1,), (1,)), ((), ())),
                    preferred_element_type=jnp.float32,
                )
                sim = jnp.where(row_ids < kept, sim, NEG)
                c_ref[pl.ds(e * docs_per_group + k, 1), :] = jnp.max(sim, axis=0, keepdims=True)

    my_slot = p2 * side + p1
    own = pltpu.make_async_copy(x_buf, g_ref.at[my_slot], own_sem)
    own.start()
    ring = []
    for d in range(1, side):
        copy = pltpu.make_async_remote_copy(
            src_ref=x_buf,
            dst_ref=g_ref.at[my_slot],
            send_sem=ring_send.at[d - 1],
            recv_sem=ring_recv.at[d - 1],
            device_id={"dp": ring_peers[d - 1]},
            device_id_type=mesh_ids,
        )
        copy.start()
        ring.append(copy)
    normalize_passages()
    for copy in ring:
        copy.wait_recv()
    own.wait()

    chunks = up_send.shape[1]
    width = side // chunks
    up_steps, dn_steps = side // 2, (side - 1) // 2
    steps = max(up_steps, dn_steps)

    def forward(t, c, peer, r, sends, recvs):
        part = pl.ds(pl.multiple_of(r * side + c * width, width), width)
        copy = pltpu.make_async_remote_copy(
            src_ref=g_ref.at[part],
            dst_ref=g_ref.at[part],
            send_sem=sends.at[t, c],
            recv_sem=recvs.at[t, c],
            device_id={"dp": peer},
            device_id_type=mesh_ids,
        )
        copy.start()
        return copy

    ups, dns = [], []
    for t in range(steps):
        ups.append([])
        dns.append([])
        for c in range(chunks):
            if t < up_steps:
                if t > 0:
                    ups[t - 1][c].wait_recv()
                ups[t].append(forward(t, c, up_peer, (p2 + side - t) % side, up_send, up_recv))
            if t < dn_steps:
                if t > 0:
                    dns[t - 1][c].wait_recv()
                dns[t].append(forward(t, c, dn_peer, (p2 + t) % side, dn_send, dn_recv))
    score_positives()
    for copy in ups[up_steps - 1] + dns[dn_steps - 1]:
        copy.wait_recv()
    sent = [copy for step in ups + dns for copy in step]
    for copy in ring + sent + docs:
        copy.wait_send()


def gather_plane(queries, id_block, positives, length_row, passages, side, groups, doc_count):
    nq, dim = queries.shape
    rows = nq + id_block.shape[0]
    doc_rows = positives.shape[0] + length_row.shape[0]
    plen = passages.shape[1]
    count = side * side
    chunks = math.gcd(side, 4)
    return pl.pallas_call(
        functools.partial(exchange_kernel, side=side, plen=plen),
        out_shape=(
            jax.ShapeDtypeStruct((count, rows, dim), jnp.bfloat16),
            jax.ShapeDtypeStruct((groups, doc_rows, dim), jnp.bfloat16),
            jax.ShapeDtypeStruct(passages.shape, jnp.bfloat16),
            jax.ShapeDtypeStruct((groups * doc_count, nq), jnp.float32),
        ),
        in_specs=[pl.BlockSpec(memory_space=pltpu.VMEM)] * 5,
        out_specs=(pl.BlockSpec(memory_space=pltpu.VMEM),) * 4,
        scratch_shapes=[
            pltpu.VMEM((rows, dim), jnp.bfloat16),
            pltpu.VMEM((doc_rows, dim), jnp.bfloat16),
            pltpu.SemaphoreType.DMA((side - 1,)),
            pltpu.SemaphoreType.DMA((side - 1,)),
            pltpu.SemaphoreType.DMA((side // 2, chunks)),
            pltpu.SemaphoreType.DMA((side // 2, chunks)),
            pltpu.SemaphoreType.DMA(((side - 1) // 2, chunks)),
            pltpu.SemaphoreType.DMA(((side - 1) // 2, chunks)),
            pltpu.SemaphoreType.DMA((groups - 1,)),
            pltpu.SemaphoreType.DMA((groups - 1,)),
            pltpu.SemaphoreType.DMA(()),
            pltpu.SemaphoreType.DMA(()),
        ],
        compiler_params=pltpu.CompilerParams(collective_id=0, has_side_effects=True),
    )(queries, id_block, positives, length_row, passages)


def score_return_kernel(
    pid_ref, len_ref, g_ref, p_ref, o_ref, x_buf, send_sems, recv_sems, own_sem, *, side
):
    mesh_ids = pl.DeviceIdType.MESH
    count = g_ref.shape[0]
    slots = pid_ref.shape[0] // count
    lanes = o_ref.shape[2]
    plen = p_ref.shape[1]
    me = lax.axis_index("dp")
    odd = lax.axis_index("blk") % 2
    barrier = pltpu.get_barrier_semaphore()

    def signal(d, carry):
        pl.semaphore_signal(
            barrier, inc=1, device_id={"dp": (me + d) % count}, device_id_type=mesh_ids
        )
        return carry

    lax.fori_loop(1, count, signal, 0)
    x_buf[...] = jnp.zeros(x_buf.shape, jnp.float32)
    row_ids = lax.broadcasted_iota(jnp.int32, (plen, lanes), 0)

    def body(s, carry):
        q = g_ref[s, 0:lanes, :]
        for r in range(slots):
            pidx = pid_ref[s * slots + r]
            sim = lax.dot_general(
                p_ref[pidx], q, (((1,), (1,)), ((), ())), preferred_element_type=jnp.float32
            )
            sim = jnp.where(row_ids < len_ref[pidx], sim, NEG)
            x_buf[s, pl.ds(r, 1), :] = jnp.max(sim, axis=0, keepdims=True)
        return carry

    def slot_of(t):
        return odd * ((t % side) * side + t // side) + (1 - odd) * t

    def source_of(s):
        return odd * ((s % side) * side + s // side) + (1 - odd) * s

    own = pltpu.make_async_copy(x_buf.at[slot_of(me)], o_ref.at[me], own_sem)

    def describe(d):
        target = (me + d) % count
        return pltpu.make_async_remote_copy(
            src_ref=x_buf.at[slot_of(target)],
            dst_ref=o_ref.at[me],
            send_sem=send_sems.at[d - 1],
            recv_sem=recv_sems.at[d - 1],
            device_id={"dp": target},
            device_id_type=mesh_ids,
        )

    def send(s):
        d = (source_of(s) + count - me) % count

        @pl.when(d == 0)
        def _():
            own.start()

        @pl.when(d != 0)
        def _():
            describe(d).start()

    def send_one(s, carry):
        send(s)
        return carry

    def score_then_send(s, carry):
        body(s, carry)
        send(s - 1)
        return carry

    early = count * 3 // 8
    lax.fori_loop(0, early, body, 0)
    pl.semaphore_wait(barrier, count - 1)
    lax.fori_loop(0, early - 1, send_one, 0)
    lax.fori_loop(early, count, score_then_send, 0)
    send(count - 1)

    def finish(d, carry):
        copy = describe(d)
        copy.wait_recv()
        copy.wait_send()
        return carry

    own.wait()
    lax.fori_loop(1, count, finish, 0)


def score_and_return(pid, lengths, gathered, passage_unit, side, lanes):
    count = gathered.shape[0]
    plen, dim = passage_unit.shape[1], passage_unit.shape[2]
    slots = pid.shape[0] // count
    return pl.pallas_call(
        functools.partial(score_return_kernel, side=side),
        out_shape=jax.ShapeDtypeStruct((count, 8, lanes), jnp.float32),
        in_specs=[pl.BlockSpec(memory_space=pltpu.SMEM)] * 2
        + [pl.BlockSpec(memory_space=pltpu.VMEM)] * 2,
        out_specs=pl.BlockSpec(memory_space=pltpu.VMEM),
        scratch_shapes=[
            pltpu.VMEM((count, 8, lanes), jnp.float32),
            pltpu.SemaphoreType.DMA((count - 1,)),
            pltpu.SemaphoreType.DMA((count - 1,)),
            pltpu.SemaphoreType.DMA(()),
        ],
        cost_estimate=pl.CostEstimate(
            flops=2 * count * slots * plen * dim * lanes,
            transcendentals=0,
            bytes_accessed=gathered.size * 2 + passage_unit.size * 2,
        ),
        compiler_params=pltpu.CompilerParams(collective_id=1, has_side_effects=True),
    )(pid, lengths, gathered, passage_unit)


def per_device(
    queries, passages, passage_lengths, positives, positive_lengths, owners, local_ids, teacher
):
    peer_count = lax.axis_size("dp")
    me = lax.axis_index("dp")
    query_count, qlen, dim = queries.shape[1], queries.shape[2], queries.shape[3]
    cand_count = owners.shape[2]
    pass_count, plen = passages.shape[1], passages.shape[2]
    pairs = query_count * cand_count
    slots = 4
    lanes = slots * qlen

    groups = lax.axis_size("blk")
    length_row = jnp.zeros((16, dim), jnp.bfloat16).at[0, :query_count].set(
        positive_lengths[0].astype(jnp.bfloat16)
    )
    id_rows = jnp.stack(
        [
            jnp.clip(owners[0, :, :, 0].reshape(pairs), 0, peer_count - 1),
            jnp.clip(local_ids[0].reshape(pairs), 0, pass_count - 1),
        ]
    ).astype(jnp.bfloat16)
    id_rows = id_rows.reshape(2 * pairs // dim, dim)
    id_block = jnp.zeros((16, dim), jnp.bfloat16).at[: id_rows.shape[0]].set(id_rows)
    side = math.isqrt(peer_count)
    gathered, column_docs, passage_unit, raw_cross = gather_plane(
        queries[0].reshape(query_count * qlen, dim),
        id_block,
        positives[0].reshape(query_count * plen, dim),
        length_row,
        passages[0],
        side,
        groups,
        query_count,
    )

    logits = jnp.sum(raw_cross.reshape(groups * query_count, query_count, qlen), axis=-1).T
    own_column = lax.axis_index("blk") * query_count + jnp.arange(query_count, dtype=jnp.int32)
    own_logit = jnp.take_along_axis(logits, own_column[:, None], axis=1)[:, 0]
    contrast = jnp.log(jnp.sum(jnp.exp(logits), axis=-1)) - own_logit

    ids = gathered[:, query_count * qlen : query_count * qlen + 2 * pairs // dim, :]
    ids = ids.reshape(peer_count, 2, pairs).astype(jnp.int32)
    pair_owner, pair_local = ids[:, 0, :], ids[:, 1, :]
    hit = (pair_owner == me).astype(jnp.int32)
    rank = jnp.cumsum(hit, axis=1) - hit
    chosen = [(hit > 0) & (rank == r) for r in range(slots)]
    slot_local = jnp.stack([jnp.sum(jnp.where(c, pair_local, 0), axis=1) for c in chosen], axis=1)
    returned = score_and_return(
        slot_local.reshape(-1), passage_lengths[0], gathered, passage_unit, side, lanes
    )
    per_query = jnp.sum(
        returned[:, :slots, :].reshape(peer_count, slots, query_count, qlen), axis=-1
    )

    my_owner = jnp.clip(owners[0, :, :, 0].reshape(pairs), 0, peer_count - 1)
    owner_hot = (my_owner[:, None] == jnp.arange(peer_count, dtype=jnp.int32)[None, :]).astype(
        jnp.int32
    )
    my_rank = jnp.sum((jnp.cumsum(owner_hot, axis=0) - owner_hot) * owner_hot, axis=1)
    my_query = jnp.arange(pairs, dtype=jnp.int32) // cand_count
    student = per_query[my_owner, jnp.minimum(my_rank, slots - 1), my_query].reshape(
        query_count, cand_count
    )

    teacher_score_rows = teacher[0]
    log_teacher = teacher_score_rows - jnp.log(
        jnp.sum(jnp.exp(teacher_score_rows), axis=-1, keepdims=True)
    )
    log_student = student - jnp.log(jnp.sum(jnp.exp(student), axis=-1, keepdims=True))
    distill = jnp.sum(jnp.exp(log_teacher) * (log_teacher - log_student), axis=-1)
    return (student[None], distill[None], contrast[None])


def solution(mesh):
    in_specs = (
        P("blk", "dp", None, None),
        P("blk", "dp", None, None),
        P("blk", "dp"),
        P("blk", "dp", None, None),
        P("blk", "dp"),
        P("blk", "dp", None, None),
        P("blk", "dp", None),
        P("blk", "dp", None),
    )
    out_specs = (P("blk", "dp", None), P("blk", "dp"), P("blk", "dp"))
    return jax.shard_map(
        per_device, mesh=mesh, in_specs=in_specs, out_specs=out_specs, check_vma=False
    )
```
